128 devices in a mesh: lat: 32 (over y, z, core), lev: 4 (over x).
Axes of the slice: x: 4, y: 4, z: 4, core: 2. Of those that a mesh axis runs over, the one named last changes fastest.
Arguments:
- probes: bfloat16 [512, 2, 256, 512], P('lat', None, None, 'lev'), may hold values from -40 to 40
- legendre: bfloat16 [512, 2, 512, 256], P('lat'), may hold values from -0.25 to 0.25
- quad_weight: float32 [512], P('lat'), may hold values from 0.5 to 2
- trunc_counts: int32 [512], P('lat'), may hold values from 128 to 512, as said below
- background: float32 [2, 512, 16, 1024], P(None, 'lat'), may hold values from 0.5 to 1.5
- level_up: float32 [16], replicated, may hold values from 0.2 to 0.5
- level_down: float32 [16], replicated, may hold values from 0.1 to 0.3
- viscosity: float32 [16], replicated, may hold values from 0.5 to 4
Outputs:
- basis_out: bfloat16 [512, 2, 256, 512], P('lat', None, None, 'lev')
- factor: float32 [16, 16], replicated
The draws below stay inside these ranges and needn't reach their ends.
Inputs may be any that keep to these rules, and one draw needn't show every extreme that they name: `trunc_counts`: wavenumbers kept on a northern latitude and on its mirror; some latitude keeps all 512.
All inputs are finite; a program needn't handle non-finite values.
Results may differ from the reference program's by a relative error of at most 0.017.
Values may be sent and summed in bfloat16 or wider, within the bound.
No kernel may reach another device: no remote copies, remote signals or barrier semaphores. Data moves between devices by JAX's collectives and lax.ppermute only.
A program may use at most 128 MiB of HBM per device.

```python
import math
import jax
import jax.numpy as jnp
from jax import lax

M = 512
K = 512
NH = 512
PROBES = 16
LEV = 16
NLON = 1024


def draw_probes(key, part):
    first_key, second_key = jax.random.split(key, 2)
    shape = (M, 2, K // 2, LEV * 2, PROBES)
    values = jax.random.normal(first_key, shape, jnp.float32)
    spread = jnp.exp(jax.random.uniform(second_key, shape[:3] + (1, 1), jnp.float32, 0.0, math.log(10.0)))
    values = jnp.clip(values * spread / 3.0, -40.0, 40.0)
    return values.reshape(M, 2, K // 2, LEV * 2 * PROBES).astype(jnp.bfloat16)


def draw_trunc_counts(key, part):
    counts = jax.random.randint(key, (NH,), M // 4, M + 1, dtype=jnp.int32)
    return counts.at[NH - 1].set(M)


def level_of(own_key, shape, pieces, least, high):
    def one(position, blocks):
        steps = jax.random.uniform(jax.random.fold_in(jax.random.fold_in(own_key, 6), position), (blocks,), jnp.float32, least / len(pieces), high / len(pieces))
        return jnp.repeat(jnp.exp(steps), shape[position] // blocks).reshape((-1,) + (1,) * (len(shape) - position - 1))

    loudness = one(*pieces[0])
    for cut in pieces[1:]:
        loudness = loudness * one(*cut)
    return loudness


def scatter_about(own_key, shape, scale, most, pieces=(), kind=jnp.bfloat16):
    result = scale * jax.random.normal(own_key, shape, jnp.float32)
    if pieces:
        result = result * level_of(own_key, shape, pieces, -0.22, 0.18)
    return jnp.clip(result, -most, most).astype(kind)


def setup_inputs(seed: int = 0) -> dict:
    seeds = jax.random.split(jax.random.key(seed), 9)
    probes = draw_probes(jax.random.fold_in(seeds[8], 71), 0)
    legendre = scatter_about(seeds[1], (M, 2, NH, K // 2), K ** -0.5, 0.25, ((0, 32),))
    quad_weight = jnp.clip(jnp.exp(math.log(2.0) - 1.3862944 * jax.random.uniform(seeds[2], (NH,), jnp.float32) ** level_of(seeds[2], (NH,), ((0, 32),), -0.2, 0.2)), 0.5, 2.0)
    trunc_counts = draw_trunc_counts(jax.random.fold_in(seeds[8], 71), 0)
    background = jnp.clip(0.5 + 1.0 * jax.random.uniform(seeds[4], (2, NH, LEV, NLON), jnp.float32) ** level_of(seeds[4], (2, NH, LEV, NLON), ((1, 32),), -0.2, 0.2), 0.5, 1.5)
    level_up = jnp.clip(jax.random.uniform(seeds[5], (LEV,), jnp.float32, 0.2, 0.5), 0.2, 0.5)
    level_down = jnp.clip(jax.random.uniform(seeds[6], (LEV,), jnp.float32, 0.1, 0.3), 0.1, 0.3)
    viscosity = jnp.clip(jnp.exp(jax.random.uniform(seeds[7], (LEV,), jnp.float32, math.log(0.5), math.log(4.0))), 0.5, 4.0)
    return dict(probes=probes, legendre=legendre, quad_weight=quad_weight, trunc_counts=trunc_counts, background=background, level_up=level_up, level_down=level_down, viscosity=viscosity)


def make_waves(wave_count, lon_count):
    zonal_ids = lax.broadcasted_iota(jnp.int32, (wave_count, lon_count), 0)
    lon_ids = lax.broadcasted_iota(jnp.int32, (wave_count, lon_count), 1)
    phase = (zonal_ids * lon_ids % lon_count).astype(jnp.float32) * (2.0 * math.pi / lon_count)
    return jnp.stack([jnp.cos(phase), -jnp.sin(phase)], axis=1).astype(jnp.bfloat16)

def damping(wave_first, wave_count, half_degree, visc_cols):
    zonal_ids = wave_first + jnp.arange(wave_count, dtype=jnp.int32)
    degree = zonal_ids[:, None, None] + 2 * jnp.arange(half_degree, dtype=jnp.int32)[None, None, :] + jnp.arange(2, dtype=jnp.int32)[None, :, None]
    scaled_deg = (degree * (degree + 1)).astype(jnp.float32) / float((M + K) * (M + K + 1))
    damp_one = 1.0 / (1.0 + scaled_deg[..., None] * visc_cols[None, None, None, :])
    return damp_one * damp_one

def unfold(parities):
    even_part = parities[:, 0].astype(jnp.float32)
    odd_part = parities[:, 1].astype(jnp.float32)
    return jnp.stack([even_part + odd_part, even_part - odd_part], axis=1)

def couple(grid_field, outer_coef, inner_coef, level_count, probe_count, reduce_levels):
    wave_count, _, row_count, col_count = grid_field.shape
    shaped = grid_field.reshape(wave_count, 2, row_count, level_count, 2, probe_count)
    level_total = reduce_levels(lax.optimization_barrier(jnp.sum(shaped * inner_coef[:, None, None], axis=3)))
    coupled = shaped + outer_coef[:, None, None] * level_total[:, :, :, None]
    return coupled.reshape(wave_count, 2, row_count, col_count)

def grid_pass(grid_field, wave_rows, gain_grid, keep_mask, weights, outer_coef, inner_coef, probe_count, promote, reduce_levels, adjoint):
    wave_count, _, row_count, col_count = grid_field.shape
    level_count = gain_grid.shape[2]
    if adjoint:
        grid_field = grid_field * weights[None, None, :, None]
    else:
        grid_field = couple(grid_field, outer_coef, inner_coef, level_count, probe_count, reduce_levels)
        grid_field = grid_field * keep_mask[:, None, :, None]
    operand = promote(grid_field.astype(jnp.bfloat16)).reshape(wave_count, 2, row_count, level_count, 2, probe_count)
    points = jnp.einsum('mhjlcs,mci->hjlsi', operand.astype(jnp.float32), promote(wave_rows).astype(jnp.float32), preferred_element_type=jnp.float32)
    points = promote((points * gain_grid[:, :, :, None, :]).astype(jnp.bfloat16))
    analysed = jnp.einsum('hjlsi,mci->mhjlcs', points.astype(jnp.float32), promote(wave_rows).astype(jnp.float32), preferred_element_type=jnp.float32)
    analysed = analysed.reshape(wave_count, 2, row_count, col_count)
    if adjoint:
        analysed = analysed * keep_mask[:, None, :, None]
        analysed = couple(analysed, outer_coef, inner_coef, level_count, probe_count, reduce_levels)
    else:
        analysed = analysed * weights[None, None, :, None]
    return jnp.stack([analysed[:, 0] + analysed[:, 1], analysed[:, 0] - analysed[:, 1]], axis=1).astype(jnp.bfloat16)

def to_parities(legendre, spectral):
    return jnp.einsum('mpjq,mpqc->mpjc', legendre.astype(jnp.float32), spectral.astype(jnp.float32), preferred_element_type=jnp.float32).astype(jnp.bfloat16)

def to_spectral(legendre, folded):
    return jnp.einsum('mpjq,mpjc->mpqc', legendre.astype(jnp.float32), folded.astype(jnp.float32), preferred_element_type=jnp.float32)

def widen(values):
    return values.astype(jnp.float32)

def same_values(values):
    return values

def reference(probes, legendre, quad_weight, trunc_counts, background, level_up, level_down, viscosity):
    lon_count = 2 * M
    wave_rows = make_waves(M, lon_count)
    zonal_ids = jnp.arange(M, dtype=jnp.int32)
    doubling = jnp.where(zonal_ids == 0, 1.0, 2.0).astype(jnp.float32)
    keep_mask = (zonal_ids[:, None] < trunc_counts[None, :]).astype(jnp.float32) * doubling[:, None]
    weights = quad_weight / float(lon_count)
    damping_sq = damping(0, M, K // 2, jnp.repeat(viscosity, 2))
    table = legendre.astype(jnp.float32)
    probe_data = jnp.moveaxis(probes.reshape(M, 2, K // 2, LEV * 2, PROBES), 4, 0)

    def one_probe(spectral):
        grid_field = unfold(to_parities(table, spectral.astype(jnp.float32)))
        folded = grid_pass(grid_field, wave_rows, background, keep_mask, weights, level_up, level_down, 1, widen, same_values, False)
        tangent = to_spectral(table, folded.astype(jnp.float32))
        damped = (tangent * damping_sq).astype(jnp.bfloat16)
        grid_field = unfold(to_parities(table, damped.astype(jnp.float32)))
        folded = grid_pass(grid_field, wave_rows, background, keep_mask, weights, level_down, level_up, 1, widen, same_values, True)
        return to_spectral(table, folded.astype(jnp.float32))
    images = lax.map(one_probe, probe_data)
    flattened = jnp.moveaxis(images.reshape(PROBES, M, 2, K // 2, LEV * 2), 0, 4).reshape(-1, PROBES)
    gram_matrix = jnp.dot(flattened.T, flattened, precision=lax.Precision.HIGHEST)
    lower_factor = jnp.linalg.cholesky(gram_matrix)
    inverse = lax.linalg.triangular_solve(lower_factor, jnp.eye(PROBES, dtype=jnp.float32), left_side=True, lower=True)
    row_scale = math.sqrt(M * K * LEV * 2)
    basis_out = (row_scale * jnp.dot(flattened, inverse.T, precision=lax.Precision.HIGHEST)).astype(jnp.bfloat16)
    basis_out = basis_out.reshape(M, 2, K // 2, LEV * 2 * PROBES)
    factor = lower_factor.T / row_scale
    return (basis_out, factor)
```

```python
import functools
import math

import jax
import jax.numpy as jnp
import ml_dtypes
import numpy as np
from jax import lax
from jax.experimental import pallas as pl
from jax.experimental.pallas import tpu as pltpu
from jax.sharding import PartitionSpec as P

M = 512
K = 512
PROBES = 16
LANES = 128
F32 = jnp.float32
BF16 = jnp.bfloat16
PARAMS = pltpu.CompilerParams(vmem_limit_bytes=56 << 20)


def wave_table(wave_count, lon_half):
    zonal = np.arange(wave_count)[:, None]
    lon = np.arange(lon_half)[None, :]
    phase = (zonal * lon % (2 * lon_half)) * (math.pi / lon_half)
    table = np.concatenate([np.cos(phase), -np.sin(phase)], axis=0)
    return table.astype(np.float32).astype(ml_dtypes.bfloat16)


def spread_table():
    rows = np.arange(16)[:, None] % 8
    lanes = np.arange(LANES)[None, :] // PROBES
    return (rows == lanes).astype(ml_dtypes.bfloat16)


def lane_ids(rows):
    return lax.broadcasted_iota(jnp.int32, (rows, LANES), 1)


def row_ids(rows):
    return lax.broadcasted_iota(jnp.int32, (rows, LANES), 0)


def swap_parts(values):
    real_lane = (lane_ids(values.shape[0]) & PROBES) == 0
    return jnp.where(
        real_lane, pltpu.roll(values, LANES - PROBES, 1), pltpu.roll(values, PROBES, 1)
    )


def sum_levels(values):
    values = values + pltpu.roll(values, 64, 1)
    return values + pltpu.roll(values, 32, 1)


def pack_levels(summed):
    rows = summed.shape[0] // 4
    group = lane_ids(rows) // 32
    packed = summed[0:rows]
    for g in range(1, 4):
        packed = jnp.where(group == g, summed[g * rows : (g + 1) * rows], packed)
    return packed


def unpack_levels(packed):
    rows = packed.shape[0]
    group = lane_ids(rows) // 32
    parts = [sum_levels(jnp.where(group == g, packed, 0.0)) for g in range(4)]
    return jnp.concatenate(parts, axis=0)


def partial_kernel(coef_ref, probes_ref, out_ref):
    count = probes_ref.shape[0]
    for m in range(count):
        for p in range(2):
            summed = sum_levels(probes_ref[m, p].astype(F32) * coef_ref[...])
            out_ref[p, m] = pack_levels(summed).astype(BF16)


def level_partial(probes, coef):
    waves, _, degrees, _ = probes.shape
    return pl.pallas_call(
        partial_kernel,
        grid=(4,),
        in_specs=[
            pl.BlockSpec((1, LANES), lambda g: (0, 0)),
            pl.BlockSpec((waves // 4, 2, degrees, LANES), lambda g: (g, 0, 0, 0)),
        ],
        out_specs=pl.BlockSpec((2, waves // 4, degrees // 4, LANES), lambda g: (0, g, 0, 0)),
        out_shape=jax.ShapeDtypeStruct((2, waves, degrees // 4, LANES), BF16),
        compiler_params=PARAMS,
        name="level_partial",
    )(coef, probes)


def legendre_kernel(coef_ref, probes_ref, *refs):
    totals = refs[:4]
    table_ref, out_ref, mixed, turned = refs[4:]
    waves = probes_ref.shape[0]
    rows = table_ref.shape[2]

    @pl.when(pl.program_id(0) == 0)
    def _():
        for m in range(waves):
            total = totals[0][0, m].astype(F32) + totals[1][0, m].astype(F32)
            total = total + (totals[2][0, m].astype(F32) + totals[3][0, m].astype(F32))
            mixed[m] = (
                probes_ref[m, 0].astype(F32) + coef_ref[...] * unpack_levels(total)
            ).astype(BF16)

    for m in range(waves):
        turned[pl.ds(m, rows, stride=waves), :] = jnp.dot(
            table_ref[m, 0], mixed[m], preferred_element_type=F32
        )
    out_ref[...] = turned[...].astype(BF16).reshape(out_ref.shape)


def legendre_forward(probes, totals, legendre, coef, parity):
    waves, _, degrees, _ = probes.shape
    lats = legendre.shape[2]
    blocks = lats // waves
    steps = 4
    total_spec = pl.BlockSpec((1, waves, degrees // 4, LANES), lambda g: (0, 0, 0, 0))
    own_spec = pl.BlockSpec((1, waves, degrees // 4, LANES), lambda g: (parity, 0, 0, 0))
    return pl.pallas_call(
        legendre_kernel,
        grid=(steps,),
        in_specs=[
            pl.BlockSpec((1, LANES), lambda g: (0, 0)),
            pl.BlockSpec((waves, 1, degrees, LANES), lambda g: (0, parity, 0, 0)),
            own_spec,
            total_spec,
            total_spec,
            total_spec,
            pl.BlockSpec((waves, 1, lats // steps, degrees), lambda g: (0, parity, g, 0)),
        ],
        out_specs=pl.BlockSpec((blocks // steps, waves, waves, LANES), lambda g: (g, 0, 0, 0)),
        out_shape=jax.ShapeDtypeStruct((blocks, waves, waves, LANES), BF16),
        scratch_shapes=[
            pltpu.VMEM((waves, degrees, LANES), BF16),
            pltpu.VMEM((lats // steps * waves, LANES), F32),
        ],
        compiler_params=PARAMS,
        name="legendre_forward",
    )(coef, probes, *totals, legendre)


def mask_rows(count):
    zonal = row_ids(M)
    factor = jnp.where(zonal == 0, 1.0, 2.0)
    return jnp.where(zonal < count, factor, 0.0).astype(F32)


def odd_sign():
    return jnp.where((row_ids(M) & 1) == 0, 1.0, -1.0).astype(F32)


def forward_waves(counts_ref, x_ref, waves_ref, masked):
    step = pl.program_id(0)
    real_lane = (lane_ids(M) & PROBES) == 0
    sign = odd_sign()
    first, second = [], []
    for k in range(2):
        x = x_ref[:, k].reshape(M, LANES).astype(F32)
        if masked:
            x = x * mask_rows(counts_ref[2 * step + k])
        swapped = swap_parts(x)
        first.append(jnp.where(real_lane, x, sign * swapped).astype(BF16))
        second.append(jnp.where(real_lane, swapped, sign * x).astype(BF16))
    operand = jnp.concatenate(
        [jnp.concatenate(first, axis=1), jnp.concatenate(second, axis=1)], axis=0
    )
    return jnp.dot(waves_ref[...], operand, preferred_element_type=F32)


def inverse_waves(counts_ref, fields, waves_ref, out_ref, masked):
    step = pl.program_id(0)
    real_lane = (lane_ids(M) & PROBES) == 0
    sign = odd_sign()
    values = jnp.dot(waves_ref[...], fields, preferred_element_type=F32)
    for k in range(2):
        cos_part = values[:M, k * LANES : (k + 1) * LANES]
        sin_part = values[M:, k * LANES : (k + 1) * LANES]
        straight = jnp.where(real_lane, cos_part, sign * sin_part)
        crossed = jnp.where(real_lane, sin_part, sign * cos_part)
        result = straight + swap_parts(crossed)
        if masked:
            result = result * mask_rows(counts_ref[2 * step + k])
        out_ref[:, k] = result.astype(BF16).reshape(out_ref.shape[0], out_ref.shape[2], LANES)


def grid_even_kernel(counts_ref, x_ref, waves_ref, out_ref, *, masked):
    u = forward_waves(counts_ref, x_ref, waves_ref, masked)
    for k in range(2):
        out_ref[k] = u[:, k * LANES : (k + 1) * LANES]


def grid_middle_kernel(
    counts_ref, x_ref, even_ref, gain_ref, spread_ref, waves_ref, turned_ref, out_ref, odd_ref,
    *, masked_in, masked_out,
):
    u = forward_waves(counts_ref, x_ref, waves_ref, masked_in)
    fields = []
    for k in range(2):
        even = even_ref[k]
        odd = u[:, k * LANES : (k + 1) * LANES]
        gains = [
            lax.dot_general(
                gain_ref[h, k], spread_ref[...], (((0,), (0,)), ((), ())),
                preferred_element_type=F32,
            )
            for h in range(2)
        ]
        north = gains[0] * (even + odd)
        south = gains[1] * (even - odd)
        fields.append((north + south).astype(BF16))
        odd_ref[k] = (north - south).astype(BF16)
    inverse_waves(
        counts_ref, jnp.concatenate(fields, axis=1), turned_ref, out_ref, masked_out
    )


def grid_odd_kernel(counts_ref, odd_ref, turned_ref, out_ref, *, masked):
    fields = jnp.concatenate([odd_ref[0], odd_ref[1]], axis=1)
    inverse_waves(counts_ref, fields, turned_ref, out_ref, masked)


def smem_spec():
    return pl.BlockSpec(memory_space=pltpu.SMEM)


def whole_spec(shape):
    return pl.BlockSpec(shape, lambda g: (0,) * len(shape))


def wave_block(x):
    return pl.BlockSpec((x.shape[0], 2, x.shape[2], LANES), lambda g: (0, g, 0, 0))


def grid_pass(arrive, depart, counts, gain, masked_in, masked_out):
    forward = wave_table(M, M)
    waves_t = jnp.asarray(np.ascontiguousarray(forward.T))
    waves = jnp.asarray(forward)
    spread = jnp.asarray(spread_table())
    x_even = arrive(0)
    lats = x_even.shape[1]
    field_spec = pl.BlockSpec((2, M, LANES), lambda g: (g, 0, 0))
    even = pl.pallas_call(
        functools.partial(grid_even_kernel, masked=masked_in),
        grid=(lats // 2,),
        in_specs=[smem_spec(), wave_block(x_even), whole_spec(waves_t.shape)],
        out_specs=field_spec,
        out_shape=jax.ShapeDtypeStruct((lats, M, LANES), F32),
        compiler_params=PARAMS,
        name="grid_even",
    )(counts, x_even, waves_t)
    x_odd = arrive(1)
    out_shape = jax.ShapeDtypeStruct(x_odd.shape, BF16)
    y_even, odd = pl.pallas_call(
        functools.partial(grid_middle_kernel, masked_in=masked_in, masked_out=masked_out),
        grid=(lats // 2,),
        in_specs=[
            smem_spec(),
            wave_block(x_odd),
            field_spec,
            pl.BlockSpec((2, 2, 16, M), lambda g: (0, g, 0, 0)),
            whole_spec(spread.shape),
            whole_spec(waves_t.shape),
            whole_spec(waves.shape),
        ],
        out_specs=(wave_block(x_odd), field_spec),
        out_shape=(out_shape, jax.ShapeDtypeStruct((lats, M, LANES), BF16)),
        compiler_params=PARAMS,
        name="grid_middle",
    )(counts, x_odd, even, gain, spread, waves_t, waves)
    depart(0, y_even)
    y_odd = pl.pallas_call(
        functools.partial(grid_odd_kernel, masked=masked_out),
        grid=(lats // 2,),
        in_specs=[smem_spec(), field_spec, whole_spec(waves.shape)],
        out_specs=wave_block(x_odd),
        out_shape=out_shape,
        compiler_params=PARAMS,
        name="grid_odd",
    )(counts, odd, waves)
    depart(1, y_odd)


def spread_rows(x_ref, scratch):
    chunk = 4
    per = x_ref.shape[1] * x_ref.shape[2]
    for b in range(0, x_ref.shape[0], chunk):
        scratch[b * per : (b + chunk) * per, :] = (
            x_ref[b : b + chunk].astype(F32).reshape(chunk * per, LANES)
        )


def transform_of(table, fields):
    return lax.dot_general(table, fields, (((0,), (0,)), ((), ())), preferred_element_type=F32)


def middle_kernel(first_ref, visc_ref, x_ref, table_ref, out_ref, taken, turned, *, parity):
    waves = x_ref.shape[2]
    lats = x_ref.shape[0] * x_ref.shape[1]
    degrees = table_ref.shape[3]
    spread_rows(x_ref, taken)
    for m in range(waves):
        fields = taken[pl.ds(m, lats, stride=waves), :].astype(BF16)
        table = table_ref[m, 0]
        tangent = transform_of(table, fields)
        degree = first_ref[0] + m + parity + 2 * row_ids(degrees)
        scaled = (degree * (degree + 1)).astype(F32) / float((M + K) * (M + K + 1))
        damp = 1.0 / (1.0 + scaled * visc_ref[...])
        damped = (tangent * (damp * damp)).astype(BF16)
        turned[pl.ds(m, lats, stride=waves), :] = jnp.dot(
            table, damped, preferred_element_type=F32
        )
    per = x_ref.shape[1] * waves
    for b in range(0, x_ref.shape[0], 4):
        out_ref[b : b + 4] = (
            turned[b * per : (b + 4) * per, :].astype(BF16).reshape(4, x_ref.shape[1], waves, LANES)
        )


def middle_stage(x, legendre, visc_lanes, wave_first, parity):
    waves, _, lats, degrees = legendre.shape
    return pl.pallas_call(
        functools.partial(middle_kernel, parity=parity),
        grid=(1,),
        in_specs=[
            smem_spec(),
            whole_spec((1, LANES)),
            whole_spec(x.shape),
            pl.BlockSpec((waves, 1, lats, degrees), lambda g: (0, parity, 0, 0)),
        ],
        out_specs=whole_spec(x.shape),
        out_shape=jax.ShapeDtypeStruct(x.shape, BF16),
        scratch_shapes=[pltpu.VMEM((lats * waves, LANES), F32)] * 2,
        compiler_params=PARAMS,
        name="middle_stage",
    )(wave_first, visc_lanes, x, legendre)


def images_kernel(coef_ref, x_ref, table_ref, out_ref, part_ref, taken):
    waves = x_ref.shape[2]
    lats = x_ref.shape[0] * x_ref.shape[1]
    spread_rows(x_ref, taken)
    for m in range(waves):
        fields = taken[pl.ds(m, lats, stride=waves), :].astype(BF16)
        image = transform_of(table_ref[m, 0], fields)
        out_ref[m] = image
        part_ref[m] = pack_levels(sum_levels(image * coef_ref[...])).astype(BF16)


def image_stage(x, legendre, coef, parity):
    waves, _, lats, degrees = legendre.shape
    return pl.pallas_call(
        images_kernel,
        grid=(1,),
        in_specs=[
            whole_spec((1, LANES)),
            whole_spec(x.shape),
            pl.BlockSpec((waves, 1, lats, degrees), lambda g: (0, parity, 0, 0)),
        ],
        out_specs=(whole_spec((waves, degrees, LANES)), whole_spec((waves, degrees // 4, LANES))),
        out_shape=(
            jax.ShapeDtypeStruct((waves, degrees, LANES), F32),
            jax.ShapeDtypeStruct((waves, degrees // 4, LANES), BF16),
        ),
        scratch_shapes=[pltpu.VMEM((lats * waves, LANES), F32)],
        compiler_params=PARAMS,
        name="image_stage",
    )(coef, x, legendre)


def halves(values):
    high = values.astype(BF16)
    return high, (values - high.astype(F32)).astype(BF16)


def gram_kernel(coef_ref, even_ref, odd_ref, *refs):
    totals = refs[:8]
    full_ref, gram_ref, acc = refs[8:]
    step = pl.program_id(0)

    @pl.when(step == 0)
    def _():
        acc[...] = jnp.zeros_like(acc)

    for m in range(even_ref.shape[0]):
        for p, image_ref in enumerate((even_ref, odd_ref)):
            parts = [ref[m].astype(F32) for ref in totals[4 * p : 4 * p + 4]]
            total = (parts[0] + parts[1]) + (parts[2] + parts[3])
            full = image_ref[m] + coef_ref[...] * unpack_levels(total)
            full_ref[m, p] = full
            high, low = halves(full)
            acc[...] += lax.dot_general(
                high, jnp.concatenate([high, low], axis=1), (((0,), (0,)), ((), ())),
                preferred_element_type=F32,
            )

    @pl.when(step == pl.num_programs(0) - 1)
    def _():
        cross = acc[:, LANES:]
        gram = acc[:, :LANES] + (cross + cross.T)
        same = (row_ids(LANES) // PROBES) == (lane_ids(LANES) // PROBES)
        gram = jnp.where(same, gram, 0.0)
        total = gram[0:PROBES]
        for b in range(1, LANES // PROBES):
            total = total + gram[b * PROBES : (b + 1) * PROBES]
        total = sum_levels(total)
        total = total + pltpu.roll(total, PROBES, 1)
        group = lane_ids(8) // PROBES
        for r in range(2):
            kept = jnp.where(group == row_ids(8), total[8 * r : 8 * r + 8], 0.0)
            line = jnp.sum(kept, axis=0, keepdims=True)
            gram_ref[:, r : r + 1, :] = jnp.broadcast_to(
                line[None], (gram_ref.shape[0], 1, LANES)
            )


def gram_stage(even, odd, totals, coef, copies):
    waves, degrees, _ = even.shape
    steps = 4
    image_spec = pl.BlockSpec((waves // steps, degrees, LANES), lambda g: (g, 0, 0))
    part_spec = pl.BlockSpec((waves // steps, degrees // 4, LANES), lambda g: (g, 0, 0))
    return pl.pallas_call(
        gram_kernel,
        grid=(steps,),
        in_specs=[whole_spec((1, LANES)), image_spec, image_spec] + [part_spec] * 8,
        out_specs=(
            pl.BlockSpec((waves // steps, 2, degrees, LANES), lambda g: (g, 0, 0, 0)),
            whole_spec((copies, 2, LANES)),
        ),
        out_shape=(
            jax.ShapeDtypeStruct((waves, 2, degrees, LANES), F32),
            jax.ShapeDtypeStruct((copies, 2, LANES), F32),
        ),
        scratch_shapes=[pltpu.VMEM((LANES, 2 * LANES), F32)],
        compiler_params=PARAMS,
        name="gram_stage",
    )(coef, even, odd, *totals)


def basis_kernel(full_ref, mix_ref, out_ref):
    mix_high, mix_low = halves(mix_ref[...])
    for m in range(full_ref.shape[0]):
        for p in range(2):
            high, low = halves(full_ref[m, p])
            value = jnp.dot(
                jnp.concatenate([high, low], axis=1),
                jnp.concatenate([mix_high, mix_high], axis=0),
                preferred_element_type=F32,
            ) + jnp.dot(high, mix_low, preferred_element_type=F32)
            out_ref[m, p] = value.astype(BF16)


def basis_stage(full, mix):
    waves, _, degrees, _ = full.shape
    steps = 4
    spec = pl.BlockSpec((waves // steps, 2, degrees, LANES), lambda g: (g, 0, 0, 0))
    return pl.pallas_call(
        basis_kernel,
        grid=(steps,),
        in_specs=[spec, whole_spec((LANES, LANES))],
        out_specs=spec,
        out_shape=jax.ShapeDtypeStruct(full.shape, BF16),
        compiler_params=PARAMS,
        name="basis_stage",
    )(full, mix)


def exchange(blocks):
    return lax.all_to_all(blocks, "lat", split_axis=0, concat_axis=0, tiled=True)


def from_levels(part):
    count = lax.axis_size("lev")
    return [
        lax.ppermute(part, "lev", [(i, (i + k) % count) for i in range(count)])
        for k in range(1, count)
    ]


def total_gram(gram_copies):
    lev_count = lax.axis_size("lev")
    lev_index = lax.axis_index("lev")
    over_lat = jnp.sum(exchange(gram_copies), axis=0)
    parts = jnp.stack([over_lat] + from_levels(over_lat))
    ordered = jnp.take(parts, (lev_index - jnp.arange(lev_count)) % lev_count, axis=0)
    return jnp.sum(ordered, axis=0).reshape(PROBES, PROBES)


def shards(
    probes, legendre, quad_weight, trunc_counts, background, level_up, level_down, viscosity
):
    lat_count = lax.axis_size("lat")
    lev_count = lax.axis_size("lev")
    lat_index = lax.axis_index("lat")
    lev_index = lax.axis_index("lev")
    wave_local = probes.shape[0]
    level_local = probes.shape[3] // (2 * PROBES)
    lon_count = 2 * M

    def own_lanes(values):
        own = lax.dynamic_slice_in_dim(values, lev_index * level_local, level_local, 0)
        return jnp.repeat(own, 2 * PROBES)[None, :]

    up_lanes = own_lanes(level_up)
    down_lanes = own_lanes(level_down)
    visc_lanes = own_lanes(viscosity)
    wave_first = (lat_index * wave_local).astype(jnp.int32).reshape(1)

    own_gain = lax.dynamic_slice_in_dim(background, lev_index * level_local, level_local, 2)
    own_gain = own_gain * (quad_weight / float(lon_count))[None, :, None, None]
    own_gain = own_gain.reshape(2, own_gain.shape[1], level_local * 2, M)
    gain_high = lax.reduce_precision(own_gain, 8, 7)
    gain_low = own_gain - gain_high
    gain = jnp.concatenate([gain_high, gain_low], axis=2).astype(BF16)

    partial = level_partial(probes, down_lanes)
    arrived = {}
    for p in range(2):
        others = from_levels(partial[p : p + 1])
        sent = legendre_forward(probes, [partial] + others, legendre, up_lanes, p)
        arrived[p] = exchange(sent)
    folded = {}

    def depart(p, values):
        folded[p] = exchange(values)

    grid_pass(lambda p: arrived[p], depart, trunc_counts, gain, True, False)
    second = {
        p: exchange(middle_stage(folded[p], legendre, visc_lanes, wave_first, p))
        for p in range(2)
    }
    folded2 = {}

    def depart2(p, values):
        folded2[p] = exchange(values)

    grid_pass(lambda p: second[p], depart2, trunc_counts, gain, False, True)
    images, totals = [], []
    for p in range(2):
        image, part = image_stage(folded2[p], legendre, up_lanes, p)
        images.append(image)
        totals += [part] + from_levels(part)
    full, gram_copies = gram_stage(images[0], images[1], totals, down_lanes, lat_count)
    gram_matrix = total_gram(gram_copies)
    lower_factor = jnp.linalg.cholesky(gram_matrix)
    inverse = lax.linalg.triangular_solve(
        lower_factor, jnp.eye(PROBES, dtype=F32), left_side=True, lower=True
    )
    row_scale = math.sqrt(M * K * 2 * level_local * lev_count)
    mix = jnp.kron(jnp.eye(LANES // PROBES, dtype=F32), row_scale * inverse.T)
    basis_out = basis_stage(full, mix)
    factor = lower_factor.T / row_scale
    return (basis_out, factor)


def solution(mesh):
    placed = (
        P("lat", None, None, "lev"),
        P("lat", None, None, None),
        P("lat"),
        P("lat"),
        P(None, "lat", None, None),
        P(),
        P(),
        P(),
    )
    return jax.shard_map(
        shards,
        mesh=mesh,
        in_specs=placed,
        out_specs=(P("lat", None, None, "lev"), P()),
        check_vma=False,
    )
```

```python
import functools
import math

import jax
import jax.numpy as jnp
import ml_dtypes
import numpy as np
from jax import lax
from jax.experimental import pallas as pl
from jax.experimental.pallas import tpu as pltpu
from jax.sharding import PartitionSpec as P


M = 512
K = 512
PROBES = 16
LANES = 128
F32 = jnp.float32
BF16 = jnp.bfloat16


def params(mib):
    return pltpu.CompilerParams(vmem_limit_bytes=mib << 20)


def in_hbm(values):
    return pltpu.with_memory_space_constraint(values, pltpu.HBM)


def hbm_result(shape, dtype):
    return pltpu.HBM(shape, dtype)


def wave_tables(wave_count):
    lon = np.arange(wave_count)[:, None]
    tables = []
    for parity in range(2):
        zonal = np.arange(parity, wave_count, 2)[None, :]
        phase = (zonal * lon % (2 * wave_count)) * (math.pi / wave_count)
        tables.append(np.concatenate([np.cos(phase), -np.sin(phase)], axis=1))
    return np.stack(tables).astype(np.float32).astype(ml_dtypes.bfloat16)


def spread_table():
    rows = np.arange(8)[:, None]
    lanes = np.arange(LANES)[None, :] // PROBES
    return (rows == lanes).astype(ml_dtypes.bfloat16)


def lane_ids(rows, lanes=LANES):
    return lax.broadcasted_iota(jnp.int32, (rows, lanes), 1)


def row_ids(rows, lanes=LANES):
    return lax.broadcasted_iota(jnp.int32, (rows, lanes), 0)


def halves(values):
    high = values.astype(BF16)
    return high, (values - high.astype(F32)).astype(BF16)


def slot(wave):
    return (wave & 1) * 8 + (wave >> 1)


def own_levels(coef_ref, lev_ref, level):
    first = lev_ref[0] * 4
    coef = jnp.where(level == 0, coef_ref[first], coef_ref[first + 1])
    return jnp.where(
        level < 2, coef, jnp.where(level == 2, coef_ref[first + 2], coef_ref[first + 3])
    )


def sum_matrix(coef_ref, lev_ref):
    rows = row_ids(LANES)
    weights = jnp.where(
        (rows & 31) == (lane_ids(LANES) & 31), own_levels(coef_ref, lev_ref, rows // 32), 0.0
    )
    return jnp.concatenate(halves(weights), axis=0)


def unpack_matrix(coef_ref, lev_ref):
    rows = row_ids(LANES, 4 * LANES)
    lanes = lane_ids(LANES, 4 * LANES)
    level = (lanes & (LANES - 1)) // 32
    hit = (rows // 32 == lanes // LANES) & ((rows & 31) == (lanes & 31))
    weights = jnp.where(hit, own_levels(coef_ref, lev_ref, level), 0.0)
    return jnp.concatenate(halves(weights), axis=0)


def twice(values):
    return jnp.concatenate([values, values], axis=1)


def pack_levels(summed):
    rows = summed.shape[0] // 4
    group = lane_ids(rows) // 32
    low = jnp.where(group == 0, summed[0:rows], summed[rows : 2 * rows])
    high = jnp.where(group == 2, summed[2 * rows : 3 * rows], summed[3 * rows :])
    return jnp.where(group < 2, low, high)


def unpack_levels(packed, matrix):
    wide = jnp.dot(twice(packed), matrix, preferred_element_type=F32)
    return jnp.concatenate([wide[:, g * LANES : (g + 1) * LANES] for g in range(4)], axis=0)


def add_totals(refs, m):
    parts = [ref[m].astype(F32) for ref in refs]
    return ((parts[0] + parts[1]) + (parts[2] + parts[3])).astype(BF16)


def smem_spec():
    return pl.BlockSpec(memory_space=pltpu.SMEM)


def whole_spec(shape):
    return pl.BlockSpec(shape, lambda g: (0,) * len(shape))


def partial_kernel(coef_ref, lev_ref, probes_ref, out_ref):
    matrix = sum_matrix(coef_ref, lev_ref)
    for m in range(probes_ref.shape[0]):
        summed = jnp.dot(twice(probes_ref[m, 0]), matrix, preferred_element_type=F32)
        out_ref[m] = pack_levels(summed).astype(BF16)


def level_partial(probes, coef, lev, parity):
    waves, _, degrees, _ = probes.shape
    steps = 2
    return pl.pallas_call(
        partial_kernel,
        grid=(steps,),
        in_specs=[
            smem_spec(),
            smem_spec(),
            pl.BlockSpec((waves // steps, 1, degrees, LANES), lambda g: (g, parity, 0, 0)),
        ],
        out_specs=pl.BlockSpec((waves // steps, degrees // 4, LANES), lambda g: (g, 0, 0)),
        out_shape=jax.ShapeDtypeStruct((waves, degrees // 4, LANES), BF16),
        compiler_params=params(8),
        name="level_partial",
    )(coef, lev, in_hbm(probes))


def legendre_kernel(coef_ref, lev_ref, probes_ref, *refs):
    totals = refs[:4]
    table_ref, out_ref, mixed, turned = refs[4:]
    waves = probes_ref.shape[0]
    rows = table_ref.shape[2]

    @pl.when(pl.program_id(0) == 0)
    def _():
        matrix = unpack_matrix(coef_ref, lev_ref)

        def mix(m, carry):
            total = add_totals(totals, m)
            mixed[m] = (probes_ref[m, 0].astype(F32) + unpack_levels(total, matrix)).astype(BF16)
            return carry

        lax.fori_loop(0, waves, mix, 0, unroll=4)

    def transform(m, carry):
        turned[pl.ds(slot(m), rows, stride=waves), :] = jnp.dot(
            table_ref[m, 0], mixed[m], preferred_element_type=F32
        )
        return carry

    lax.fori_loop(0, waves, transform, 0, unroll=4)
    out_ref[...] = turned[...].astype(BF16).reshape(out_ref.shape)


def legendre_forward(probes, totals, legendre, coef, lev, parity):
    waves, _, degrees, _ = probes.shape
    lats = legendre.shape[2]
    blocks = lats // waves
    steps = 4
    total_spec = whole_spec(totals[0].shape)
    return pl.pallas_call(
        legendre_kernel,
        grid=(steps,),
        in_specs=[
            smem_spec(),
            smem_spec(),
            pl.BlockSpec((waves, 1, degrees, LANES), lambda g: (0, parity, 0, 0)),
        ]
        + [total_spec] * 4
        + [pl.BlockSpec((waves, 1, lats // steps, degrees), lambda g: (0, parity, g, 0))],
        out_specs=pl.BlockSpec((blocks // steps, waves, waves, LANES), lambda g: (g, 0, 0, 0)),
        out_shape=hbm_result((blocks, waves, waves, LANES), BF16),
        scratch_shapes=[
            pltpu.VMEM((waves, degrees, LANES), BF16),
            pltpu.VMEM((lats // steps * waves, LANES), F32),
        ],
        compiler_params=params(14),
        name="legendre_forward",
    )(coef, lev, in_hbm(probes), *totals, in_hbm(legendre))


HALF = M // 2


def mask_rows(count, parity):
    zonal = 2 * row_ids(HALF) + parity
    factor = jnp.where(zonal == 0, 1.0, 2.0)
    return jnp.where(zonal < count, factor, 0.0).astype(F32)


def load_waves(counts_ref, x_ref, operand, masked):
    step = pl.program_id(0)
    real_lane = (lane_ids(HALF) & PROBES) == 0
    for pair in range(2):
        both = [x_ref[:, 2 * pair + k].astype(F32) for k in range(2)]
        lanes = slice(pair * LANES, (pair + 1) * LANES)
        for parity in range(2):
            first, second = [
                x[:, 8 * parity : 8 * parity + 8].reshape(HALF, LANES) for x in both
            ]
            if masked:
                first = first * mask_rows(counts_ref[4 * step + 2 * pair], parity)
                second = second * mask_rows(counts_ref[4 * step + 2 * pair + 1], parity)
            operand[parity, :HALF, lanes] = jnp.where(
                real_lane, first, pltpu.roll(second, PROBES, 1)
            ).astype(BF16)
            operand[parity, HALF:, lanes] = jnp.where(
                real_lane, pltpu.roll(first, LANES - PROBES, 1), second
            ).astype(BF16)


def store_waves(counts_ref, fields, table_ref, out_ref, masked):
    step = pl.program_id(0)
    real_lane = (lane_ids(HALF) & PROBES) == 0
    results = {}
    for parity in range(2):
        cos_part = jnp.dot(table_ref[parity, :HALF], fields[parity], preferred_element_type=F32)
        sin_part = jnp.dot(table_ref[parity, HALF:], fields[parity], preferred_element_type=F32)
        for pair in range(2):
            cosine = cos_part[:, pair * LANES : (pair + 1) * LANES]
            sine = sin_part[:, pair * LANES : (pair + 1) * LANES]
            first = jnp.where(real_lane, cosine, pltpu.roll(sine, PROBES, 1))
            second = jnp.where(real_lane, pltpu.roll(cosine, LANES - PROBES, 1), sine)
            if masked:
                first = first * mask_rows(counts_ref[4 * step + 2 * pair], parity)
                second = second * mask_rows(counts_ref[4 * step + 2 * pair + 1], parity)
            results[2 * pair, parity] = first.reshape(-1, 8, LANES)
            results[2 * pair + 1, parity] = second.reshape(-1, 8, LANES)
    for k in range(4):
        out_ref[:, k] = jnp.concatenate([results[k, 0], results[k, 1]], axis=1).astype(BF16)


def grid_even_kernel(counts_ref, x_ref, table_ref, out_ref, operand, *, masked):
    load_waves(counts_ref, x_ref, operand, masked)
    even = jnp.dot(table_ref[0], operand[0], preferred_element_type=F32)
    odd = jnp.dot(table_ref[1], operand[1], preferred_element_type=F32)
    out_ref[0, 0] = even + odd
    out_ref[0, 1] = even - odd


def grid_middle_kernel(
    counts_ref, x_ref, even_ref, gain_ref, forward_ref, inverse_ref, out_ref, odd_ref,
    operand, fields, *, masked_in, masked_out,
):
    load_waves(counts_ref, x_ref, operand, masked_in)
    size = 256
    for r in range(0, M, size):
        rows = slice(r, r + size)
        even = jnp.dot(forward_ref[0, rows], operand[0], preferred_element_type=F32)
        odd = jnp.dot(forward_ref[1, rows], operand[1], preferred_element_type=F32)
        for pair in range(2):
            lanes = slice(pair * LANES, (pair + 1) * LANES)
            kept = []
            for half, sent in enumerate((even[:, lanes] + odd[:, lanes], even[:, lanes] - odd[:, lanes])):
                base = even_ref[0, half, rows, lanes]
                longitudes = slice(half * M + r, half * M + r + size)
                north = gain_ref[0, pair, longitudes].astype(F32) * (base + sent)
                south = gain_ref[1, pair, longitudes].astype(F32) * (base - sent)
                kept.append((north + south, north - south))
            fields[0, rows, lanes] = (kept[0][0] + kept[1][0]).astype(BF16)
            fields[1, rows, lanes] = (kept[0][0] - kept[1][0]).astype(BF16)
            odd_ref[0, 0, rows, lanes] = (kept[0][1] + kept[1][1]).astype(BF16)
            odd_ref[0, 1, rows, lanes] = (kept[0][1] - kept[1][1]).astype(BF16)
    store_waves(counts_ref, fields, inverse_ref, out_ref, masked_out)


def grid_odd_kernel(counts_ref, odd_ref, table_ref, out_ref, *, masked):
    store_waves(counts_ref, odd_ref[0], table_ref, out_ref, masked)


def gain_kernel(gain_ref, spread_ref, out_ref):
    for h in range(2):
        out_ref[h, 0] = lax.dot_general(
            gain_ref[h, 0], spread_ref[...], (((0,), (0,)), ((), ())), preferred_element_type=F32
        ).astype(BF16)


def spread_gain(gain):
    pairs = gain.shape[1]
    return pl.pallas_call(
        gain_kernel,
        grid=(pairs,),
        in_specs=[
            pl.BlockSpec((2, 1, 8, 2 * M), lambda g: (0, g, 0, 0)),
            whole_spec((8, LANES)),
        ],
        out_specs=pl.BlockSpec((2, 1, 2 * M, LANES), lambda g: (0, g, 0, 0)),
        out_shape=hbm_result((2, pairs, 2 * M, LANES), BF16),
        compiler_params=params(8),
        name="spread_gain",
    )(gain, jnp.asarray(spread_table()))


def wave_block(x):
    return pl.BlockSpec((x.shape[0], 4, x.shape[2], LANES), lambda g: (0, g, 0, 0))


def grid_pass(arrive, depart, counts, gain, tables, masked_in, masked_out):
    forward, inverse = tables
    x_even = arrive(0)
    steps = x_even.shape[1] // 4
    field_spec = pl.BlockSpec((1, 2, M, 2 * LANES), lambda g: (g, 0, 0, 0))
    field_shape = (steps, 2, M, 2 * LANES)
    operand = pltpu.VMEM((2, M, 2 * LANES), BF16)
    even = pl.pallas_call(
        functools.partial(grid_even_kernel, masked=masked_in),
        grid=(steps,),
        in_specs=[smem_spec(), wave_block(x_even), whole_spec(forward.shape)],
        out_specs=field_spec,
        out_shape=hbm_result(field_shape, F32),
        scratch_shapes=[operand],
        compiler_params=params(16),
        name="grid_even",
    )(counts, in_hbm(x_even), in_hbm(forward))
    x_odd = arrive(1)
    out_shape = hbm_result(x_odd.shape, BF16)
    y_even, odd = pl.pallas_call(
        functools.partial(grid_middle_kernel, masked_in=masked_in, masked_out=masked_out),
        grid=(steps,),
        in_specs=[
            smem_spec(),
            wave_block(x_odd),
            field_spec,
            pl.BlockSpec((2, 2, 2 * M, LANES), lambda g: (0, g, 0, 0)),
            whole_spec(forward.shape),
            whole_spec(inverse.shape),
        ],
        out_specs=(wave_block(x_odd), field_spec),
        out_shape=(out_shape, hbm_result(field_shape, BF16)),
        scratch_shapes=[operand, operand],
        compiler_params=params(24),
        name="grid_middle",
    )(counts, x_odd, in_hbm(even), in_hbm(gain), in_hbm(forward), in_hbm(inverse))
    depart(0, y_even)
    y_odd = odd_stage(counts, odd, inverse, x_odd, masked_out)
    depart(1, y_odd)


def odd_stage(counts, odd, inverse, like, masked_out):
    steps = odd.shape[0]
    field_spec = pl.BlockSpec((1, 2, M, 2 * LANES), lambda g: (g, 0, 0, 0))
    return pl.pallas_call(
        functools.partial(grid_odd_kernel, masked=masked_out),
        grid=(steps,),
        in_specs=[smem_spec(), field_spec, whole_spec(inverse.shape)],
        out_specs=wave_block(like),
        out_shape=hbm_result(like.shape, BF16),
        compiler_params=params(16),
        name="grid_odd",
    )(counts, in_hbm(odd), in_hbm(inverse))


def spread_rows(x_ref, scratch):
    chunk = 4
    per = x_ref.shape[1] * x_ref.shape[2]

    def widen(b, carry):
        scratch[pl.ds(b * chunk * per, chunk * per), :] = (
            x_ref[pl.ds(b * chunk, chunk)].astype(F32).reshape(chunk * per, LANES)
        )
        return carry

    lax.fori_loop(0, x_ref.shape[0] // chunk, widen, 0, unroll=2)


def transform_of(table, fields):
    return lax.dot_general(table, fields, (((0,), (0,)), ((), ())), preferred_element_type=F32)


def middle_kernel(first_ref, visc_ref, lev_ref, x_ref, table_ref, out_ref, taken, turned, *, parity):
    waves = x_ref.shape[2]
    lats = x_ref.shape[0] * x_ref.shape[1]
    degrees = table_ref.shape[3]
    spread_rows(x_ref, taken)
    visc = own_levels(visc_ref, lev_ref, lane_ids(degrees) // 32)

    def one_wave(m, carry):
        fields = taken[pl.ds(slot(m), lats, stride=waves), :].astype(BF16)
        table = table_ref[m, 0]
        tangent = transform_of(table, fields)
        degree = first_ref[0] + m + parity + 2 * row_ids(degrees)
        scaled = (degree * (degree + 1)).astype(F32) / float((M + K) * (M + K + 1))
        damp = 1.0 / (1.0 + scaled * visc)
        damped = (tangent * (damp * damp)).astype(BF16)
        turned[pl.ds(slot(m), lats, stride=waves), :] = jnp.dot(
            table, damped, preferred_element_type=F32
        )
        return carry

    lax.fori_loop(0, waves, one_wave, 0, unroll=2)
    per = x_ref.shape[1] * waves

    def narrow(b, carry):
        out_ref[pl.ds(b * 4, 4)] = (
            turned[pl.ds(b * 4 * per, 4 * per), :]
            .astype(BF16)
            .reshape(4, x_ref.shape[1], waves, LANES)
        )
        return carry

    lax.fori_loop(0, x_ref.shape[0] // 4, narrow, 0, unroll=2)


def middle_stage(x, legendre, viscosity, lev, wave_first, parity):
    waves, _, lats, degrees = legendre.shape
    return pl.pallas_call(
        functools.partial(middle_kernel, parity=parity),
        grid=(1,),
        in_specs=[
            smem_spec(),
            smem_spec(),
            smem_spec(),
            whole_spec(x.shape),
            pl.BlockSpec((waves, 1, lats, degrees), lambda g: (0, parity, 0, 0)),
        ],
        out_specs=whole_spec(x.shape),
        out_shape=hbm_result(x.shape, BF16),
        scratch_shapes=[pltpu.VMEM((lats * waves, LANES), F32)] * 2,
        compiler_params=params(26),
        name="middle_stage",
    )(wave_first, viscosity, lev, x, in_hbm(legendre))


def images_kernel(up_ref, down_ref, lev_ref, x_ref, table_ref, out_ref, part_ref, low_ref, taken):
    waves = x_ref.shape[2]
    lats = x_ref.shape[0] * x_ref.shape[1]
    count = table_ref.shape[0]
    step = pl.program_id(0)

    @pl.when(step == 0)
    def _():
        spread_rows(x_ref, taken)

    up_matrix = sum_matrix(up_ref, lev_ref)
    down_matrix = sum_matrix(down_ref, lev_ref)
    for k in range(count):
        fields = taken[pl.ds(slot(step * count + k), lats, stride=waves), :].astype(BF16)
        image = transform_of(table_ref[k, 0], fields)
        high, low = halves(image)
        out_ref[k] = jnp.concatenate([high, low], axis=1)
        up_sum = jnp.dot(twice(high), up_matrix, preferred_element_type=F32)
        part_ref[k] = pack_levels(up_sum).astype(BF16)
        down_sum = jnp.dot(twice(high), down_matrix, preferred_element_type=F32) + jnp.dot(
            low, down_matrix[:LANES], preferred_element_type=F32
        )
        low_ref[k] = jnp.concatenate(halves(pack_levels(down_sum)), axis=1)


def image_stage(x, legendre, up, down, lev, parity):
    x = in_hbm(x) if parity == 0 else x
    waves, _, lats, degrees = legendre.shape
    steps = 4
    count = waves // steps
    return pl.pallas_call(
        images_kernel,
        grid=(steps,),
        in_specs=[
            smem_spec(),
            smem_spec(),
            smem_spec(),
            whole_spec(x.shape),
            pl.BlockSpec((count, 1, lats, degrees), lambda g: (g, parity, 0, 0)),
        ],
        out_specs=(
            pl.BlockSpec((count, degrees, 2 * LANES), lambda g: (g, 0, 0)),
            pl.BlockSpec((count, degrees // 4, LANES), lambda g: (g, 0, 0)),
            pl.BlockSpec((count, degrees // 4, 2 * LANES), lambda g: (g, 0, 0)),
        ),
        out_shape=(
            hbm_result((waves, degrees, 2 * LANES), BF16),
            jax.ShapeDtypeStruct((waves, degrees // 4, LANES), BF16),
            hbm_result((waves, degrees // 4, 2 * LANES), BF16),
        ),
        scratch_shapes=[pltpu.VMEM((lats * waves, LANES), F32)],
        compiler_params=params(20),
        name="image_stage",
    )(up, down, lev, x, in_hbm(legendre))


def gram_of(high, both):
    return lax.dot_general(high, both, (((0,), (0,)), ((), ())), preferred_element_type=F32)


def gram_kernel(image_ref, out_ref):
    @pl.when(pl.program_id(0) == 0)
    def _():
        out_ref[...] = jnp.zeros_like(out_ref)

    rows = image_ref.shape[0] * image_ref.shape[1]
    both = image_ref[...].reshape(rows, 2 * LANES)
    out_ref[...] += gram_of(both[:, :LANES], both)


def gram_stage(images):
    waves, degrees, _ = images.shape
    steps = 4
    return pl.pallas_call(
        gram_kernel,
        grid=(steps,),
        in_specs=[pl.BlockSpec((waves // steps, degrees, 2 * LANES), lambda g: (g, 0, 0))],
        out_specs=whole_spec((LANES, 2 * LANES)),
        out_shape=jax.ShapeDtypeStruct((LANES, 2 * LANES), F32),
        compiler_params=params(12),
        name="gram_stage",
    )(in_hbm(images))


def finish_kernel(down_ref, lev_ref, *refs):
    first = lev_ref[0] * 4
    square = down_ref[first] * down_ref[first]
    for k in range(1, 4):
        square = square + down_ref[first + k] * down_ref[first + k]
    grams = refs[:2]
    lows = refs[2:4]
    totals = refs[4:12]
    total_ref, gram_ref = refs[12:]
    sums = grams[0][...] + grams[1][...]
    cross = sums[:, LANES:]
    gram = sums[:, :LANES] + (cross + cross.T)
    for p in range(2):
        parts = [ref[...].astype(F32) for ref in totals[4 * p : 4 * p + 4]]
        total = ((parts[0] + parts[1]) + (parts[2] + parts[3])).astype(BF16)
        total_ref[p] = total
        flat = total.reshape(-1, LANES)
        low = lows[p][...].reshape(-1, 2 * LANES)
        operand = jnp.concatenate([flat, low], axis=1)
        result = gram_of(flat, operand)
        mixed = result[:, LANES : 2 * LANES] + result[:, 2 * LANES :]
        gram = gram + square * result[:, :LANES] + (mixed + mixed.T)
    same = (row_ids(LANES) // PROBES) == (lane_ids(LANES) // PROBES)
    gram = jnp.where(same, gram, 0.0)
    summed = gram[0:PROBES]
    for b in range(1, LANES // PROBES):
        summed = summed + gram[b * PROBES : (b + 1) * PROBES]
    for shift in (64, 32, 16):
        summed = summed + pltpu.roll(summed, shift, 1)
    gram_ref[...] = jnp.broadcast_to(summed[None], gram_ref.shape)


def finish_stage(grams, lows, totals, down, lev, copies):
    shape = totals[0].shape
    return pl.pallas_call(
        finish_kernel,
        in_specs=[smem_spec(), smem_spec()] + [pl.BlockSpec(memory_space=pltpu.VMEM)] * 12,
        out_shape=(
            hbm_result((2,) + shape, BF16),
            hbm_result((copies, PROBES, LANES), F32),
        ),
        compiler_params=params(16),
        name="finish_stage",
    )(down, lev, *grams, *lows, *totals)


def factor_of(gram):
    rows = row_ids(PROBES)
    lanes = lane_ids(PROBES) & (PROBES - 1)
    upper = jnp.zeros_like(gram)
    inverse = jnp.where(rows == lanes, 1.0, 0.0).astype(F32)
    for k in range(PROBES):
        scale = lax.rsqrt(gram[k : k + 1, k : k + 1])
        scale = scale * (1.5 - 0.5 * gram[k : k + 1, k : k + 1] * scale * scale)
        line = jnp.where(lanes[0:1] >= k, gram[k : k + 1] * scale, 0.0)
        solved = inverse[k : k + 1] * scale
        column = jnp.where(rows[:, 0:1] > k, gram[:, k : k + 1] * scale, 0.0)
        upper = jnp.where(rows == k, line, upper)
        gram = gram - column * line
        inverse = jnp.where(rows == k, solved, inverse - column * solved)
    return upper, inverse


def basis_kernel(
    down_ref, lev_ref, own_ref, one_ref, two_ref, three_ref, even_ref, odd_ref, total_ref,
    out_ref, factor_ref, mix, *, row_scale,
):
    @pl.when(pl.program_id(0) == 0)
    def _():
        gram = (own_ref[...] + two_ref[...]) + (one_ref[...] + three_ref[...])
        upper, inverse = factor_of(gram)
        factor_ref[...] = upper[:, :PROBES] / row_scale
        pick = ((lane_ids(PROBES) & (PROBES - 1)) == row_ids(PROBES)).astype(BF16)
        same = (row_ids(LANES) // PROBES) == (lane_ids(LANES) // PROBES)
        high, low = halves(inverse * row_scale)
        mix_high = jnp.where(same, gram_of(high, pick), 0.0).astype(BF16)
        mix_low = jnp.where(same, gram_of(low, pick), 0.0).astype(BF16)
        mix[0:LANES] = mix_high
        mix[LANES : 2 * LANES] = mix_high
        mix[2 * LANES :] = mix_low

    matrix = unpack_matrix(down_ref, lev_ref)
    for m in range(even_ref.shape[0]):
        for p, image_ref in enumerate((even_ref, odd_ref)):
            both = image_ref[m]
            full = (both[:, :LANES].astype(F32) + both[:, LANES:].astype(F32)) + unpack_levels(
                total_ref[p, m], matrix
            )
            high, low = halves(full)
            value = jnp.dot(
                jnp.concatenate([high, low, high], axis=1), mix[...], preferred_element_type=F32
            )
            out_ref[m, p] = value.astype(BF16)


def basis_stage(grams, images, total, down, lev, row_scale):
    waves, degrees, _ = images[0].shape
    steps = 4
    count = waves // steps
    image_spec = pl.BlockSpec((count, degrees, 2 * LANES), lambda g: (g, 0, 0))
    return pl.pallas_call(
        functools.partial(basis_kernel, row_scale=row_scale),
        grid=(steps,),
        in_specs=[smem_spec(), smem_spec()]
        + [whole_spec((PROBES, LANES))] * 4
        + [
            image_spec,
            image_spec,
            pl.BlockSpec((2, count, degrees // 4, LANES), lambda g: (0, g, 0, 0)),
        ],
        out_specs=(
            pl.BlockSpec((count, 2, degrees, LANES), lambda g: (g, 0, 0, 0)),
            whole_spec((PROBES, PROBES)),
        ),
        out_shape=(
            hbm_result((waves, 2, degrees, LANES), BF16),
            hbm_result((PROBES, PROBES), F32),
        ),
        scratch_shapes=[pltpu.VMEM((3 * LANES, LANES), BF16)],
        compiler_params=params(14),
        name="basis_stage",
    )(down, lev, *grams, in_hbm(images[0]), in_hbm(images[1]), in_hbm(total))


def exchange(blocks):
    return lax.all_to_all(blocks, "lat", split_axis=0, concat_axis=0, tiled=True)


def from_levels(part):
    count = lax.axis_size("lev")
    return [
        lax.ppermute(part, "lev", [(i, (i + k) % count) for i in range(count)])
        for k in range(1, count)
    ]


def shards(
    probes, legendre, quad_weight, trunc_counts, background, level_up, level_down, viscosity
):
    lat_count = lax.axis_size("lat")
    lev_count = lax.axis_size("lev")
    lat_index = lax.axis_index("lat")
    lev_index = lax.axis_index("lev")
    wave_local = probes.shape[0]
    level_local = probes.shape[3] // (2 * PROBES)
    lon_count = 2 * M

    lev = lev_index.astype(jnp.int32).reshape(1)
    wave_first = (lat_index * wave_local).astype(jnp.int32).reshape(1)
    forward = wave_tables(M)
    tables = (jnp.asarray(forward), jnp.asarray(np.ascontiguousarray(forward.transpose(0, 2, 1))))

    sent = {}
    for p in range(2):
        partial = level_partial(probes, level_down, lev, p)
        totals = [partial] + from_levels(partial)
        blocks = legendre_forward(probes, totals, legendre, level_up, lev, p)
        sent[p] = exchange(blocks)

    own_gain = lax.dynamic_slice_in_dim(background, lev_index * level_local, level_local, 2)
    own_gain = own_gain * (quad_weight / float(lon_count))[None, :, None, None]
    own_gain = own_gain.reshape(2, -1, 2, level_local, lon_count).swapaxes(2, 3)
    own_gain = own_gain.reshape(2, -1, 2 * level_local, lon_count).astype(BF16)
    gain = spread_gain(own_gain)

    folded = {}

    def depart(p, values):
        folded[p] = exchange(values)

    grid_pass(lambda p: sent[p], depart, trunc_counts, gain, tables, True, False)
    second = {
        p: exchange(middle_stage(folded[p], legendre, viscosity, lev, wave_first, p))
        for p in range(2)
    }
    folded2 = {}

    def depart2(p, values):
        folded2[p] = exchange(values)

    grid_pass(lambda p: second[p], depart2, trunc_counts, gain, tables, False, True)
    images, lows, grams, totals = [], [], [], []
    for p in range(2):
        image, part, low = image_stage(folded2[p], legendre, level_up, level_down, lev, p)
        images.append(image)
        lows.append(low)
        grams.append(gram_stage(image))
        totals += [part] + from_levels(part)
    total, gram_copies = finish_stage(grams, lows, totals, level_down, lev, lat_count)
    over_lat = jnp.sum(exchange(gram_copies), axis=0)
    row_scale = math.sqrt(M * K * 2 * level_local * lev_count)
    return basis_stage(
        [over_lat] + from_levels(over_lat), images, total, level_down, lev, row_scale
    )


def solution(mesh):
    placed = (
        P("lat", None, None, "lev"),
        P("lat", None, None, None),
        P("lat"),
        P("lat"),
        P(None, "lat", None, None),
        P(),
        P(),
        P(),
    )
    return jax.shard_map(
        shards,
        mesh=mesh,
        in_specs=placed,
        out_specs=(P("lat", None, None, "lev"), P()),
        check_vma=False,
    )
```

```python
import functools
import math

import jax
import jax.numpy as jnp
import ml_dtypes
import numpy as np
from jax import lax
from jax.experimental import pallas as pl
from jax.experimental.pallas import tpu as pltpu
from jax.sharding import PartitionSpec as P


M = 512
K = 512
PROBES = 16
LANES = 128
F32 = jnp.float32
BF16 = jnp.bfloat16


def params(mib):
    return pltpu.CompilerParams(vmem_limit_bytes=mib << 20)


def in_hbm(values):
    return pltpu.with_memory_space_constraint(values, pltpu.HBM)


def hbm_result(shape, dtype):
    return pltpu.HBM(shape, dtype)


def wave_tables(wave_count):
    lon = np.arange(wave_count)[:, None]
    tables = []
    for parity in range(2):
        zonal = np.arange(parity, wave_count, 2)[None, :]
        phase = (zonal * lon % (2 * wave_count)) * (math.pi / wave_count)
        tables.append(np.concatenate([np.cos(phase), -np.sin(phase)], axis=1))
    return np.stack(tables).astype(np.float32).astype(ml_dtypes.bfloat16)


def spread_table():
    rows = np.arange(8)[:, None]
    lanes = np.arange(LANES)[None, :] // PROBES
    return (rows == lanes).astype(ml_dtypes.bfloat16)


def lane_ids(rows, lanes=LANES):
    return lax.broadcasted_iota(jnp.int32, (rows, lanes), 1)


def row_ids(rows, lanes=LANES):
    return lax.broadcasted_iota(jnp.int32, (rows, lanes), 0)


def halves(values):
    high = values.astype(BF16)
    return high, (values - high.astype(F32)).astype(BF16)


def slot(wave):
    return (wave & 1) * 8 + (wave >> 1)


def own_levels(coef_ref, lev_ref, level):
    first = lev_ref[0] * 4
    coef = jnp.where(level == 0, coef_ref[first], coef_ref[first + 1])
    return jnp.where(
        level < 2, coef, jnp.where(level == 2, coef_ref[first + 2], coef_ref[first + 3])
    )


def sum_matrix(coef_ref, lev_ref):
    rows = row_ids(LANES)
    weights = jnp.where(
        (rows & 31) == (lane_ids(LANES) & 31), own_levels(coef_ref, lev_ref, rows // 32), 0.0
    )
    return jnp.concatenate(halves(weights), axis=0)


def unpack_matrix(coef_ref, lev_ref):
    rows = row_ids(LANES, 4 * LANES)
    lanes = lane_ids(LANES, 4 * LANES)
    level = (lanes & (LANES - 1)) // 32
    hit = (rows // 32 == lanes // LANES) & ((rows & 31) == (lanes & 31))
    weights = jnp.where(hit, own_levels(coef_ref, lev_ref, level), 0.0)
    return jnp.concatenate(halves(weights), axis=0)


def twice(values):
    return jnp.concatenate([values, values], axis=1)


def pack_levels(summed):
    rows = summed.shape[0] // 4
    group = lane_ids(rows) // 32
    low = jnp.where(group == 0, summed[0:rows], summed[rows : 2 * rows])
    high = jnp.where(group == 2, summed[2 * rows : 3 * rows], summed[3 * rows :])
    return jnp.where(group < 2, low, high)


def unpack_levels(packed, matrix):
    wide = jnp.dot(twice(packed), matrix, preferred_element_type=F32)
    return jnp.concatenate([wide[:, g * LANES : (g + 1) * LANES] for g in range(4)], axis=0)


def add_totals(refs, m):
    parts = [ref[m].astype(F32) for ref in refs]
    return ((parts[0] + parts[1]) + (parts[2] + parts[3])).astype(BF16)


def smem_spec():
    return pl.BlockSpec(memory_space=pltpu.SMEM)


def whole_spec(shape):
    return pl.BlockSpec(shape, lambda g: (0,) * len(shape))


def partial_kernel(coef_ref, lev_ref, probes_ref, out_ref):
    matrix = sum_matrix(coef_ref, lev_ref)
    for m in range(probes_ref.shape[0]):
        summed = jnp.dot(twice(probes_ref[m, 0]), matrix, preferred_element_type=F32)
        out_ref[m] = pack_levels(summed).astype(BF16)


def level_partial(probes, coef, lev, parity):
    waves, _, degrees, _ = probes.shape
    steps = 2
    return pl.pallas_call(
        partial_kernel,
        grid=(steps,),
        in_specs=[
            smem_spec(),
            smem_spec(),
            pl.BlockSpec((waves // steps, 1, degrees, LANES), lambda g: (g, parity, 0, 0)),
        ],
        out_specs=pl.BlockSpec((waves // steps, degrees // 4, LANES), lambda g: (g, 0, 0)),
        out_shape=jax.ShapeDtypeStruct((waves, degrees // 4, LANES), BF16),
        compiler_params=params(8),
        name="level_partial",
    )(coef, lev, in_hbm(probes))


def legendre_raw_kernel(probes_ref, table_ref, out_ref, turned):
    waves = probes_ref.shape[0]
    rows = table_ref.shape[2]
    for m in range(waves):
        turned[pl.ds(slot(m), rows, stride=waves), :] = jnp.dot(
            table_ref[m, 0], probes_ref[m, 0], preferred_element_type=F32
        )
    out_ref[...] = turned[...].astype(BF16).reshape(out_ref.shape)


def legendre_raw(probes, legendre, parity):
    waves, _, degrees, _ = probes.shape
    lats = legendre.shape[2]
    blocks = lats // waves
    steps = 4
    return pl.pallas_call(
        legendre_raw_kernel,
        grid=(steps,),
        in_specs=[
            pl.BlockSpec((waves, 1, degrees, LANES), lambda g: (0, parity, 0, 0)),
            pl.BlockSpec((waves, 1, lats // steps, degrees), lambda g: (0, parity, g, 0)),
        ],
        out_specs=pl.BlockSpec((blocks // steps, waves, waves, LANES), lambda g: (g, 0, 0, 0)),
        out_shape=hbm_result((blocks, waves, waves, LANES), BF16),
        scratch_shapes=[pltpu.VMEM((lats // steps * waves, LANES), F32)],
        compiler_params=params(14),
        name="legendre_raw",
    )(in_hbm(probes), in_hbm(legendre))


def grid_sum_kernel(coef_ref, lev_ref, x_ref, out_ref):
    matrix = sum_matrix(coef_ref, lev_ref)
    blocks, _, waves, _ = x_ref.shape
    group = lane_ids(blocks * waves) // 32
    for k in range(4):
        packed = None
        for g in range(4):
            x = x_ref[:, 4 * g + k].reshape(blocks * waves, LANES)
            summed = jnp.dot(twice(x), matrix, preferred_element_type=F32)
            packed = summed if g == 0 else jnp.where(group == g, summed, packed)
        out_ref[:, k] = packed.astype(BF16).reshape(blocks, waves, LANES)


def grid_sum(x, coef, lev):
    blocks, lats, waves, _ = x.shape
    steps = 4
    return pl.pallas_call(
        grid_sum_kernel,
        grid=(steps,),
        in_specs=[
            smem_spec(),
            smem_spec(),
            pl.BlockSpec((blocks // steps, lats, waves, LANES), lambda g: (g, 0, 0, 0)),
        ],
        out_specs=pl.BlockSpec((blocks // steps, 4, waves, LANES), lambda g: (g, 0, 0, 0)),
        out_shape=jax.ShapeDtypeStruct((blocks, 4, waves, LANES), BF16),
        compiler_params=params(12),
        name="grid_sum",
    )(coef, lev, in_hbm(x))


def grid_total_kernel(counts_ref, *refs):
    totals = refs[:4]
    table_ref, out_ref, operand = refs[4:]
    real_lane = (lane_ids(HALF) & PROBES) == 0
    group = lane_ids(HALF) // 32
    zonal = 2 * row_ids(HALF)
    for pair in range(2):
        both = []
        for k in range(2):
            parts = [ref[:, 2 * pair + k].astype(F32) for ref in totals]
            both.append((parts[0] + parts[1]) + (parts[2] + parts[3]))
        lanes = slice(pair * LANES, (pair + 1) * LANES)
        for parity in range(2):
            masked = []
            for k in range(2):
                x = both[k][:, 8 * parity : 8 * parity + 8].reshape(HALF, LANES)
                lat = 2 * pair + k
                count = jnp.where(
                    group < 2,
                    jnp.where(group == 0, counts_ref[lat], counts_ref[4 + lat]),
                    jnp.where(group == 2, counts_ref[8 + lat], counts_ref[12 + lat]),
                )
                factor = jnp.where(zonal + parity == 0, 1.0, 2.0)
                masked.append(x * jnp.where(zonal + parity < count, factor, 0.0))
            first, second = masked
            operand[parity, :HALF, lanes] = jnp.where(
                real_lane, first, pltpu.roll(second, PROBES, 1)
            ).astype(BF16)
            operand[parity, HALF:, lanes] = jnp.where(
                real_lane, pltpu.roll(first, LANES - PROBES, 1), second
            ).astype(BF16)
    even = jnp.dot(table_ref[0], operand[0], preferred_element_type=F32)
    odd = jnp.dot(table_ref[1], operand[1], preferred_element_type=F32)
    out_ref[0] = (even + odd).astype(BF16)
    out_ref[1] = (even - odd).astype(BF16)


def grid_total(counts, totals, forward):
    shape = (2, M, 2 * LANES)
    vmem = pl.BlockSpec(memory_space=pltpu.VMEM)
    return pl.pallas_call(
        grid_total_kernel,
        in_specs=[smem_spec()] + [vmem] * 5,
        out_shape=hbm_result(shape, BF16),
        scratch_shapes=[pltpu.VMEM(shape, BF16)],
        compiler_params=params(12),
        name="grid_total",
    )(counts, *totals, forward)


def place_matrix(coef_ref, lev_ref, taken_group):
    rows = row_ids(LANES)
    lanes = lane_ids(LANES)
    hit = (rows // 32 == taken_group) & ((rows & 31) == (lanes & 31))
    weights = jnp.where(hit, own_levels(coef_ref, lev_ref, lanes // 32), 0.0)
    return jnp.concatenate(halves(weights), axis=0)


def legendre_kernel(coef_ref, lev_ref, probes_ref, *refs):
    totals = refs[:4]
    table_ref, out_ref, mixed, turned = refs[4:]
    waves = probes_ref.shape[0]
    rows = table_ref.shape[2]

    @pl.when(pl.program_id(0) == 0)
    def _():
        matrix = unpack_matrix(coef_ref, lev_ref)

        def mix(m, carry):
            total = add_totals(totals, m)
            mixed[m] = (probes_ref[m, 0].astype(F32) + unpack_levels(total, matrix)).astype(BF16)
            return carry

        lax.fori_loop(0, waves, mix, 0, unroll=4)

    def transform(m, carry):
        turned[pl.ds(slot(m), rows, stride=waves), :] = jnp.dot(
            table_ref[m, 0], mixed[m], preferred_element_type=F32
        )
        return carry

    lax.fori_loop(0, waves, transform, 0, unroll=4)
    out_ref[...] = turned[...].astype(BF16).reshape(out_ref.shape)


def legendre_forward(probes, totals, legendre, coef, lev, parity):
    waves, _, degrees, _ = probes.shape
    lats = legendre.shape[2]
    blocks = lats // waves
    steps = 4
    total_spec = whole_spec(totals[0].shape)
    return pl.pallas_call(
        legendre_kernel,
        grid=(steps,),
        in_specs=[
            smem_spec(),
            smem_spec(),
            pl.BlockSpec((waves, 1, degrees, LANES), lambda g: (0, parity, 0, 0)),
        ]
        + [total_spec] * 4
        + [pl.BlockSpec((waves, 1, lats // steps, degrees), lambda g: (0, parity, g, 0))],
        out_specs=pl.BlockSpec((blocks // steps, waves, waves, LANES), lambda g: (g, 0, 0, 0)),
        out_shape=hbm_result((blocks, waves, waves, LANES), BF16),
        scratch_shapes=[
            pltpu.VMEM((waves, degrees, LANES), BF16),
            pltpu.VMEM((lats // steps * waves, LANES), F32),
        ],
        compiler_params=params(14),
        name="legendre_forward",
    )(coef, lev, in_hbm(probes), *totals, in_hbm(legendre))


HALF = M // 2


def mask_rows(count, parity):
    zonal = 2 * row_ids(HALF) + parity
    factor = jnp.where(zonal == 0, 1.0, 2.0)
    return jnp.where(zonal < count, factor, 0.0).astype(F32)


def load_waves(counts_ref, x_ref, operand, masked):
    step = pl.program_id(0)
    real_lane = (lane_ids(HALF) & PROBES) == 0
    for pair in range(2):
        both = [x_ref[:, 2 * pair + k].astype(F32) for k in range(2)]
        lanes = slice(pair * LANES, (pair + 1) * LANES)
        for parity in range(2):
            first, second = [
                x[:, 8 * parity : 8 * parity + 8].reshape(HALF, LANES) for x in both
            ]
            if masked:
                first = first * mask_rows(counts_ref[4 * step + 2 * pair], parity)
                second = second * mask_rows(counts_ref[4 * step + 2 * pair + 1], parity)
            operand[parity, :HALF, lanes] = jnp.where(
                real_lane, first, pltpu.roll(second, PROBES, 1)
            ).astype(BF16)
            operand[parity, HALF:, lanes] = jnp.where(
                real_lane, pltpu.roll(first, LANES - PROBES, 1), second
            ).astype(BF16)


def store_waves(counts_ref, fields, table_ref, out_ref, masked):
    step = pl.program_id(0)
    real_lane = (lane_ids(HALF) & PROBES) == 0
    results = {}
    for parity in range(2):
        cos_part = jnp.dot(table_ref[parity, :HALF], fields[parity], preferred_element_type=F32)
        sin_part = jnp.dot(table_ref[parity, HALF:], fields[parity], preferred_element_type=F32)
        for pair in range(2):
            cosine = cos_part[:, pair * LANES : (pair + 1) * LANES]
            sine = sin_part[:, pair * LANES : (pair + 1) * LANES]
            first = jnp.where(real_lane, cosine, pltpu.roll(sine, PROBES, 1))
            second = jnp.where(real_lane, pltpu.roll(cosine, LANES - PROBES, 1), sine)
            if masked:
                first = first * mask_rows(counts_ref[4 * step + 2 * pair], parity)
                second = second * mask_rows(counts_ref[4 * step + 2 * pair + 1], parity)
            results[2 * pair, parity] = first.reshape(-1, 8, LANES)
            results[2 * pair + 1, parity] = second.reshape(-1, 8, LANES)
    for k in range(4):
        out_ref[:, k] = jnp.concatenate([results[k, 0], results[k, 1]], axis=1).astype(BF16)


def grid_even_kernel(counts_ref, x_ref, table_ref, out_ref, operand, *, masked):
    load_waves(counts_ref, x_ref, operand, masked)
    even = jnp.dot(table_ref[0], operand[0], preferred_element_type=F32)
    odd = jnp.dot(table_ref[1], operand[1], preferred_element_type=F32)
    out_ref[0, 0] = even + odd
    out_ref[0, 1] = even - odd


def grid_middle_kernel(
    counts_ref, coef_ref, lev_ref, x_ref, even_ref, total_ref, gain_ref, forward_ref, inverse_ref,
    out_ref, odd_ref, operand, fields, *, coupled, masked_in, masked_out,
):
    if coupled:
        place = place_matrix(coef_ref, lev_ref, pl.program_id(0))
    load_waves(counts_ref, x_ref, operand, masked_in)
    size = 256
    for r in range(0, M, size):
        rows = slice(r, r + size)
        even = jnp.dot(forward_ref[0, rows], operand[0], preferred_element_type=F32)
        odd = jnp.dot(forward_ref[1, rows], operand[1], preferred_element_type=F32)
        for pair in range(2):
            lanes = slice(pair * LANES, (pair + 1) * LANES)
            kept = []
            for half, sent in enumerate((even[:, lanes] + odd[:, lanes], even[:, lanes] - odd[:, lanes])):
                base = even_ref[0, half, rows, lanes]
                if coupled:
                    base = base + jnp.dot(
                        twice(total_ref[half, rows, lanes]), place, preferred_element_type=F32
                    )
                longitudes = slice(half * M + r, half * M + r + size)
                north = gain_ref[0, pair, longitudes].astype(F32) * (base + sent)
                south = gain_ref[1, pair, longitudes].astype(F32) * (base - sent)
                kept.append((north + south, north - south))
            fields[0, rows, lanes] = (kept[0][0] + kept[1][0]).astype(BF16)
            fields[1, rows, lanes] = (kept[0][0] - kept[1][0]).astype(BF16)
            odd_ref[0, 0, rows, lanes] = (kept[0][1] + kept[1][1]).astype(BF16)
            odd_ref[0, 1, rows, lanes] = (kept[0][1] - kept[1][1]).astype(BF16)
    store_waves(counts_ref, fields, inverse_ref, out_ref, masked_out)


def grid_odd_kernel(counts_ref, odd_ref, table_ref, out_ref, *, masked):
    store_waves(counts_ref, odd_ref[0], table_ref, out_ref, masked)


def gain_kernel(gain_ref, spread_ref, out_ref):
    for h in range(2):
        out_ref[h, 0] = lax.dot_general(
            gain_ref[h, 0], spread_ref[...], (((0,), (0,)), ((), ())), preferred_element_type=F32
        ).astype(BF16)


def spread_gain(gain):
    pairs = gain.shape[1]
    return pl.pallas_call(
        gain_kernel,
        grid=(pairs,),
        in_specs=[
            pl.BlockSpec((2, 1, 8, 2 * M), lambda g: (0, g, 0, 0)),
            whole_spec((8, LANES)),
        ],
        out_specs=pl.BlockSpec((2, 1, 2 * M, LANES), lambda g: (0, g, 0, 0)),
        out_shape=hbm_result((2, pairs, 2 * M, LANES), BF16),
        compiler_params=params(8),
        name="spread_gain",
    )(gain, jnp.asarray(spread_table()))


def wave_block(x):
    return pl.BlockSpec((x.shape[0], 4, x.shape[2], LANES), lambda g: (0, g, 0, 0))


def grid_pass(arrive, depart, counts, gain, tables, coupling, masked_in, masked_out):
    forward, inverse = tables
    x_even = arrive(0)
    steps = x_even.shape[1] // 4
    field_spec = pl.BlockSpec((1, 2, M, 2 * LANES), lambda g: (g, 0, 0, 0))
    field_shape = (steps, 2, M, 2 * LANES)
    operand = pltpu.VMEM((2, M, 2 * LANES), BF16)
    even = pl.pallas_call(
        functools.partial(grid_even_kernel, masked=masked_in),
        grid=(steps,),
        in_specs=[smem_spec(), wave_block(x_even), whole_spec(forward.shape)],
        out_specs=field_spec,
        out_shape=hbm_result(field_shape, F32),
        scratch_shapes=[operand],
        compiler_params=params(16),
        name="grid_even",
    )(counts, in_hbm(x_even), in_hbm(forward))
    x_odd = arrive(1)
    out_shape = hbm_result(x_odd.shape, BF16)
    coupled, coef, lev, total = coupling(x_even)
    y_even, odd = pl.pallas_call(
        functools.partial(
            grid_middle_kernel, coupled=coupled, masked_in=masked_in, masked_out=masked_out
        ),
        grid=(steps,),
        in_specs=[
            smem_spec(),
            smem_spec(),
            smem_spec(),
            wave_block(x_odd),
            field_spec,
            whole_spec(total.shape),
            pl.BlockSpec((2, 2, 2 * M, LANES), lambda g: (0, g, 0, 0)),
            whole_spec(forward.shape),
            whole_spec(inverse.shape),
        ],
        out_specs=(wave_block(x_odd), field_spec),
        out_shape=(out_shape, hbm_result(field_shape, BF16)),
        scratch_shapes=[operand, operand],
        compiler_params=params(24),
        name="grid_middle",
    )(counts, coef, lev, x_odd, in_hbm(even), in_hbm(total), in_hbm(gain), in_hbm(forward), in_hbm(inverse))
    depart(0, y_even)
    y_odd = odd_stage(counts, odd, inverse, x_odd, masked_out)
    depart(1, y_odd)


def odd_stage(counts, odd, inverse, like, masked_out):
    steps = odd.shape[0]
    field_spec = pl.BlockSpec((1, 2, M, 2 * LANES), lambda g: (g, 0, 0, 0))
    return pl.pallas_call(
        functools.partial(grid_odd_kernel, masked=masked_out),
        grid=(steps,),
        in_specs=[smem_spec(), field_spec, whole_spec(inverse.shape)],
        out_specs=wave_block(like),
        out_shape=hbm_result(like.shape, BF16),
        compiler_params=params(16),
        name="grid_odd",
    )(counts, in_hbm(odd), in_hbm(inverse))


def spread_rows(x_ref, scratch):
    chunk = 4
    per = x_ref.shape[1] * x_ref.shape[2]

    def widen(b, carry):
        scratch[pl.ds(b * chunk * per, chunk * per), :] = (
            x_ref[pl.ds(b * chunk, chunk)].astype(F32).reshape(chunk * per, LANES)
        )
        return carry

    lax.fori_loop(0, x_ref.shape[0] // chunk, widen, 0, unroll=2)


def transform_of(table, fields):
    return lax.dot_general(table, fields, (((0,), (0,)), ((), ())), preferred_element_type=F32)


def middle_kernel(first_ref, visc_ref, lev_ref, x_ref, table_ref, out_ref, taken, turned, *, parity):
    waves = x_ref.shape[2]
    lats = x_ref.shape[0] * x_ref.shape[1]
    degrees = table_ref.shape[3]
    spread_rows(x_ref, taken)
    visc = own_levels(visc_ref, lev_ref, lane_ids(degrees) // 32)

    def one_wave(m, carry):
        fields = taken[pl.ds(slot(m), lats, stride=waves), :].astype(BF16)
        table = table_ref[m, 0]
        tangent = transform_of(table, fields)
        degree = first_ref[0] + m + parity + 2 * row_ids(degrees)
        scaled = (degree * (degree + 1)).astype(F32) / float((M + K) * (M + K + 1))
        damp = 1.0 / (1.0 + scaled * visc)
        damped = (tangent * (damp * damp)).astype(BF16)
        turned[pl.ds(slot(m), lats, stride=waves), :] = jnp.dot(
            table, damped, preferred_element_type=F32
        )
        return carry

    lax.fori_loop(0, waves, one_wave, 0, unroll=2)
    per = x_ref.shape[1] * waves

    def narrow(b, carry):
        out_ref[pl.ds(b * 4, 4)] = (
            turned[pl.ds(b * 4 * per, 4 * per), :]
            .astype(BF16)
            .reshape(4, x_ref.shape[1], waves, LANES)
        )
        return carry

    lax.fori_loop(0, x_ref.shape[0] // 4, narrow, 0, unroll=2)


def middle_stage(x, legendre, viscosity, lev, wave_first, parity):
    waves, _, lats, degrees = legendre.shape
    return pl.pallas_call(
        functools.partial(middle_kernel, parity=parity),
        grid=(1,),
        in_specs=[
            smem_spec(),
            smem_spec(),
            smem_spec(),
            whole_spec(x.shape),
            pl.BlockSpec((waves, 1, lats, degrees), lambda g: (0, parity, 0, 0)),
        ],
        out_specs=whole_spec(x.shape),
        out_shape=hbm_result(x.shape, BF16),
        scratch_shapes=[pltpu.VMEM((lats * waves, LANES), F32)] * 2,
        compiler_params=params(26),
        name="middle_stage",
    )(wave_first, viscosity, lev, x, in_hbm(legendre))


def images_kernel(up_ref, down_ref, lev_ref, x_ref, table_ref, out_ref, part_ref, low_ref, taken):
    waves = x_ref.shape[2]
    lats = x_ref.shape[0] * x_ref.shape[1]
    count = table_ref.shape[0]
    step = pl.program_id(0)

    @pl.when(step == 0)
    def _():
        spread_rows(x_ref, taken)

    up_matrix = sum_matrix(up_ref, lev_ref)
    down_matrix = sum_matrix(down_ref, lev_ref)
    for k in range(count):
        fields = taken[pl.ds(slot(step * count + k), lats, stride=waves), :].astype(BF16)
        image = transform_of(table_ref[k, 0], fields)
        high, low = halves(image)
        out_ref[k] = jnp.concatenate([high, low], axis=1)
        up_sum = jnp.dot(twice(high), up_matrix, preferred_element_type=F32)
        part_ref[k] = pack_levels(up_sum).astype(BF16)
        down_sum = jnp.dot(twice(high), down_matrix, preferred_element_type=F32) + jnp.dot(
            low, down_matrix[:LANES], preferred_element_type=F32
        )
        low_ref[k] = jnp.concatenate(halves(pack_levels(down_sum)), axis=1)


def image_stage(x, legendre, up, down, lev, parity):
    x = in_hbm(x) if parity == 0 else x
    waves, _, lats, degrees = legendre.shape
    steps = 4
    count = waves // steps
    return pl.pallas_call(
        images_kernel,
        grid=(steps,),
        in_specs=[
            smem_spec(),
            smem_spec(),
            smem_spec(),
            whole_spec(x.shape),
            pl.BlockSpec((count, 1, lats, degrees), lambda g: (g, parity, 0, 0)),
        ],
        out_specs=(
            pl.BlockSpec((count, degrees, 2 * LANES), lambda g: (g, 0, 0)),
            pl.BlockSpec((count, degrees // 4, LANES), lambda g: (g, 0, 0)),
            pl.BlockSpec((count, degrees // 4, 2 * LANES), lambda g: (g, 0, 0)),
        ),
        out_shape=(
            hbm_result((waves, degrees, 2 * LANES), BF16),
            jax.ShapeDtypeStruct((waves, degrees // 4, LANES), BF16),
            hbm_result((waves, degrees // 4, 2 * LANES), BF16),
        ),
        scratch_shapes=[pltpu.VMEM((lats * waves, LANES), F32)],
        compiler_params=params(20),
        name="image_stage",
    )(up, down, lev, x, in_hbm(legendre))


def gram_of(high, both):
    return lax.dot_general(high, both, (((0,), (0,)), ((), ())), preferred_element_type=F32)


def gram_kernel(image_ref, out_ref):
    @pl.when(pl.program_id(0) == 0)
    def _():
        out_ref[...] = jnp.zeros_like(out_ref)

    rows = image_ref.shape[0] * image_ref.shape[1]
    both = image_ref[...].reshape(rows, 2 * LANES)
    out_ref[...] += gram_of(both[:, :LANES], both)


def gram_stage(images):
    waves, degrees, _ = images.shape
    steps = 4
    return pl.pallas_call(
        gram_kernel,
        grid=(steps,),
        in_specs=[pl.BlockSpec((waves // steps, degrees, 2 * LANES), lambda g: (g, 0, 0))],
        out_specs=whole_spec((LANES, 2 * LANES)),
        out_shape=jax.ShapeDtypeStruct((LANES, 2 * LANES), F32),
        compiler_params=params(12),
        name="gram_stage",
    )(in_hbm(images))


def finish_kernel(down_ref, lev_ref, *refs):
    first = lev_ref[0] * 4
    square = down_ref[first] * down_ref[first]
    for k in range(1, 4):
        square = square + down_ref[first + k] * down_ref[first + k]
    grams = refs[:2]
    lows = refs[2:4]
    totals = refs[4:12]
    total_ref, gram_ref = refs[12:]
    sums = grams[0][...] + grams[1][...]
    cross = sums[:, LANES:]
    gram = sums[:, :LANES] + (cross + cross.T)
    for p in range(2):
        parts = [ref[...].astype(F32) for ref in totals[4 * p : 4 * p + 4]]
        total = ((parts[0] + parts[1]) + (parts[2] + parts[3])).astype(BF16)
        total_ref[p] = total
        flat = total.reshape(-1, LANES)
        low = lows[p][...].reshape(-1, 2 * LANES)
        operand = jnp.concatenate([flat, low], axis=1)
        result = gram_of(flat, operand)
        mixed = result[:, LANES : 2 * LANES] + result[:, 2 * LANES :]
        gram = gram + square * result[:, :LANES] + (mixed + mixed.T)
    same = (row_ids(LANES) // PROBES) == (lane_ids(LANES) // PROBES)
    gram = jnp.where(same, gram, 0.0)
    summed = gram[0:PROBES]
    for b in range(1, LANES // PROBES):
        summed = summed + gram[b * PROBES : (b + 1) * PROBES]
    for shift in (64, 32, 16):
        summed = summed + pltpu.roll(summed, shift, 1)
    gram_ref[...] = jnp.broadcast_to(summed[None], gram_ref.shape)


def finish_stage(grams, lows, totals, down, lev, copies):
    shape = totals[0].shape
    return pl.pallas_call(
        finish_kernel,
        in_specs=[smem_spec(), smem_spec()] + [pl.BlockSpec(memory_space=pltpu.VMEM)] * 12,
        out_shape=(
            hbm_result((2,) + shape, BF16),
            hbm_result((copies, PROBES, LANES), F32),
        ),
        compiler_params=params(16),
        name="finish_stage",
    )(down, lev, *grams, *lows, *totals)


def factor_of(gram):
    rows = row_ids(PROBES)
    lanes = lane_ids(PROBES) & (PROBES - 1)
    upper = jnp.zeros_like(gram)
    inverse = jnp.where(rows == lanes, 1.0, 0.0).astype(F32)
    for k in range(PROBES):
        scale = lax.rsqrt(gram[k : k + 1, k : k + 1])
        scale = scale * (1.5 - 0.5 * gram[k : k + 1, k : k + 1] * scale * scale)
        line = jnp.where(lanes[0:1] >= k, gram[k : k + 1] * scale, 0.0)
        solved = inverse[k : k + 1] * scale
        column = jnp.where(rows[:, 0:1] > k, gram[:, k : k + 1] * scale, 0.0)
        upper = jnp.where(rows == k, line, upper)
        gram = gram - column * line
        inverse = jnp.where(rows == k, solved, inverse - column * solved)
    return upper, inverse


def basis_kernel(
    down_ref, lev_ref, own_ref, one_ref, two_ref, three_ref, even_ref, odd_ref, total_ref,
    out_ref, factor_ref, mix, *, row_scale,
):
    @pl.when(pl.program_id(0) == 0)
    def _():
        gram = (own_ref[...] + two_ref[...]) + (one_ref[...] + three_ref[...])
        upper, inverse = factor_of(gram)
        factor_ref[...] = upper[:, :PROBES] / row_scale
        pick = ((lane_ids(PROBES) & (PROBES - 1)) == row_ids(PROBES)).astype(BF16)
        same = (row_ids(LANES) // PROBES) == (lane_ids(LANES) // PROBES)
        high, low = halves(inverse * row_scale)
        mix_high = jnp.where(same, gram_of(high, pick), 0.0).astype(BF16)
        mix_low = jnp.where(same, gram_of(low, pick), 0.0).astype(BF16)
        mix[0:LANES] = mix_high
        mix[LANES : 2 * LANES] = mix_high
        mix[2 * LANES :] = mix_low

    matrix = unpack_matrix(down_ref, lev_ref)
    for m in range(even_ref.shape[0]):
        for p, image_ref in enumerate((even_ref, odd_ref)):
            both = image_ref[m]
            full = (both[:, :LANES].astype(F32) + both[:, LANES:].astype(F32)) + unpack_levels(
                total_ref[p, m], matrix
            )
            high, low = halves(full)
            value = jnp.dot(
                jnp.concatenate([high, low, high], axis=1), mix[...], preferred_element_type=F32
            )
            out_ref[m, p] = value.astype(BF16)


def basis_stage(grams, images, total, down, lev, row_scale):
    waves, degrees, _ = images[0].shape
    steps = 4
    count = waves // steps
    image_spec = pl.BlockSpec((count, degrees, 2 * LANES), lambda g: (g, 0, 0))
    return pl.pallas_call(
        functools.partial(basis_kernel, row_scale=row_scale),
        grid=(steps,),
        in_specs=[smem_spec(), smem_spec()]
        + [whole_spec((PROBES, LANES))] * 4
        + [
            image_spec,
            image_spec,
            pl.BlockSpec((2, count, degrees // 4, LANES), lambda g: (0, g, 0, 0)),
        ],
        out_specs=(
            pl.BlockSpec((count, 2, degrees, LANES), lambda g: (g, 0, 0, 0)),
            whole_spec((PROBES, PROBES)),
        ),
        out_shape=(
            hbm_result((waves, 2, degrees, LANES), BF16),
            hbm_result((PROBES, PROBES), F32),
        ),
        scratch_shapes=[pltpu.VMEM((3 * LANES, LANES), BF16)],
        compiler_params=params(14),
        name="basis_stage",
    )(down, lev, *grams, in_hbm(images[0]), in_hbm(images[1]), in_hbm(total))


def exchange(blocks):
    return lax.all_to_all(blocks, "lat", split_axis=0, concat_axis=0, tiled=True)


def from_levels(part):
    count = lax.axis_size("lev")
    return [
        lax.ppermute(part, "lev", [(i, (i + k) % count) for i in range(count)])
        for k in range(1, count)
    ]


def shards(
    probes, legendre, quad_weight, trunc_counts, background, level_up, level_down, viscosity
):
    lat_count = lax.axis_size("lat")
    lev_count = lax.axis_size("lev")
    lat_index = lax.axis_index("lat")
    lev_index = lax.axis_index("lev")
    wave_local = probes.shape[0]
    level_local = probes.shape[3] // (2 * PROBES)
    lon_count = 2 * M

    lev = lev_index.astype(jnp.int32).reshape(1)
    wave_first = (lat_index * wave_local).astype(jnp.int32).reshape(1)
    forward = wave_tables(M)
    tables = (jnp.asarray(forward), jnp.asarray(np.ascontiguousarray(forward.transpose(0, 2, 1))))

    sent = {0: exchange(legendre_raw(probes, legendre, 0))}
    partial = level_partial(probes, level_down, lev, 1)
    totals = [partial] + from_levels(partial)
    sent[1] = exchange(legendre_forward(probes, totals, legendre, level_up, lev, 1))

    own_gain = lax.dynamic_slice_in_dim(background, lev_index * level_local, level_local, 2)
    own_gain = own_gain * (quad_weight / float(lon_count))[None, :, None, None]
    own_gain = own_gain.reshape(2, -1, 2, level_local, lon_count).swapaxes(2, 3)
    own_gain = own_gain.reshape(2, -1, 2 * level_local, lon_count).astype(BF16)
    gain = spread_gain(own_gain)

    folded = {}

    def depart(p, values):
        folded[p] = exchange(values)

    def couple_first(x):
        partial = grid_sum(x, level_down, lev)
        total = grid_total(trunc_counts, [partial] + from_levels(partial), tables[0])
        return True, level_up, lev, total

    def couple_none(x):
        return False, level_up, lev, jnp.zeros((8, LANES), BF16)

    grid_pass(lambda p: sent[p], depart, trunc_counts, gain, tables, couple_first, True, False)
    second = {
        p: exchange(middle_stage(folded[p], legendre, viscosity, lev, wave_first, p))
        for p in range(2)
    }
    folded2 = {}

    def depart2(p, values):
        folded2[p] = exchange(values)

    grid_pass(lambda p: second[p], depart2, trunc_counts, gain, tables, couple_none, False, True)
    images, lows, grams, totals = [], [], [], []
    for p in range(2):
        image, part, low = image_stage(folded2[p], legendre, level_up, level_down, lev, p)
        images.append(image)
        lows.append(low)
        grams.append(gram_stage(image))
        totals += [part] + from_levels(part)
    total, gram_copies = finish_stage(grams, lows, totals, level_down, lev, lat_count)
    over_lat = jnp.sum(exchange(gram_copies), axis=0)
    row_scale = math.sqrt(M * K * 2 * level_local * lev_count)
    return basis_stage(
        [over_lat] + from_levels(over_lat), images, total, level_down, lev, row_scale
    )


def solution(mesh):
    placed = (
        P("lat", None, None, "lev"),
        P("lat", None, None, None),
        P("lat"),
        P("lat"),
        P(None, "lat", None, None),
        P(),
        P(),
        P(),
    )
    return jax.shard_map(
        shards,
        mesh=mesh,
        in_specs=placed,
        out_specs=(P("lat", None, None, "lev"), P()),
        check_vma=False,
    )
```

```python
import functools
import math

import jax
import jax.numpy as jnp
import ml_dtypes
import numpy as np
from jax import lax
from jax.experimental import pallas as pl
from jax.experimental.pallas import tpu as pltpu
from jax.sharding import PartitionSpec as P


M = 512
K = 512
PROBES = 16
LANES = 128
F32 = jnp.float32
BF16 = jnp.bfloat16


def params(mib):
    return pltpu.CompilerParams(vmem_limit_bytes=mib << 20)


def in_hbm(values):
    return pltpu.with_memory_space_constraint(values, pltpu.HBM)


def hbm_result(shape, dtype):
    return pltpu.HBM(shape, dtype)


def wave_tables(wave_count):
    lon = np.arange(wave_count)[:, None]
    tables = []
    for parity in range(2):
        zonal = np.arange(parity, wave_count, 2)[None, :]
        phase = (zonal * lon % (2 * wave_count)) * (math.pi / wave_count)
        tables.append(np.concatenate([np.cos(phase), -np.sin(phase)], axis=1))
    return np.stack(tables).astype(np.float32).astype(ml_dtypes.bfloat16)


def spread_table():
    rows = np.arange(8)[:, None]
    lanes = np.arange(LANES)[None, :] // PROBES
    return (rows == lanes).astype(ml_dtypes.bfloat16)


def lane_ids(rows, lanes=LANES):
    return lax.broadcasted_iota(jnp.int32, (rows, lanes), 1)


def row_ids(rows, lanes=LANES):
    return lax.broadcasted_iota(jnp.int32, (rows, lanes), 0)


def halves(values):
    high = values.astype(BF16)
    return high, (values - high.astype(F32)).astype(BF16)


def slot(wave):
    return (wave & 1) * 8 + (wave >> 1)


def own_levels(coef_ref, lev_ref, level):
    first = lev_ref[0] * 4
    coef = jnp.where(level == 0, coef_ref[first], coef_ref[first + 1])
    return jnp.where(
        level < 2, coef, jnp.where(level == 2, coef_ref[first + 2], coef_ref[first + 3])
    )


def sum_matrix(coef_ref, lev_ref):
    rows = row_ids(LANES)
    weights = jnp.where(
        (rows & 31) == (lane_ids(LANES) & 31), own_levels(coef_ref, lev_ref, rows // 32), 0.0
    )
    return jnp.concatenate(halves(weights), axis=0)


def unpack_matrix(coef_ref, lev_ref):
    rows = row_ids(LANES, 4 * LANES)
    lanes = lane_ids(LANES, 4 * LANES)
    level = (lanes & (LANES - 1)) // 32
    hit = (rows // 32 == lanes // LANES) & ((rows & 31) == (lanes & 31))
    weights = jnp.where(hit, own_levels(coef_ref, lev_ref, level), 0.0)
    return jnp.concatenate(halves(weights), axis=0)


def twice(values):
    return jnp.concatenate([values, values], axis=1)


def pack_levels(summed):
    rows = summed.shape[0] // 4
    group = lane_ids(rows) // 32
    low = jnp.where(group == 0, summed[0:rows], summed[rows : 2 * rows])
    high = jnp.where(group == 2, summed[2 * rows : 3 * rows], summed[3 * rows :])
    return jnp.where(group < 2, low, high)


def smem_spec():
    return pl.BlockSpec(memory_space=pltpu.SMEM)


def whole_spec(shape):
    return pl.BlockSpec(shape, lambda g: (0,) * len(shape))


def partial_kernel(coef_ref, lev_ref, probes_ref, out_ref):
    waves, _, degrees, _ = probes_ref.shape
    flat = probes_ref[:, 0].reshape(waves * degrees, LANES)
    summed = jnp.dot(twice(flat), sum_matrix(coef_ref, lev_ref), preferred_element_type=F32)
    for m in range(waves):
        out_ref[m] = pack_levels(summed[m * degrees : (m + 1) * degrees]).astype(BF16)


def level_partial(probes, coef, lev, parity):
    waves, _, degrees, _ = probes.shape
    steps = 2
    return pl.pallas_call(
        partial_kernel,
        grid=(steps,),
        in_specs=[
            smem_spec(),
            smem_spec(),
            pl.BlockSpec((waves // steps, 1, degrees, LANES), lambda g: (g, parity, 0, 0)),
        ],
        out_specs=pl.BlockSpec((waves // steps, degrees // 4, LANES), lambda g: (g, 0, 0)),
        out_shape=jax.ShapeDtypeStruct((waves, degrees // 4, LANES), BF16),
        compiler_params=params(8),
        name="level_partial",
    )(coef, lev, in_hbm(probes))


def legendre_raw_kernel(probes_ref, table_ref, out_ref, turned):
    waves = probes_ref.shape[0]
    rows = table_ref.shape[2]
    for m in range(waves):
        turned[pl.ds(slot(m), rows, stride=waves), :] = jnp.dot(
            table_ref[m, 0], probes_ref[m, 0], preferred_element_type=F32
        )
    out_ref[...] = turned[...].astype(BF16).reshape(out_ref.shape)


def legendre_raw(probes, legendre, parity):
    waves, _, degrees, _ = probes.shape
    lats = legendre.shape[2]
    blocks = lats // waves
    steps = 2
    return pl.pallas_call(
        legendre_raw_kernel,
        grid=(steps,),
        in_specs=[
            pl.BlockSpec((waves, 1, degrees, LANES), lambda g: (0, parity, 0, 0)),
            pl.BlockSpec((waves, 1, lats // steps, degrees), lambda g: (0, parity, g, 0)),
        ],
        out_specs=pl.BlockSpec((blocks // steps, waves, waves, LANES), lambda g: (g, 0, 0, 0)),
        out_shape=hbm_result((blocks, waves, waves, LANES), BF16),
        scratch_shapes=[pltpu.VMEM((lats // steps * waves, LANES), F32)],
        compiler_params=params(20),
        name="legendre_raw",
    )(in_hbm(probes), in_hbm(legendre))


def grid_sum_kernel(coef_ref, lev_ref, x_ref, out_ref):
    blocks, lats, waves, _ = x_ref.shape
    flat = x_ref[...].reshape(blocks * lats * waves, LANES)
    summed = jnp.dot(twice(flat), sum_matrix(coef_ref, lev_ref), preferred_element_type=F32)
    summed = summed.reshape(blocks, lats, waves, LANES)
    group = lax.broadcasted_iota(jnp.int32, (blocks, 4, waves, LANES), 3) // 32
    low = jnp.where(group == 0, summed[:, 0:4], summed[:, 4:8])
    high = jnp.where(group == 2, summed[:, 8:12], summed[:, 12:16])
    out_ref[...] = jnp.where(group < 2, low, high).astype(BF16)


def grid_sum(x, coef, lev):
    blocks, lats, waves, _ = x.shape
    steps = 4
    return pl.pallas_call(
        grid_sum_kernel,
        grid=(steps,),
        in_specs=[
            smem_spec(),
            smem_spec(),
            pl.BlockSpec((blocks // steps, lats, waves, LANES), lambda g: (g, 0, 0, 0)),
        ],
        out_specs=pl.BlockSpec((blocks // steps, 4, waves, LANES), lambda g: (g, 0, 0, 0)),
        out_shape=jax.ShapeDtypeStruct((blocks, 4, waves, LANES), BF16),
        compiler_params=params(12),
        name="grid_sum",
    )(coef, lev, in_hbm(x))


def grid_total_kernel(counts_ref, *refs):
    totals = refs[:4]
    table_ref, out_ref, operand = refs[4:]
    real_lane = (lane_ids(HALF) & PROBES) == 0
    group = lane_ids(HALF) // 32
    zonal = 2 * row_ids(HALF)
    for pair in range(2):
        both = []
        for k in range(2):
            parts = [ref[:, 2 * pair + k].astype(F32) for ref in totals]
            both.append((parts[0] + parts[1]) + (parts[2] + parts[3]))
        lanes = slice(pair * LANES, (pair + 1) * LANES)
        for parity in range(2):
            masked = []
            for k in range(2):
                x = both[k][:, 8 * parity : 8 * parity + 8].reshape(HALF, LANES)
                lat = 2 * pair + k
                count = jnp.where(
                    group < 2,
                    jnp.where(group == 0, counts_ref[lat], counts_ref[4 + lat]),
                    jnp.where(group == 2, counts_ref[8 + lat], counts_ref[12 + lat]),
                )
                factor = jnp.where(zonal + parity == 0, 1.0, 2.0)
                masked.append(x * jnp.where(zonal + parity < count, factor, 0.0))
            first, second = masked
            operand[parity, :HALF, lanes] = jnp.where(
                real_lane, first, pltpu.roll(second, PROBES, 1)
            ).astype(BF16)
            operand[parity, HALF:, lanes] = jnp.where(
                real_lane, pltpu.roll(first, LANES - PROBES, 1), second
            ).astype(BF16)
    even = jnp.dot(table_ref[0], operand[0], preferred_element_type=F32)
    odd = jnp.dot(table_ref[1], operand[1], preferred_element_type=F32)
    out_ref[0] = (even + odd).astype(BF16)
    out_ref[1] = (even - odd).astype(BF16)


def grid_total(counts, totals, forward):
    shape = (2, M, 2 * LANES)
    vmem = pl.BlockSpec(memory_space=pltpu.VMEM)
    return pl.pallas_call(
        grid_total_kernel,
        in_specs=[smem_spec()] + [vmem] * 5,
        out_shape=hbm_result(shape, BF16),
        scratch_shapes=[pltpu.VMEM(shape, BF16)],
        compiler_params=params(12),
        name="grid_total",
    )(counts, *totals, forward)


def place_matrix(coef_ref, lev_ref, taken_group):
    rows = row_ids(LANES)
    lanes = lane_ids(LANES)
    hit = (rows // 32 == taken_group) & ((rows & 31) == (lanes & 31))
    weights = jnp.where(hit, own_levels(coef_ref, lev_ref, lanes // 32), 0.0)
    return jnp.concatenate(halves(weights), axis=0)


def legendre_kernel(coef_ref, lev_ref, probes_ref, *refs):
    totals = refs[:4]
    table_ref, out_ref, mixed, turned = refs[4:]
    waves = probes_ref.shape[0]
    rows = table_ref.shape[2]

    @pl.when(pl.program_id(0) == 0)
    def _():
        parts = [ref[...].astype(F32) for ref in totals]
        total = ((parts[0] + parts[1]) + (parts[2] + parts[3])).astype(BF16)
        quarter = total.shape[1]
        wide = jnp.dot(
            twice(total.reshape(waves * quarter, LANES)),
            unpack_matrix(coef_ref, lev_ref),
            preferred_element_type=F32,
        )
        for m in range(waves):
            for g in range(4):
                piece = slice(g * quarter, (g + 1) * quarter)
                mixed[m, piece] = (
                    probes_ref[m, 0, piece].astype(F32)
                    + wide[m * quarter : (m + 1) * quarter, g * LANES : (g + 1) * LANES]
                ).astype(BF16)

    for m in range(waves):
        turned[pl.ds(slot(m), rows, stride=waves), :] = jnp.dot(
            table_ref[m, 0], mixed[m], preferred_element_type=F32
        )
    out_ref[...] = turned[...].astype(BF16).reshape(out_ref.shape)


def legendre_forward(probes, totals, legendre, coef, lev, parity):
    waves, _, degrees, _ = probes.shape
    lats = legendre.shape[2]
    blocks = lats // waves
    steps = 2
    total_spec = whole_spec(totals[0].shape)
    return pl.pallas_call(
        legendre_kernel,
        grid=(steps,),
        in_specs=[
            smem_spec(),
            smem_spec(),
            pl.BlockSpec((waves, 1, degrees, LANES), lambda g: (0, parity, 0, 0)),
        ]
        + [total_spec] * 4
        + [pl.BlockSpec((waves, 1, lats // steps, degrees), lambda g: (0, parity, g, 0))],
        out_specs=pl.BlockSpec((blocks // steps, waves, waves, LANES), lambda g: (g, 0, 0, 0)),
        out_shape=hbm_result((blocks, waves, waves, LANES), BF16),
        scratch_shapes=[
            pltpu.VMEM((waves, degrees, LANES), BF16),
            pltpu.VMEM((lats // steps * waves, LANES), F32),
        ],
        compiler_params=params(24),
        name="legendre_forward",
    )(coef, lev, in_hbm(probes), *totals, in_hbm(legendre))


HALF = M // 2


def mask_rows(count, parity):
    zonal = 2 * row_ids(HALF) + parity
    factor = jnp.where(zonal == 0, 1.0, 2.0)
    return jnp.where(zonal < count, factor, 0.0).astype(F32)


def load_waves(counts_ref, x_ref, operand, masked):
    step = pl.program_id(0)
    real_lane = (lane_ids(HALF) & PROBES) == 0
    for pair in range(2):
        both = [x_ref[:, 2 * pair + k].astype(F32) for k in range(2)]
        lanes = slice(pair * LANES, (pair + 1) * LANES)
        for parity in range(2):
            first, second = [
                x[:, 8 * parity : 8 * parity + 8].reshape(HALF, LANES) for x in both
            ]
            if masked:
                first = first * mask_rows(counts_ref[4 * step + 2 * pair], parity)
                second = second * mask_rows(counts_ref[4 * step + 2 * pair + 1], parity)
            operand[parity, :HALF, lanes] = jnp.where(
                real_lane, first, pltpu.roll(second, PROBES, 1)
            ).astype(BF16)
            operand[parity, HALF:, lanes] = jnp.where(
                real_lane, pltpu.roll(first, LANES - PROBES, 1), second
            ).astype(BF16)


def store_waves(counts_ref, fields, table_ref, out_ref, masked):
    step = pl.program_id(0)
    real_lane = (lane_ids(HALF) & PROBES) == 0
    results = {}
    for parity in range(2):
        cos_part = jnp.dot(table_ref[parity, :HALF], fields[parity], preferred_element_type=F32)
        sin_part = jnp.dot(table_ref[parity, HALF:], fields[parity], preferred_element_type=F32)
        for pair in range(2):
            cosine = cos_part[:, pair * LANES : (pair + 1) * LANES]
            sine = sin_part[:, pair * LANES : (pair + 1) * LANES]
            first = jnp.where(real_lane, cosine, pltpu.roll(sine, PROBES, 1))
            second = jnp.where(real_lane, pltpu.roll(cosine, LANES - PROBES, 1), sine)
            if masked:
                first = first * mask_rows(counts_ref[4 * step + 2 * pair], parity)
                second = second * mask_rows(counts_ref[4 * step + 2 * pair + 1], parity)
            results[2 * pair, parity] = first.reshape(-1, 8, LANES)
            results[2 * pair + 1, parity] = second.reshape(-1, 8, LANES)
    for k in range(4):
        out_ref[:, k] = jnp.concatenate([results[k, 0], results[k, 1]], axis=1).astype(BF16)


def grid_even_kernel(counts_ref, x_ref, table_ref, out_ref, operand, *, masked):
    load_waves(counts_ref, x_ref, operand, masked)
    even = jnp.dot(table_ref[0], operand[0], preferred_element_type=F32)
    odd = jnp.dot(table_ref[1], operand[1], preferred_element_type=F32)
    out_ref[0, 0] = (even + odd).astype(BF16)
    out_ref[0, 1] = (even - odd).astype(BF16)


def grid_middle_kernel(
    counts_ref, coef_ref, lev_ref, x_ref, even_ref, *refs, coupled, masked_in, masked_out
):
    if coupled:
        total_ref, refs = refs[0], refs[1:]
    gain_ref, forward_ref, inverse_ref, out_ref, odd_ref, operand, fields = refs
    if coupled:
        place = place_matrix(coef_ref, lev_ref, pl.program_id(0))
    load_waves(counts_ref, x_ref, operand, masked_in)
    size = 256
    for r in range(0, M, size):
        rows = slice(r, r + size)
        even = jnp.dot(forward_ref[0, rows], operand[0], preferred_element_type=F32)
        odd = jnp.dot(forward_ref[1, rows], operand[1], preferred_element_type=F32)
        for pair in range(2):
            lanes = slice(pair * LANES, (pair + 1) * LANES)
            kept = []
            for half, sent in enumerate((even[:, lanes] + odd[:, lanes], even[:, lanes] - odd[:, lanes])):
                base = even_ref[0, half, rows, lanes].astype(F32)
                if coupled:
                    base = base + jnp.dot(
                        twice(total_ref[half, rows, lanes]), place, preferred_element_type=F32
                    )
                longitudes = slice(half * M + r, half * M + r + size)
                north = gain_ref[0, pair, longitudes].astype(F32) * (base + sent)
                south = gain_ref[1, pair, longitudes].astype(F32) * (base - sent)
                kept.append((north + south, north - south))
            fields[0, rows, lanes] = (kept[0][0] + kept[1][0]).astype(BF16)
            fields[1, rows, lanes] = (kept[0][0] - kept[1][0]).astype(BF16)
            odd_ref[0, 0, rows, lanes] = (kept[0][1] + kept[1][1]).astype(BF16)
            odd_ref[0, 1, rows, lanes] = (kept[0][1] - kept[1][1]).astype(BF16)
    store_waves(counts_ref, fields, inverse_ref, out_ref, masked_out)


def grid_odd_kernel(counts_ref, odd_ref, table_ref, out_ref, *, masked):
    store_waves(counts_ref, odd_ref[0], table_ref, out_ref, masked)


def gain_kernel(gain_ref, spread_ref, out_ref):
    for h in range(2):
        out_ref[h, 0] = lax.dot_general(
            gain_ref[h, 0], spread_ref[...], (((0,), (0,)), ((), ())), preferred_element_type=F32
        ).astype(BF16)


def spread_gain(gain):
    pairs = gain.shape[1]
    return pl.pallas_call(
        gain_kernel,
        grid=(pairs,),
        in_specs=[
            pl.BlockSpec((2, 1, 8, 2 * M), lambda g: (0, g, 0, 0)),
            whole_spec((8, LANES)),
        ],
        out_specs=pl.BlockSpec((2, 1, 2 * M, LANES), lambda g: (0, g, 0, 0)),
        out_shape=hbm_result((2, pairs, 2 * M, LANES), BF16),
        compiler_params=params(8),
        name="spread_gain",
    )(gain, jnp.asarray(spread_table()))


def wave_block(x):
    return pl.BlockSpec((x.shape[0], 4, x.shape[2], LANES), lambda g: (0, g, 0, 0))


def grid_pass(arrive, depart, counts, gain, tables, coupling, masked_in, masked_out):
    forward, inverse = tables
    x_even = arrive(0)
    steps = x_even.shape[1] // 4
    field_spec = pl.BlockSpec((1, 2, M, 2 * LANES), lambda g: (g, 0, 0, 0))
    field_shape = (steps, 2, M, 2 * LANES)
    operand = pltpu.VMEM((2, M, 2 * LANES), BF16)
    even = pl.pallas_call(
        functools.partial(grid_even_kernel, masked=masked_in),
        grid=(steps,),
        in_specs=[smem_spec(), wave_block(x_even), whole_spec(forward.shape)],
        out_specs=field_spec,
        out_shape=hbm_result(field_shape, BF16),
        scratch_shapes=[operand],
        compiler_params=params(16),
        name="grid_even",
    )(counts, in_hbm(x_even), in_hbm(forward))
    x_odd = arrive(1)
    out_shape = hbm_result(x_odd.shape, BF16)
    coupled, coef, lev, total = coupling(x_even)
    y_even, odd = pl.pallas_call(
        functools.partial(
            grid_middle_kernel, coupled=coupled, masked_in=masked_in, masked_out=masked_out
        ),
        grid=(steps,),
        in_specs=[
            smem_spec(),
            smem_spec(),
            smem_spec(),
            wave_block(x_odd),
            field_spec,
        ]
        + [whole_spec(x.shape) for x in total]
        + [
            pl.BlockSpec((2, 2, 2 * M, LANES), lambda g: (0, g, 0, 0)),
            whole_spec(forward.shape),
            whole_spec(inverse.shape),
        ],
        out_specs=(wave_block(x_odd), field_spec),
        out_shape=(out_shape, hbm_result(field_shape, BF16)),
        scratch_shapes=[operand, operand],
        compiler_params=params(24),
        name="grid_middle",
    )(counts, coef, lev, x_odd, in_hbm(even), *[in_hbm(x) for x in total], in_hbm(gain), in_hbm(forward), in_hbm(inverse))
    depart(0, y_even)
    y_odd = odd_stage(counts, odd, inverse, x_odd, masked_out)
    depart(1, y_odd)


def odd_stage(counts, odd, inverse, like, masked_out):
    steps = odd.shape[0]
    field_spec = pl.BlockSpec((1, 2, M, 2 * LANES), lambda g: (g, 0, 0, 0))
    return pl.pallas_call(
        functools.partial(grid_odd_kernel, masked=masked_out),
        grid=(steps,),
        in_specs=[smem_spec(), field_spec, whole_spec(inverse.shape)],
        out_specs=wave_block(like),
        out_shape=hbm_result(like.shape, BF16),
        compiler_params=params(16),
        name="grid_odd",
    )(counts, in_hbm(odd), in_hbm(inverse))


def spread_rows(x_ref, scratch):
    chunk = 4
    per = x_ref.shape[1] * x_ref.shape[2]

    def widen(b, carry):
        scratch[pl.ds(b * chunk * per, chunk * per), :] = (
            x_ref[pl.ds(b * chunk, chunk)].astype(F32).reshape(chunk * per, LANES)
        )
        return carry

    lax.fori_loop(0, x_ref.shape[0] // chunk, widen, 0, unroll=2)


def transform_of(table, fields):
    return lax.dot_general(table, fields, (((0,), (0,)), ((), ())), preferred_element_type=F32)


def middle_kernel(first_ref, visc_ref, lev_ref, x_ref, table_ref, out_ref, taken, turned, *, parity):
    waves = x_ref.shape[2]
    lats = x_ref.shape[0] * x_ref.shape[1]
    degrees = table_ref.shape[3]
    spread_rows(x_ref, taken)
    visc = own_levels(visc_ref, lev_ref, lane_ids(degrees) // 32)

    def one_wave(m, carry):
        fields = taken[pl.ds(slot(m), lats, stride=waves), :].astype(BF16)
        table = table_ref[m, 0]
        tangent = transform_of(table, fields)
        degree = first_ref[0] + m + parity + 2 * row_ids(degrees)
        scaled = (degree * (degree + 1)).astype(F32) / float((M + K) * (M + K + 1))
        damp = 1.0 / (1.0 + scaled * visc)
        damped = (tangent * (damp * damp)).astype(BF16)
        turned[pl.ds(slot(m), lats, stride=waves), :] = jnp.dot(
            table, damped, preferred_element_type=F32
        )
        return carry

    lax.fori_loop(0, waves, one_wave, 0, unroll=2)
    per = x_ref.shape[1] * waves

    def narrow(b, carry):
        out_ref[pl.ds(b * 4, 4)] = (
            turned[pl.ds(b * 4 * per, 4 * per), :]
            .astype(BF16)
            .reshape(4, x_ref.shape[1], waves, LANES)
        )
        return carry

    lax.fori_loop(0, x_ref.shape[0] // 4, narrow, 0, unroll=2)


def middle_stage(x, legendre, viscosity, lev, wave_first, parity):
    waves, _, lats, degrees = legendre.shape
    return pl.pallas_call(
        functools.partial(middle_kernel, parity=parity),
        grid=(1,),
        in_specs=[
            smem_spec(),
            smem_spec(),
            smem_spec(),
            whole_spec(x.shape),
            pl.BlockSpec((waves, 1, lats, degrees), lambda g: (0, parity, 0, 0)),
        ],
        out_specs=whole_spec(x.shape),
        out_shape=hbm_result(x.shape, BF16),
        scratch_shapes=[pltpu.VMEM((lats * waves, LANES), F32)] * 2,
        compiler_params=params(26),
        name="middle_stage",
    )(wave_first, viscosity, lev, x, in_hbm(legendre))


def images_kernel(up_ref, down_ref, lev_ref, x_ref, table_ref, out_ref, part_ref, low_ref, taken):
    waves = x_ref.shape[2]
    lats = x_ref.shape[0] * x_ref.shape[1]
    count = table_ref.shape[0]
    step = pl.program_id(0)

    @pl.when(step == 0)
    def _():
        spread_rows(x_ref, taken)

    up_matrix = sum_matrix(up_ref, lev_ref)
    down_matrix = sum_matrix(down_ref, lev_ref)
    for k in range(count):
        fields = taken[pl.ds(slot(step * count + k), lats, stride=waves), :].astype(BF16)
        image = transform_of(table_ref[k, 0], fields)
        high, low = halves(image)
        out_ref[k] = jnp.concatenate([high, low], axis=1)
        up_sum = jnp.dot(twice(high), up_matrix, preferred_element_type=F32)
        part_ref[k] = pack_levels(up_sum).astype(BF16)
        down_sum = jnp.dot(twice(high), down_matrix, preferred_element_type=F32) + jnp.dot(
            low, down_matrix[:LANES], preferred_element_type=F32
        )
        low_ref[k] = jnp.concatenate(halves(pack_levels(down_sum)), axis=1)


def image_stage(x, legendre, up, down, lev, parity):
    x = in_hbm(x) if parity == 0 else x
    waves, _, lats, degrees = legendre.shape
    steps = 4
    count = waves // steps
    return pl.pallas_call(
        images_kernel,
        grid=(steps,),
        in_specs=[
            smem_spec(),
            smem_spec(),
            smem_spec(),
            whole_spec(x.shape),
            pl.BlockSpec((count, 1, lats, degrees), lambda g: (g, parity, 0, 0)),
        ],
        out_specs=(
            pl.BlockSpec((count, degrees, 2 * LANES), lambda g: (g, 0, 0)),
            pl.BlockSpec((count, degrees // 4, LANES), lambda g: (g, 0, 0)),
            pl.BlockSpec((count, degrees // 4, 2 * LANES), lambda g: (g, 0, 0)),
        ),
        out_shape=(
            hbm_result((waves, degrees, 2 * LANES), BF16),
            jax.ShapeDtypeStruct((waves, degrees // 4, LANES), BF16),
            hbm_result((waves, degrees // 4, 2 * LANES), BF16),
        ),
        scratch_shapes=[pltpu.VMEM((lats * waves, LANES), F32)],
        compiler_params=params(20),
        name="image_stage",
    )(up, down, lev, x, in_hbm(legendre))


def gram_of(high, both):
    return lax.dot_general(high, both, (((0,), (0,)), ((), ())), preferred_element_type=F32)


def gram_kernel(image_ref, out_ref):
    @pl.when(pl.program_id(0) == 0)
    def _():
        out_ref[...] = jnp.zeros_like(out_ref)

    rows = image_ref.shape[0] * image_ref.shape[1]
    both = image_ref[...].reshape(rows, 2 * LANES)
    out_ref[...] += gram_of(both[:, :LANES], both)


def gram_stage(images):
    waves, degrees, _ = images.shape
    steps = 4
    return pl.pallas_call(
        gram_kernel,
        grid=(steps,),
        in_specs=[pl.BlockSpec((waves // steps, degrees, 2 * LANES), lambda g: (g, 0, 0))],
        out_specs=whole_spec((LANES, 2 * LANES)),
        out_shape=jax.ShapeDtypeStruct((LANES, 2 * LANES), F32),
        compiler_params=params(12),
        name="gram_stage",
    )(in_hbm(images))


def finish_kernel(down_ref, lev_ref, *refs):
    first = lev_ref[0] * 4
    square = down_ref[first] * down_ref[first]
    for k in range(1, 4):
        square = square + down_ref[first + k] * down_ref[first + k]
    grams = refs[:2]
    lows = refs[2:4]
    totals = refs[4:12]
    total_ref, gram_ref = refs[12:]
    sums = grams[0][...] + grams[1][...]
    cross = sums[:, LANES:]
    gram = sums[:, :LANES] + (cross + cross.T)
    for p in range(2):
        parts = [ref[...].astype(F32) for ref in totals[4 * p : 4 * p + 4]]
        total = ((parts[0] + parts[1]) + (parts[2] + parts[3])).astype(BF16)
        total_ref[p] = total
        flat = total.reshape(-1, LANES)
        low = lows[p][...].reshape(-1, 2 * LANES)
        operand = jnp.concatenate([flat, low], axis=1)
        result = gram_of(flat, operand)
        mixed = result[:, LANES : 2 * LANES] + result[:, 2 * LANES :]
        gram = gram + square * result[:, :LANES] + (mixed + mixed.T)
    same = (row_ids(LANES) // PROBES) == (lane_ids(LANES) // PROBES)
    gram = jnp.where(same, gram, 0.0)
    summed = gram[0:PROBES]
    for b in range(1, LANES // PROBES):
        summed = summed + gram[b * PROBES : (b + 1) * PROBES]
    for shift in (64, 32, 16):
        summed = summed + pltpu.roll(summed, shift, 1)
    top_lane = (lane_ids(8) & PROBES) == 0
    packed = jnp.where(top_lane, summed[:8], summed[8:])
    gram_ref[...] = jnp.broadcast_to(packed[None], gram_ref.shape)


def finish_stage(grams, lows, totals, down, lev, copies):
    shape = totals[0].shape
    return pl.pallas_call(
        finish_kernel,
        in_specs=[smem_spec(), smem_spec()] + [pl.BlockSpec(memory_space=pltpu.VMEM)] * 12,
        out_shape=(
            hbm_result((2,) + shape, BF16),
            hbm_result((copies, 8, LANES), F32),
        ),
        compiler_params=params(16),
        name="finish_stage",
    )(down, lev, *grams, *lows, *totals)


def factor_of(gram):
    rows = row_ids(PROBES)
    lanes = lane_ids(PROBES) & (PROBES - 1)
    upper = jnp.zeros_like(gram)
    inverse = jnp.where(rows == lanes, 1.0, 0.0).astype(F32)
    for k in range(PROBES):
        scale = lax.rsqrt(gram[k : k + 1, k : k + 1])
        scale = scale * (1.5 - 0.5 * gram[k : k + 1, k : k + 1] * scale * scale)
        line = jnp.where(lanes[0:1] >= k, gram[k : k + 1] * scale, 0.0)
        solved = inverse[k : k + 1] * scale
        column = jnp.where(rows[:, 0:1] > k, gram[:, k : k + 1] * scale, 0.0)
        upper = jnp.where(rows == k, line, upper)
        gram = gram - column * line
        inverse = jnp.where(rows == k, solved, inverse - column * solved)
    return upper, inverse


def basis_kernel(
    own_ref, one_ref, two_ref, three_ref, full_ref, out_ref, factor_ref, mix, *, row_scale
):
    @pl.when(pl.program_id(0) == 0)
    def _():
        packed = (own_ref[...] + two_ref[...]) + (one_ref[...] + three_ref[...])
        top_lane = (lane_ids(8) & PROBES) == 0
        gram = jnp.concatenate(
            [
                jnp.where(top_lane, packed, pltpu.roll(packed, PROBES, 1)),
                jnp.where(top_lane, pltpu.roll(packed, LANES - PROBES, 1), packed),
            ],
            axis=0,
        )
        upper, inverse = factor_of(gram)
        factor_ref[...] = upper[:, :PROBES] / row_scale
        pick = ((lane_ids(PROBES) & (PROBES - 1)) == row_ids(PROBES)).astype(BF16)
        same = (row_ids(LANES) // PROBES) == (lane_ids(LANES) // PROBES)
        high, low = halves(inverse * row_scale)
        mix_high = jnp.where(same, gram_of(high, pick), 0.0).astype(BF16)
        mix_low = jnp.where(same, gram_of(low, pick), 0.0).astype(BF16)
        mix[0:LANES] = mix_high
        mix[LANES : 2 * LANES] = mix_high
        mix[2 * LANES :] = mix_low

    for m in range(full_ref.shape[0]):
        for p in range(2):
            both = full_ref[m, p]
            value = jnp.dot(both, mix[: 2 * LANES], preferred_element_type=F32) + jnp.dot(
                both[:, :LANES], mix[2 * LANES :], preferred_element_type=F32
            )
            out_ref[m, p] = value.astype(BF16)


def full_kernel(down_ref, lev_ref, even_ref, odd_ref, total_ref, out_ref):
    _, waves, quarter, _ = total_ref.shape
    wide = jnp.dot(
        twice(total_ref[...].reshape(2 * waves * quarter, LANES)),
        unpack_matrix(down_ref, lev_ref),
        preferred_element_type=F32,
    )
    for p, image_ref in enumerate((even_ref, odd_ref)):
        for m in range(waves):
            first = (p * waves + m) * quarter
            for g in range(4):
                piece = slice(g * quarter, (g + 1) * quarter)
                both = image_ref[m, piece]
                full = (both[:, :LANES].astype(F32) + both[:, LANES:].astype(F32)) + wide[
                    first : first + quarter, g * LANES : (g + 1) * LANES
                ]
                out_ref[m, p, piece] = jnp.concatenate(halves(full), axis=1)


def full_stage(images, total, down, lev):
    waves, degrees, _ = images[0].shape
    steps = 4
    count = waves // steps
    image_spec = pl.BlockSpec((count, degrees, 2 * LANES), lambda g: (g, 0, 0))
    return pl.pallas_call(
        full_kernel,
        grid=(steps,),
        in_specs=[
            smem_spec(),
            smem_spec(),
            image_spec,
            image_spec,
            pl.BlockSpec((2, count, degrees // 4, LANES), lambda g: (0, g, 0, 0)),
        ],
        out_specs=pl.BlockSpec((count, 2, degrees, 2 * LANES), lambda g: (g, 0, 0, 0)),
        out_shape=hbm_result((waves, 2, degrees, 2 * LANES), BF16),
        compiler_params=params(14),
        name="full_stage",
    )(down, lev, in_hbm(images[0]), in_hbm(images[1]), in_hbm(total))


def basis_stage(grams, full, row_scale):
    waves, _, degrees, _ = full.shape
    steps = 4
    count = waves // steps
    return pl.pallas_call(
        functools.partial(basis_kernel, row_scale=row_scale),
        grid=(steps,),
        in_specs=[whole_spec((8, LANES))] * 4
        + [pl.BlockSpec((count, 2, degrees, 2 * LANES), lambda g: (g, 0, 0, 0))],
        out_specs=(
            pl.BlockSpec((count, 2, degrees, LANES), lambda g: (g, 0, 0, 0)),
            whole_spec((PROBES, PROBES)),
        ),
        out_shape=(
            hbm_result((waves, 2, degrees, LANES), BF16),
            hbm_result((PROBES, PROBES), F32),
        ),
        scratch_shapes=[pltpu.VMEM((3 * LANES, LANES), BF16)],
        compiler_params=params(14),
        name="basis_stage",
    )(*grams, in_hbm(full))


def exchange(blocks):
    return lax.all_to_all(blocks, "lat", split_axis=0, concat_axis=0, tiled=True)


def from_levels(part):
    count = lax.axis_size("lev")
    return [
        lax.ppermute(part, "lev", [(i, (i + k) % count) for i in range(count)])
        for k in range(1, count)
    ]


def shards(
    probes, legendre, quad_weight, trunc_counts, background, level_up, level_down, viscosity
):
    lat_count = lax.axis_size("lat")
    lev_count = lax.axis_size("lev")
    lat_index = lax.axis_index("lat")
    lev_index = lax.axis_index("lev")
    wave_local = probes.shape[0]
    level_local = probes.shape[3] // (2 * PROBES)
    lon_count = 2 * M

    lev = lev_index.astype(jnp.int32).reshape(1)
    wave_first = (lat_index * wave_local).astype(jnp.int32).reshape(1)
    forward = wave_tables(M)
    tables = (jnp.asarray(forward), jnp.asarray(np.ascontiguousarray(forward.transpose(0, 2, 1))))

    sent = {0: exchange(legendre_raw(probes, legendre, 0))}
    partial = level_partial(probes, level_down, lev, 1)
    totals = [partial] + from_levels(partial)
    sent[1] = exchange(legendre_forward(probes, totals, legendre, level_up, lev, 1))

    own_gain = lax.dynamic_slice_in_dim(background, lev_index * level_local, level_local, 2)
    own_gain = own_gain * (quad_weight / float(lon_count))[None, :, None, None]
    own_gain = own_gain.reshape(2, -1, 2, level_local, lon_count).swapaxes(2, 3)
    own_gain = own_gain.reshape(2, -1, 2 * level_local, lon_count).astype(BF16)
    gain = spread_gain(own_gain)

    folded = {}

    def depart(p, values):
        folded[p] = exchange(values)

    def couple_first(x):
        partial = grid_sum(x, level_down, lev)
        total = grid_total(trunc_counts, [partial] + from_levels(partial), tables[0])
        return True, level_up, lev, [total]

    def couple_none(x):
        return False, level_up, lev, []

    grid_pass(lambda p: sent[p], depart, trunc_counts, gain, tables, couple_first, True, False)
    second = {
        p: exchange(middle_stage(folded[p], legendre, viscosity, lev, wave_first, p))
        for p in range(2)
    }
    folded2 = {}

    def depart2(p, values):
        folded2[p] = exchange(values)

    grid_pass(lambda p: second[p], depart2, trunc_counts, gain, tables, couple_none, False, True)
    images, lows, grams, totals = [], [], [], []
    for p in range(2):
        image, part, low = image_stage(folded2[p], legendre, level_up, level_down, lev, p)
        images.append(image)
        lows.append(low)
        grams.append(gram_stage(image))
        totals += [part] + from_levels(part)
    total, gram_copies = finish_stage(grams, lows, totals, level_down, lev, lat_count)
    received = exchange(gram_copies)
    full = full_stage(images, total, level_down, lev)
    over_lat = jnp.sum(received, axis=0)
    row_scale = math.sqrt(M * K * 2 * level_local * lev_count)
    return basis_stage([over_lat] + from_levels(over_lat), full, row_scale)


def solution(mesh):
    placed = (
        P("lat", None, None, "lev"),
        P("lat", None, None, None),
        P("lat"),
        P("lat"),
        P(None, "lat", None, None),
        P(),
        P(),
        P(),
    )
    return jax.shard_map(
        shards,
        mesh=mesh,
        in_specs=placed,
        out_specs=(P("lat", None, None, "lev"), P()),
        check_vma=False,
    )
```

```python
import functools
import math

import jax
import jax.numpy as jnp
import ml_dtypes
import numpy as np
from jax import lax
from jax.experimental import pallas as pl
from jax.experimental.pallas import tpu as pltpu
from jax.sharding import PartitionSpec as P


M = 512
K = 512
PROBES = 16
LANES = 128
F32 = jnp.float32
BF16 = jnp.bfloat16


def params(mib):
    return pltpu.CompilerParams(vmem_limit_bytes=mib << 20)


def in_hbm(values):
    return pltpu.with_memory_space_constraint(values, pltpu.HBM)


def hbm_result(shape, dtype):
    return pltpu.HBM(shape, dtype)


def wave_tables(wave_count):
    lon = np.arange(wave_count)[:, None]
    tables = []
    for parity in range(2):
        zonal = np.arange(parity, wave_count, 2)[None, :]
        phase = (zonal * lon % (2 * wave_count)) * (math.pi / wave_count)
        tables.append(np.concatenate([np.cos(phase), -np.sin(phase)], axis=1))
    return np.stack(tables).astype(np.float32).astype(ml_dtypes.bfloat16)


def spread_table():
    rows = np.arange(8)[:, None]
    lanes = np.arange(LANES)[None, :] // PROBES
    return (rows == lanes).astype(ml_dtypes.bfloat16)


def lane_ids(rows, lanes=LANES):
    return lax.broadcasted_iota(jnp.int32, (rows, lanes), 1)


def row_ids(rows, lanes=LANES):
    return lax.broadcasted_iota(jnp.int32, (rows, lanes), 0)


def halves(values):
    high = values.astype(BF16)
    return high, (values - high.astype(F32)).astype(BF16)


def slot(wave):
    return (wave & 1) * 8 + (wave >> 1)


def own_levels(coef_ref, lev_ref, level):
    first = lev_ref[0] * 4
    coef = jnp.where(level == 0, coef_ref[first], coef_ref[first + 1])
    return jnp.where(
        level < 2, coef, jnp.where(level == 2, coef_ref[first + 2], coef_ref[first + 3])
    )


def sum_matrix(coef_ref, lev_ref):
    rows = row_ids(LANES)
    weights = jnp.where(
        (rows & 31) == (lane_ids(LANES) & 31), own_levels(coef_ref, lev_ref, rows // 32), 0.0
    )
    return jnp.concatenate(halves(weights), axis=0)


def unpack_matrix(coef_ref, lev_ref):
    rows = row_ids(LANES, 4 * LANES)
    lanes = lane_ids(LANES, 4 * LANES)
    level = (lanes & (LANES - 1)) // 32
    hit = (rows // 32 == lanes // LANES) & ((rows & 31) == (lanes & 31))
    weights = jnp.where(hit, own_levels(coef_ref, lev_ref, level), 0.0)
    return jnp.concatenate(halves(weights), axis=0)


def twice(values):
    return jnp.concatenate([values, values], axis=1)


def pack_levels(summed):
    rows = summed.shape[0] // 4
    group = lane_ids(rows) // 32
    low = jnp.where(group == 0, summed[0:rows], summed[rows : 2 * rows])
    high = jnp.where(group == 2, summed[2 * rows : 3 * rows], summed[3 * rows :])
    return jnp.where(group < 2, low, high)


def smem_spec():
    return pl.BlockSpec(memory_space=pltpu.SMEM)


def whole_spec(shape):
    return pl.BlockSpec(shape, lambda g: (0,) * len(shape))


def partial_kernel(coef_ref, lev_ref, probes_ref, out_ref):
    waves, _, degrees, _ = probes_ref.shape
    flat = probes_ref[:, 0].reshape(waves * degrees, LANES)
    summed = jnp.dot(twice(flat), sum_matrix(coef_ref, lev_ref), preferred_element_type=F32)
    for m in range(waves):
        out_ref[m] = pack_levels(summed[m * degrees : (m + 1) * degrees]).astype(BF16)


def level_partial(probes, coef, lev, parity):
    waves, _, degrees, _ = probes.shape
    steps = 2
    return pl.pallas_call(
        partial_kernel,
        grid=(steps,),
        in_specs=[
            smem_spec(),
            smem_spec(),
            pl.BlockSpec((waves // steps, 1, degrees, LANES), lambda g: (g, parity, 0, 0)),
        ],
        out_specs=pl.BlockSpec((waves // steps, degrees // 4, LANES), lambda g: (g, 0, 0)),
        out_shape=jax.ShapeDtypeStruct((waves, degrees // 4, LANES), BF16),
        compiler_params=params(8),
        name="level_partial",
    )(coef, lev, in_hbm(probes))


def legendre_raw_kernel(probes_ref, table_ref, out_ref, turned):
    waves = probes_ref.shape[0]
    rows = table_ref.shape[2]
    for m in range(waves):
        turned[pl.ds(slot(m), rows, stride=waves), :] = jnp.dot(
            table_ref[m, 0], probes_ref[m, 0], preferred_element_type=F32
        )
    out_ref[...] = turned[...].astype(BF16).reshape(out_ref.shape)


def legendre_raw(probes, legendre, parity):
    waves, _, degrees, _ = probes.shape
    lats = legendre.shape[2]
    blocks = lats // waves
    steps = 2
    return pl.pallas_call(
        legendre_raw_kernel,
        grid=(steps,),
        in_specs=[
            pl.BlockSpec((waves, 1, degrees, LANES), lambda g: (0, parity, 0, 0)),
            pl.BlockSpec((waves, 1, lats // steps, degrees), lambda g: (0, parity, g, 0)),
        ],
        out_specs=pl.BlockSpec((blocks // steps, waves, waves, LANES), lambda g: (g, 0, 0, 0)),
        out_shape=hbm_result((blocks, waves, waves, LANES), BF16),
        scratch_shapes=[pltpu.VMEM((lats // steps * waves, LANES), F32)],
        compiler_params=params(20),
        name="legendre_raw",
    )(in_hbm(probes), in_hbm(legendre))


def grid_sum_kernel(coef_ref, lev_ref, x_ref, first_ref, second_ref):
    blocks, lats, waves, _ = x_ref.shape
    flat = x_ref[...].reshape(blocks * lats * waves, LANES)
    summed = jnp.dot(twice(flat), sum_matrix(coef_ref, lev_ref), preferred_element_type=F32)
    summed = summed.reshape(blocks, lats, waves, LANES)
    group = lax.broadcasted_iota(jnp.int32, (blocks, 4, waves, LANES), 3) // 32
    low = jnp.where(group == 0, summed[:, 0:4], summed[:, 4:8])
    high = jnp.where(group == 2, summed[:, 8:12], summed[:, 12:16])
    packed = jnp.where(group < 2, low, high).astype(BF16)
    first_ref[...] = packed[:, :2]
    second_ref[...] = packed[:, 2:]


def grid_sum(x, coef, lev):
    blocks, lats, waves, _ = x.shape
    steps = 4
    return pl.pallas_call(
        grid_sum_kernel,
        grid=(steps,),
        in_specs=[
            smem_spec(),
            smem_spec(),
            pl.BlockSpec((blocks // steps, lats, waves, LANES), lambda g: (g, 0, 0, 0)),
        ],
        out_specs=[pl.BlockSpec((blocks // steps, 2, waves, LANES), lambda g: (g, 0, 0, 0))] * 2,
        out_shape=[jax.ShapeDtypeStruct((blocks, 2, waves, LANES), BF16)] * 2,
        compiler_params=params(12),
        name="grid_sum",
    )(coef, lev, in_hbm(x))


def grid_total_kernel(counts_ref, *refs):
    totals = refs[:4]
    table_ref, out_ref, operand = refs[4:]
    real_lane = (lane_ids(HALF) & PROBES) == 0
    group = lane_ids(HALF) // 32
    zonal = 2 * row_ids(HALF)
    for pair in range(2):
        both = []
        for k in range(2):
            parts = [ref[:, k].astype(F32) for ref in totals[2 * pair : 2 * pair + 2]]
            both.append(parts[0] + parts[1])
        lanes = slice(pair * LANES, (pair + 1) * LANES)
        for parity in range(2):
            masked = []
            for k in range(2):
                x = both[k][:, 8 * parity : 8 * parity + 8].reshape(HALF, LANES)
                lat = 2 * pair + k
                count = jnp.where(
                    group < 2,
                    jnp.where(group == 0, counts_ref[lat], counts_ref[4 + lat]),
                    jnp.where(group == 2, counts_ref[8 + lat], counts_ref[12 + lat]),
                )
                factor = jnp.where(zonal + parity == 0, 1.0, 2.0)
                masked.append(x * jnp.where(zonal + parity < count, factor, 0.0))
            first, second = masked
            operand[parity, :HALF, lanes] = jnp.where(
                real_lane, first, pltpu.roll(second, PROBES, 1)
            ).astype(BF16)
            operand[parity, HALF:, lanes] = jnp.where(
                real_lane, pltpu.roll(first, LANES - PROBES, 1), second
            ).astype(BF16)
    even = jnp.dot(table_ref[0], operand[0], preferred_element_type=F32)
    odd = jnp.dot(table_ref[1], operand[1], preferred_element_type=F32)
    out_ref[0] = (even + odd).astype(BF16)
    out_ref[1] = (even - odd).astype(BF16)


def grid_total(counts, totals, forward):
    shape = (2, M, 2 * LANES)
    vmem = pl.BlockSpec(memory_space=pltpu.VMEM)
    return pl.pallas_call(
        grid_total_kernel,
        in_specs=[smem_spec()] + [vmem] * 5,
        out_shape=hbm_result(shape, BF16),
        scratch_shapes=[pltpu.VMEM(shape, BF16)],
        compiler_params=params(12),
        name="grid_total",
    )(counts, *totals, forward)


def place_matrix(coef_ref, lev_ref, taken_group):
    rows = row_ids(LANES)
    lanes = lane_ids(LANES)
    hit = (rows // 32 == taken_group) & ((rows & 31) == (lanes & 31))
    weights = jnp.where(hit, own_levels(coef_ref, lev_ref, lanes // 32), 0.0)
    return jnp.concatenate(halves(weights), axis=0)


def legendre_kernel(coef_ref, lev_ref, probes_ref, *refs):
    totals = refs[:4]
    table_ref, out_ref, mixed, turned = refs[4:]
    waves = probes_ref.shape[0]
    rows = table_ref.shape[2]

    @pl.when(pl.program_id(0) == 0)
    def _():
        parts = [ref[...].astype(F32) for ref in totals]
        total = ((parts[0] + parts[1]) + (parts[2] + parts[3])).astype(BF16)
        quarter = total.shape[1]
        wide = jnp.dot(
            twice(total.reshape(waves * quarter, LANES)),
            unpack_matrix(coef_ref, lev_ref),
            preferred_element_type=F32,
        )
        for m in range(waves):
            for g in range(4):
                piece = slice(g * quarter, (g + 1) * quarter)
                mixed[m, piece] = (
                    probes_ref[m, 0, piece].astype(F32)
                    + wide[m * quarter : (m + 1) * quarter, g * LANES : (g + 1) * LANES]
                ).astype(BF16)

    for m in range(waves):
        turned[pl.ds(slot(m), rows, stride=waves), :] = jnp.dot(
            table_ref[m, 0], mixed[m], preferred_element_type=F32
        )
    out_ref[...] = turned[...].astype(BF16).reshape(out_ref.shape)


def legendre_forward(probes, totals, legendre, coef, lev, parity):
    waves, _, degrees, _ = probes.shape
    lats = legendre.shape[2]
    blocks = lats // waves
    steps = 2
    total_spec = whole_spec(totals[0].shape)
    return pl.pallas_call(
        legendre_kernel,
        grid=(steps,),
        in_specs=[
            smem_spec(),
            smem_spec(),
            pl.BlockSpec((waves, 1, degrees, LANES), lambda g: (0, parity, 0, 0)),
        ]
        + [total_spec] * 4
        + [pl.BlockSpec((waves, 1, lats // steps, degrees), lambda g: (0, parity, g, 0))],
        out_specs=pl.BlockSpec((blocks // steps, waves, waves, LANES), lambda g: (g, 0, 0, 0)),
        out_shape=hbm_result((blocks, waves, waves, LANES), BF16),
        scratch_shapes=[
            pltpu.VMEM((waves, degrees, LANES), BF16),
            pltpu.VMEM((lats // steps * waves, LANES), F32),
        ],
        compiler_params=params(24),
        name="legendre_forward",
    )(coef, lev, in_hbm(probes), *totals, in_hbm(legendre))


HALF = M // 2


def mask_rows(count, parity):
    zonal = 2 * row_ids(HALF) + parity
    factor = jnp.where(zonal == 0, 1.0, 2.0)
    return jnp.where(zonal < count, factor, 0.0).astype(F32)


def load_waves(counts_ref, x_ref, operand, masked):
    step = pl.program_id(0)
    real_lane = (lane_ids(HALF) & PROBES) == 0
    for pair in range(2):
        both = [x_ref[:, 2 * pair + k].astype(F32) for k in range(2)]
        lanes = slice(pair * LANES, (pair + 1) * LANES)
        for parity in range(2):
            first, second = [
                x[:, 8 * parity : 8 * parity + 8].reshape(HALF, LANES) for x in both
            ]
            if masked:
                first = first * mask_rows(counts_ref[4 * step + 2 * pair], parity)
                second = second * mask_rows(counts_ref[4 * step + 2 * pair + 1], parity)
            operand[parity, :HALF, lanes] = jnp.where(
                real_lane, first, pltpu.roll(second, PROBES, 1)
            ).astype(BF16)
            operand[parity, HALF:, lanes] = jnp.where(
                real_lane, pltpu.roll(first, LANES - PROBES, 1), second
            ).astype(BF16)


def store_waves(counts_ref, fields, table_ref, out_ref, masked):
    step = pl.program_id(0)
    real_lane = (lane_ids(HALF) & PROBES) == 0
    results = {}
    for parity in range(2):
        cos_part = jnp.dot(table_ref[parity, :HALF], fields[parity], preferred_element_type=F32)
        sin_part = jnp.dot(table_ref[parity, HALF:], fields[parity], preferred_element_type=F32)
        for pair in range(2):
            cosine = cos_part[:, pair * LANES : (pair + 1) * LANES]
            sine = sin_part[:, pair * LANES : (pair + 1) * LANES]
            first = jnp.where(real_lane, cosine, pltpu.roll(sine, PROBES, 1))
            second = jnp.where(real_lane, pltpu.roll(cosine, LANES - PROBES, 1), sine)
            if masked:
                first = first * mask_rows(counts_ref[4 * step + 2 * pair], parity)
                second = second * mask_rows(counts_ref[4 * step + 2 * pair + 1], parity)
            results[2 * pair, parity] = first.reshape(-1, 8, LANES)
            results[2 * pair + 1, parity] = second.reshape(-1, 8, LANES)
    for k in range(4):
        out_ref[:, k] = jnp.concatenate([results[k, 0], results[k, 1]], axis=1).astype(BF16)


def grid_even_kernel(counts_ref, x_ref, table_ref, out_ref, operand, *, masked):
    load_waves(counts_ref, x_ref, operand, masked)
    even = jnp.dot(table_ref[0], operand[0], preferred_element_type=F32)
    odd = jnp.dot(table_ref[1], operand[1], preferred_element_type=F32)
    out_ref[0, 0] = (even + odd).astype(BF16)
    out_ref[0, 1] = (even - odd).astype(BF16)


def grid_middle_kernel(
    counts_ref, coef_ref, lev_ref, x_ref, even_ref, *refs, coupled, masked_in, masked_out
):
    if coupled:
        total_ref, refs = refs[0], refs[1:]
    gain_ref, forward_ref, inverse_ref, out_ref, odd_ref, operand, fields = refs
    if coupled:
        place = place_matrix(coef_ref, lev_ref, pl.program_id(0))
    load_waves(counts_ref, x_ref, operand, masked_in)
    size = 256
    for r in range(0, M, size):
        rows = slice(r, r + size)
        even = jnp.dot(forward_ref[0, rows], operand[0], preferred_element_type=F32)
        odd = jnp.dot(forward_ref[1, rows], operand[1], preferred_element_type=F32)
        for pair in range(2):
            lanes = slice(pair * LANES, (pair + 1) * LANES)
            kept = []
            for half, sent in enumerate((even[:, lanes] + odd[:, lanes], even[:, lanes] - odd[:, lanes])):
                base = even_ref[0, half, rows, lanes].astype(F32)
                if coupled:
                    base = base + jnp.dot(
                        twice(total_ref[half, rows, lanes]), place, preferred_element_type=F32
                    )
                longitudes = slice(half * M + r, half * M + r + size)
                north = gain_ref[0, pair, longitudes].astype(F32) * (base + sent)
                south = gain_ref[1, pair, longitudes].astype(F32) * (base - sent)
                kept.append((north + south, north - south))
            fields[0, rows, lanes] = (kept[0][0] + kept[1][0]).astype(BF16)
            fields[1, rows, lanes] = (kept[0][0] - kept[1][0]).astype(BF16)
            odd_ref[0, 0, rows, lanes] = (kept[0][1] + kept[1][1]).astype(BF16)
            odd_ref[0, 1, rows, lanes] = (kept[0][1] - kept[1][1]).astype(BF16)
    store_waves(counts_ref, fields, inverse_ref, out_ref, masked_out)


def grid_odd_kernel(counts_ref, odd_ref, table_ref, out_ref, *, masked):
    store_waves(counts_ref, odd_ref[0], table_ref, out_ref, masked)


def gain_kernel(gain_ref, spread_ref, out_ref):
    for h in range(2):
        out_ref[h, 0] = lax.dot_general(
            gain_ref[h, 0], spread_ref[...], (((0,), (0,)), ((), ())), preferred_element_type=F32
        ).astype(BF16)


def spread_gain(gain):
    pairs = gain.shape[1]
    return pl.pallas_call(
        gain_kernel,
        grid=(pairs,),
        in_specs=[
            pl.BlockSpec((2, 1, 8, 2 * M), lambda g: (0, g, 0, 0)),
            whole_spec((8, LANES)),
        ],
        out_specs=pl.BlockSpec((2, 1, 2 * M, LANES), lambda g: (0, g, 0, 0)),
        out_shape=hbm_result((2, pairs, 2 * M, LANES), BF16),
        compiler_params=params(8),
        name="spread_gain",
    )(gain, jnp.asarray(spread_table()))


def wave_block(x):
    return pl.BlockSpec((x.shape[0], 4, x.shape[2], LANES), lambda g: (0, g, 0, 0))


def grid_pass(arrive, depart, counts, gain, tables, coupling, masked_in, masked_out):
    forward, inverse = tables
    x_even = arrive(0)
    steps = x_even.shape[1] // 4
    field_spec = pl.BlockSpec((1, 2, M, 2 * LANES), lambda g: (g, 0, 0, 0))
    field_shape = (steps, 2, M, 2 * LANES)
    operand = pltpu.VMEM((2, M, 2 * LANES), BF16)
    even = pl.pallas_call(
        functools.partial(grid_even_kernel, masked=masked_in),
        grid=(steps,),
        in_specs=[smem_spec(), wave_block(x_even), whole_spec(forward.shape)],
        out_specs=field_spec,
        out_shape=hbm_result(field_shape, BF16),
        scratch_shapes=[operand],
        compiler_params=params(16),
        name="grid_even",
    )(counts, in_hbm(x_even), in_hbm(forward))
    x_odd = arrive(1)
    out_shape = hbm_result(x_odd.shape, BF16)
    coupled, coef, lev, total = coupling(x_even)
    y_even, odd = pl.pallas_call(
        functools.partial(
            grid_middle_kernel, coupled=coupled, masked_in=masked_in, masked_out=masked_out
        ),
        grid=(steps,),
        in_specs=[
            smem_spec(),
            smem_spec(),
            smem_spec(),
            wave_block(x_odd),
            field_spec,
        ]
        + [whole_spec(x.shape) for x in total]
        + [
            pl.BlockSpec((2, 2, 2 * M, LANES), lambda g: (0, g, 0, 0)),
            whole_spec(forward.shape),
            whole_spec(inverse.shape),
        ],
        out_specs=(wave_block(x_odd), field_spec),
        out_shape=(out_shape, hbm_result(field_shape, BF16)),
        scratch_shapes=[operand, operand],
        compiler_params=params(24),
        name="grid_middle",
    )(counts, coef, lev, x_odd, in_hbm(even), *[in_hbm(x) for x in total], in_hbm(gain), in_hbm(forward), in_hbm(inverse))
    depart(0, y_even)
    y_odd = odd_stage(counts, odd, inverse, x_odd, masked_out)
    depart(1, y_odd)


def odd_stage(counts, odd, inverse, like, masked_out):
    steps = odd.shape[0]
    field_spec = pl.BlockSpec((1, 2, M, 2 * LANES), lambda g: (g, 0, 0, 0))
    return pl.pallas_call(
        functools.partial(grid_odd_kernel, masked=masked_out),
        grid=(steps,),
        in_specs=[smem_spec(), field_spec, whole_spec(inverse.shape)],
        out_specs=wave_block(like),
        out_shape=hbm_result(like.shape, BF16),
        compiler_params=params(16),
        name="grid_odd",
    )(counts, in_hbm(odd), in_hbm(inverse))


def spread_rows(x_ref, scratch):
    chunk = 4
    per = x_ref.shape[1] * x_ref.shape[2]

    def widen(b, carry):
        scratch[pl.ds(b * chunk * per, chunk * per), :] = (
            x_ref[pl.ds(b * chunk, chunk)].astype(F32).reshape(chunk * per, LANES)
        )
        return carry

    lax.fori_loop(0, x_ref.shape[0] // chunk, widen, 0, unroll=2)


def transform_of(table, fields):
    return lax.dot_general(table, fields, (((0,), (0,)), ((), ())), preferred_element_type=F32)


def middle_kernel(first_ref, visc_ref, lev_ref, x_ref, table_ref, out_ref, taken, turned, *, parity):
    waves = x_ref.shape[2]
    lats = x_ref.shape[0] * x_ref.shape[1]
    degrees = table_ref.shape[3]
    spread_rows(x_ref, taken)
    visc = own_levels(visc_ref, lev_ref, lane_ids(degrees) // 32)

    def one_wave(m, carry):
        fields = taken[pl.ds(slot(m), lats, stride=waves), :].astype(BF16)
        table = table_ref[m, 0]
        tangent = transform_of(table, fields)
        degree = first_ref[0] + m + parity + 2 * row_ids(degrees)
        scaled = (degree * (degree + 1)).astype(F32) / float((M + K) * (M + K + 1))
        damp = 1.0 / (1.0 + scaled * visc)
        damped = (tangent * (damp * damp)).astype(BF16)
        turned[pl.ds(slot(m), lats, stride=waves), :] = jnp.dot(
            table, damped, preferred_element_type=F32
        )
        return carry

    lax.fori_loop(0, waves, one_wave, 0, unroll=2)
    per = x_ref.shape[1] * waves

    def narrow(b, carry):
        out_ref[pl.ds(b * 4, 4)] = (
            turned[pl.ds(b * 4 * per, 4 * per), :]
            .astype(BF16)
            .reshape(4, x_ref.shape[1], waves, LANES)
        )
        return carry

    lax.fori_loop(0, x_ref.shape[0] // 4, narrow, 0, unroll=2)


def middle_stage(x, legendre, viscosity, lev, wave_first, parity):
    waves, _, lats, degrees = legendre.shape
    return pl.pallas_call(
        functools.partial(middle_kernel, parity=parity),
        grid=(1,),
        in_specs=[
            smem_spec(),
            smem_spec(),
            smem_spec(),
            whole_spec(x.shape),
            pl.BlockSpec((waves, 1, lats, degrees), lambda g: (0, parity, 0, 0)),
        ],
        out_specs=whole_spec(x.shape),
        out_shape=hbm_result(x.shape, BF16),
        scratch_shapes=[pltpu.VMEM((lats * waves, LANES), F32)] * 2,
        compiler_params=params(26),
        name="middle_stage",
    )(wave_first, viscosity, lev, x, in_hbm(legendre))


def images_kernel(up_ref, down_ref, lev_ref, x_ref, table_ref, out_ref, part_ref, low_ref, taken):
    waves = x_ref.shape[2]
    lats = x_ref.shape[0] * x_ref.shape[1]
    count = table_ref.shape[0]
    step = pl.program_id(0)

    @pl.when(step == 0)
    def _():
        spread_rows(x_ref, taken)

    down_matrix = sum_matrix(down_ref, lev_ref)
    matrix = jnp.concatenate([sum_matrix(up_ref, lev_ref), down_matrix], axis=1)
    highs, lows = [], []
    for k in range(count):
        fields = taken[pl.ds(slot(step * count + k), lats, stride=waves), :].astype(BF16)
        high, low = halves(transform_of(table_ref[k, 0], fields))
        out_ref[k] = jnp.concatenate([high, low], axis=1)
        highs.append(high)
        lows.append(low)
    sums = jnp.dot(
        twice(jnp.concatenate(highs, axis=0)), matrix, preferred_element_type=F32
    )
    rest = jnp.dot(
        jnp.concatenate(lows, axis=0), down_matrix[:LANES], preferred_element_type=F32
    )
    degrees = table_ref.shape[3]
    for k in range(count):
        rows = slice(k * degrees, (k + 1) * degrees)
        part_ref[k] = pack_levels(sums[rows, :LANES]).astype(BF16)
        low_ref[k] = jnp.concatenate(
            halves(pack_levels(sums[rows, LANES:] + rest[rows])), axis=1
        )


def image_stage(x, legendre, up, down, lev, parity):
    x = in_hbm(x) if parity == 0 else x
    waves, _, lats, degrees = legendre.shape
    steps = 4
    count = waves // steps
    return pl.pallas_call(
        images_kernel,
        grid=(steps,),
        in_specs=[
            smem_spec(),
            smem_spec(),
            smem_spec(),
            whole_spec(x.shape),
            pl.BlockSpec((count, 1, lats, degrees), lambda g: (g, parity, 0, 0)),
        ],
        out_specs=(
            pl.BlockSpec((count, degrees, 2 * LANES), lambda g: (g, 0, 0)),
            pl.BlockSpec((count, degrees // 4, LANES), lambda g: (g, 0, 0)),
            pl.BlockSpec((count, degrees // 4, 2 * LANES), lambda g: (g, 0, 0)),
        ),
        out_shape=(
            hbm_result((waves, degrees, 2 * LANES), BF16),
            jax.ShapeDtypeStruct((waves, degrees // 4, LANES), BF16),
            hbm_result((waves, degrees // 4, 2 * LANES), BF16),
        ),
        scratch_shapes=[pltpu.VMEM((lats * waves, LANES), F32)],
        compiler_params=params(20),
        name="image_stage",
    )(up, down, lev, x, in_hbm(legendre))


def gram_of(high, both):
    return lax.dot_general(high, both, (((0,), (0,)), ((), ())), preferred_element_type=F32)


def gram_kernel(image_ref, out_ref):
    @pl.when(pl.program_id(0) == 0)
    def _():
        out_ref[...] = jnp.zeros_like(out_ref)

    rows = image_ref.shape[0] * image_ref.shape[1]
    both = image_ref[...].reshape(rows, 2 * LANES)
    out_ref[...] += gram_of(both[:, :LANES], both)


def gram_stage(images):
    waves, degrees, _ = images.shape
    steps = 4
    return pl.pallas_call(
        gram_kernel,
        grid=(steps,),
        in_specs=[pl.BlockSpec((waves // steps, degrees, 2 * LANES), lambda g: (g, 0, 0))],
        out_specs=whole_spec((LANES, 2 * LANES)),
        out_shape=jax.ShapeDtypeStruct((LANES, 2 * LANES), F32),
        compiler_params=params(12),
        name="gram_stage",
    )(in_hbm(images))


def finish_kernel(down_ref, lev_ref, *refs):
    first = lev_ref[0] * 4
    square = down_ref[first] * down_ref[first]
    for k in range(1, 4):
        square = square + down_ref[first + k] * down_ref[first + k]
    grams = refs[:2]
    lows = refs[2:4]
    totals = refs[4:12]
    total_ref, gram_ref = refs[12:]
    sums = grams[0][...] + grams[1][...]
    cross = sums[:, LANES:]
    gram = sums[:, :LANES] + (cross + cross.T)
    for p in range(2):
        parts = [ref[...].astype(F32) for ref in totals[4 * p : 4 * p + 4]]
        total = ((parts[0] + parts[1]) + (parts[2] + parts[3])).astype(BF16)
        total_ref[p] = total
        flat = total.reshape(-1, LANES)
        low = lows[p][...].reshape(-1, 2 * LANES)
        operand = jnp.concatenate([flat, low], axis=1)
        result = gram_of(flat, operand)
        mixed = result[:, LANES : 2 * LANES] + result[:, 2 * LANES :]
        gram = gram + square * result[:, :LANES] + (mixed + mixed.T)
    same = (row_ids(LANES) // PROBES) == (lane_ids(LANES) // PROBES)
    gram = jnp.where(same, gram, 0.0)
    summed = gram[0:PROBES]
    for b in range(1, LANES // PROBES):
        summed = summed + gram[b * PROBES : (b + 1) * PROBES]
    for shift in (64, 32, 16):
        summed = summed + pltpu.roll(summed, shift, 1)
    top_lane = (lane_ids(8) & PROBES) == 0
    packed = jnp.where(top_lane, summed[:8], summed[8:])
    gram_ref[...] = jnp.broadcast_to(packed[None], gram_ref.shape)


def finish_stage(grams, lows, totals, down, lev, copies):
    shape = totals[0].shape
    return pl.pallas_call(
        finish_kernel,
        in_specs=[smem_spec(), smem_spec()] + [pl.BlockSpec(memory_space=pltpu.VMEM)] * 12,
        out_shape=(
            hbm_result((2,) + shape, BF16),
            hbm_result((copies, 8, LANES), F32),
        ),
        compiler_params=params(16),
        name="finish_stage",
    )(down, lev, *grams, *lows, *totals)


def factor_of(gram):
    rows = row_ids(PROBES)
    lanes = lane_ids(PROBES) & (PROBES - 1)
    upper = jnp.zeros_like(gram)
    inverse = jnp.where(rows == lanes, 1.0, 0.0).astype(F32)
    for k in range(PROBES):
        scale = lax.rsqrt(gram[k : k + 1, k : k + 1])
        scale = scale * (1.5 - 0.5 * gram[k : k + 1, k : k + 1] * scale * scale)
        line = jnp.where(lanes[0:1] >= k, gram[k : k + 1] * scale, 0.0)
        solved = inverse[k : k + 1] * scale
        column = jnp.where(rows[:, 0:1] > k, gram[:, k : k + 1] * scale, 0.0)
        upper = jnp.where(rows == k, line, upper)
        gram = gram - column * line
        inverse = jnp.where(rows == k, solved, inverse - column * solved)
    return upper, inverse


def basis_kernel(
    own_ref, one_ref, two_ref, three_ref, full_ref, out_ref, factor_ref, mix, *, row_scale
):
    @pl.when(pl.program_id(0) == 0)
    def _():
        packed = (own_ref[...] + two_ref[...]) + (one_ref[...] + three_ref[...])
        top_lane = (lane_ids(8) & PROBES) == 0
        gram = jnp.concatenate(
            [
                jnp.where(top_lane, packed, pltpu.roll(packed, PROBES, 1)),
                jnp.where(top_lane, pltpu.roll(packed, LANES - PROBES, 1), packed),
            ],
            axis=0,
        )
        upper, inverse = factor_of(gram)
        factor_ref[...] = upper[:, :PROBES] / row_scale
        pick = ((lane_ids(PROBES) & (PROBES - 1)) == row_ids(PROBES)).astype(BF16)
        same = (row_ids(LANES) // PROBES) == (lane_ids(LANES) // PROBES)
        high, low = halves(inverse * row_scale)
        mix_high = jnp.where(same, gram_of(high, pick), 0.0).astype(BF16)
        mix_low = jnp.where(same, gram_of(low, pick), 0.0).astype(BF16)
        mix[0:LANES] = mix_high
        mix[LANES : 2 * LANES] = mix_high
        mix[2 * LANES :] = mix_low

    for m in range(full_ref.shape[0]):
        for p in range(2):
            both = full_ref[m, p]
            value = jnp.dot(both, mix[: 2 * LANES], preferred_element_type=F32) + jnp.dot(
                both[:, :LANES], mix[2 * LANES :], preferred_element_type=F32
            )
            out_ref[m, p] = value.astype(BF16)


def full_kernel(down_ref, lev_ref, even_ref, odd_ref, total_ref, out_ref):
    _, waves, quarter, _ = total_ref.shape
    wide = jnp.dot(
        twice(total_ref[...].reshape(2 * waves * quarter, LANES)),
        unpack_matrix(down_ref, lev_ref),
        preferred_element_type=F32,
    )
    for p, image_ref in enumerate((even_ref, odd_ref)):
        for m in range(waves):
            first = (p * waves + m) * quarter
            for g in range(4):
                piece = slice(g * quarter, (g + 1) * quarter)
                both = image_ref[m, piece]
                full = (both[:, :LANES].astype(F32) + both[:, LANES:].astype(F32)) + wide[
                    first : first + quarter, g * LANES : (g + 1) * LANES
                ]
                out_ref[m, p, piece] = jnp.concatenate(halves(full), axis=1)


def full_stage(images, total, down, lev):
    waves, degrees, _ = images[0].shape
    steps = 4
    count = waves // steps
    image_spec = pl.BlockSpec((count, degrees, 2 * LANES), lambda g: (g, 0, 0))
    return pl.pallas_call(
        full_kernel,
        grid=(steps,),
        in_specs=[
            smem_spec(),
            smem_spec(),
            image_spec,
            image_spec,
            pl.BlockSpec((2, count, degrees // 4, LANES), lambda g: (0, g, 0, 0)),
        ],
        out_specs=pl.BlockSpec((count, 2, degrees, 2 * LANES), lambda g: (g, 0, 0, 0)),
        out_shape=hbm_result((waves, 2, degrees, 2 * LANES), BF16),
        compiler_params=params(14),
        name="full_stage",
    )(down, lev, in_hbm(images[0]), in_hbm(images[1]), in_hbm(total))


def basis_stage(grams, full, row_scale):
    waves, _, degrees, _ = full.shape
    steps = 4
    count = waves // steps
    return pl.pallas_call(
        functools.partial(basis_kernel, row_scale=row_scale),
        grid=(steps,),
        in_specs=[whole_spec((8, LANES))] * 4
        + [pl.BlockSpec((count, 2, degrees, 2 * LANES), lambda g: (g, 0, 0, 0))],
        out_specs=(
            pl.BlockSpec((count, 2, degrees, LANES), lambda g: (g, 0, 0, 0)),
            whole_spec((PROBES, PROBES)),
        ),
        out_shape=(
            hbm_result((waves, 2, degrees, LANES), BF16),
            hbm_result((PROBES, PROBES), F32),
        ),
        scratch_shapes=[pltpu.VMEM((3 * LANES, LANES), BF16)],
        compiler_params=params(14),
        name="basis_stage",
    )(*grams, in_hbm(full))


def exchange(blocks):
    return lax.all_to_all(blocks, "lat", split_axis=0, concat_axis=0, tiled=True)


def from_levels(part):
    count = lax.axis_size("lev")
    return [
        lax.ppermute(part, "lev", [(i, (i + k) % count) for i in range(count)])
        for k in range(1, count)
    ]


def add_partner(values, pairs):
    return (values.astype(F32) + lax.ppermute(values, "lev", pairs).astype(F32)).astype(BF16)


def shards(
    probes, legendre, quad_weight, trunc_counts, background, level_up, level_down, viscosity
):
    lat_count = lax.axis_size("lat")
    lev_count = lax.axis_size("lev")
    lat_index = lax.axis_index("lat")
    lev_index = lax.axis_index("lev")
    wave_local = probes.shape[0]
    level_local = probes.shape[3] // (2 * PROBES)
    lon_count = 2 * M

    lev = lev_index.astype(jnp.int32).reshape(1)
    wave_first = (lat_index * wave_local).astype(jnp.int32).reshape(1)
    forward = wave_tables(M)
    tables = (jnp.asarray(forward), jnp.asarray(np.ascontiguousarray(forward.transpose(0, 2, 1))))

    sent = {0: exchange(legendre_raw(probes, legendre, 0))}
    partial = level_partial(probes, level_down, lev, 1)
    totals = [partial] + from_levels(partial)
    sent[1] = exchange(legendre_forward(probes, totals, legendre, level_up, lev, 1))

    own_gain = lax.dynamic_slice_in_dim(background, lev_index * level_local, level_local, 2)
    own_gain = own_gain * (quad_weight / float(lon_count))[None, :, None, None]
    own_gain = own_gain.reshape(2, -1, 2, level_local, lon_count).swapaxes(2, 3)
    own_gain = own_gain.reshape(2, -1, 2 * level_local, lon_count).astype(BF16)
    gain = spread_gain(own_gain)

    folded = {}

    def depart(p, values):
        folded[p] = exchange(values)

    def couple_first(x):
        near = [(i, i ^ 1) for i in range(lev_count)]
        far = [(i, lev_count - 1 - i) for i in range(lev_count)]
        first, second = grid_sum(x, level_down, lev)
        first = add_partner(first, near)
        second = add_partner(second, far)
        parts = [
            first,
            lax.ppermute(first, "lev", far),
            second,
            lax.ppermute(second, "lev", near),
        ]
        total = grid_total(trunc_counts, parts, tables[0])
        return True, level_up, lev, [total]

    def couple_none(x):
        return False, level_up, lev, []

    grid_pass(lambda p: sent[p], depart, trunc_counts, gain, tables, couple_first, True, False)
    second = {
        p: exchange(middle_stage(folded[p], legendre, viscosity, lev, wave_first, p))
        for p in range(2)
    }
    folded2 = {}

    def depart2(p, values):
        folded2[p] = exchange(values)

    grid_pass(lambda p: second[p], depart2, trunc_counts, gain, tables, couple_none, False, True)
    images, lows, grams, totals = [], [], [], []
    for p in range(2):
        image, part, low = image_stage(folded2[p], legendre, level_up, level_down, lev, p)
        images.append(image)
        lows.append(low)
        grams.append(gram_stage(image))
        totals += [part] + from_levels(part)
    total, gram_copies = finish_stage(grams, lows, totals, level_down, lev, lat_count)
    received = exchange(gram_copies)
    full = full_stage(images, total, level_down, lev)
    over_lat = jnp.sum(received, axis=0)
    row_scale = math.sqrt(M * K * 2 * level_local * lev_count)
    return basis_stage([over_lat] + from_levels(over_lat), full, row_scale)


def solution(mesh):
    placed = (
        P("lat", None, None, "lev"),
        P("lat", None, None, None),
        P("lat"),
        P("lat"),
        P(None, "lat", None, None),
        P(),
        P(),
        P(),
    )
    return jax.shard_map(
        shards,
        mesh=mesh,
        in_specs=placed,
        out_specs=(P("lat", None, None, "lev"), P()),
        check_vma=False,
    )
```

```python
import functools
import math

import jax
import jax.numpy as jnp
import ml_dtypes
import numpy as np
from jax import lax
from jax.experimental import pallas as pl
from jax.experimental.pallas import tpu as pltpu
from jax.sharding import PartitionSpec as P


M = 512
K = 512
PROBES = 16
LANES = 128
F32 = jnp.float32
BF16 = jnp.bfloat16


def params(mib):
    return pltpu.CompilerParams(vmem_limit_bytes=mib << 20)


def in_hbm(values):
    return pltpu.with_memory_space_constraint(values, pltpu.HBM)


def hbm_result(shape, dtype):
    return pltpu.HBM(shape, dtype)


def wave_tables(wave_count):
    lon = np.arange(wave_count)[:, None]
    tables = []
    for parity in range(2):
        zonal = np.arange(parity, wave_count, 2)[None, :]
        phase = (zonal * lon % (2 * wave_count)) * (math.pi / wave_count)
        tables.append(np.concatenate([np.cos(phase), -np.sin(phase)], axis=1))
    return np.stack(tables).astype(np.float32).astype(ml_dtypes.bfloat16)


def spread_table():
    rows = np.arange(8)[:, None]
    lanes = np.arange(LANES)[None, :] // PROBES
    return (rows == lanes).astype(ml_dtypes.bfloat16)


def lane_ids(rows, lanes=LANES):
    return lax.broadcasted_iota(jnp.int32, (rows, lanes), 1)


def row_ids(rows, lanes=LANES):
    return lax.broadcasted_iota(jnp.int32, (rows, lanes), 0)


def halves(values):
    high = values.astype(BF16)
    return high, (values - high.astype(F32)).astype(BF16)


def slot(wave):
    return (wave & 1) * 8 + (wave >> 1)


def own_levels(coef_ref, lev_ref, level):
    first = lev_ref[0] * 4
    coef = jnp.where(level == 0, coef_ref[first], coef_ref[first + 1])
    return jnp.where(
        level < 2, coef, jnp.where(level == 2, coef_ref[first + 2], coef_ref[first + 3])
    )


def sum_matrix(coef_ref, lev_ref):
    rows = row_ids(LANES)
    weights = jnp.where(
        (rows & 31) == (lane_ids(LANES) & 31), own_levels(coef_ref, lev_ref, rows // 32), 0.0
    )
    return jnp.concatenate(halves(weights), axis=0)


def unpack_matrix(coef_ref, lev_ref):
    rows = row_ids(LANES, 4 * LANES)
    lanes = lane_ids(LANES, 4 * LANES)
    level = (lanes & (LANES - 1)) // 32
    hit = (rows // 32 == lanes // LANES) & ((rows & 31) == (lanes & 31))
    weights = jnp.where(hit, own_levels(coef_ref, lev_ref, level), 0.0)
    return jnp.concatenate(halves(weights), axis=0)


def twice(values):
    return jnp.concatenate([values, values], axis=1)


def pack_levels(summed):
    rows = summed.shape[0] // 4
    group = lane_ids(rows) // 32
    low = jnp.where(group == 0, summed[0:rows], summed[rows : 2 * rows])
    high = jnp.where(group == 2, summed[2 * rows : 3 * rows], summed[3 * rows :])
    return jnp.where(group < 2, low, high)


def smem_spec():
    return pl.BlockSpec(memory_space=pltpu.SMEM)


def whole_spec(shape):
    return pl.BlockSpec(shape, lambda g: (0,) * len(shape))


def partial_kernel(coef_ref, lev_ref, probes_ref, out_ref):
    waves, _, degrees, _ = probes_ref.shape
    flat = probes_ref[:, 0].reshape(waves * degrees, LANES)
    summed = jnp.dot(twice(flat), sum_matrix(coef_ref, lev_ref), preferred_element_type=F32)
    for m in range(waves):
        out_ref[m] = pack_levels(summed[m * degrees : (m + 1) * degrees]).astype(BF16)


def level_partial(probes, coef, lev, parity):
    waves, _, degrees, _ = probes.shape
    steps = 2
    return pl.pallas_call(
        partial_kernel,
        grid=(steps,),
        in_specs=[
            smem_spec(),
            smem_spec(),
            pl.BlockSpec((waves // steps, 1, degrees, LANES), lambda g: (g, parity, 0, 0)),
        ],
        out_specs=pl.BlockSpec((waves // steps, degrees // 4, LANES), lambda g: (g, 0, 0)),
        out_shape=jax.ShapeDtypeStruct((waves, degrees // 4, LANES), BF16),
        compiler_params=params(8),
        name="level_partial",
    )(coef, lev, in_hbm(probes))


def legendre_raw_kernel(probes_ref, table_ref, out_ref, turned):
    waves = probes_ref.shape[0]
    rows = table_ref.shape[2]
    for m in range(waves):
        turned[pl.ds(slot(m), rows, stride=waves), :] = jnp.dot(
            table_ref[m, 0], probes_ref[m, 0], preferred_element_type=F32
        )
    out_ref[...] = turned[...].astype(BF16).reshape(out_ref.shape)


def legendre_raw(probes, legendre, parity):
    waves, _, degrees, _ = probes.shape
    lats = legendre.shape[2]
    blocks = lats // waves
    steps = 2
    return pl.pallas_call(
        legendre_raw_kernel,
        grid=(steps,),
        in_specs=[
            pl.BlockSpec((waves, 1, degrees, LANES), lambda g: (0, parity, 0, 0)),
            pl.BlockSpec((waves, 1, lats // steps, degrees), lambda g: (0, parity, g, 0)),
        ],
        out_specs=pl.BlockSpec((blocks // steps, waves, waves, LANES), lambda g: (g, 0, 0, 0)),
        out_shape=hbm_result((blocks, waves, waves, LANES), BF16),
        scratch_shapes=[pltpu.VMEM((lats // steps * waves, LANES), F32)],
        compiler_params=params(20),
        name="legendre_raw",
    )(in_hbm(probes), in_hbm(legendre))


def grid_sum_kernel(coef_ref, lev_ref, x_ref, first_ref, second_ref):
    blocks, lats, waves, _ = x_ref.shape
    flat = x_ref[...].reshape(blocks * lats * waves, LANES)
    summed = jnp.dot(twice(flat), sum_matrix(coef_ref, lev_ref), preferred_element_type=F32)
    summed = summed.reshape(blocks, lats, waves, LANES)
    group = lax.broadcasted_iota(jnp.int32, (blocks, 4, waves, LANES), 3) // 32
    low = jnp.where(group == 0, summed[:, 0:4], summed[:, 4:8])
    high = jnp.where(group == 2, summed[:, 8:12], summed[:, 12:16])
    packed = jnp.where(group < 2, low, high).astype(BF16)
    first_ref[...] = packed[:, :2]
    second_ref[...] = packed[:, 2:]


def grid_sum(x, coef, lev):
    blocks, lats, waves, _ = x.shape
    steps = 4
    return pl.pallas_call(
        grid_sum_kernel,
        grid=(steps,),
        in_specs=[
            smem_spec(),
            smem_spec(),
            pl.BlockSpec((blocks // steps, lats, waves, LANES), lambda g: (g, 0, 0, 0)),
        ],
        out_specs=[pl.BlockSpec((blocks // steps, 2, waves, LANES), lambda g: (g, 0, 0, 0))] * 2,
        out_shape=[jax.ShapeDtypeStruct((blocks, 2, waves, LANES), BF16)] * 2,
        compiler_params=params(12),
        name="grid_sum",
    )(coef, lev, in_hbm(x))


def grid_total_kernel(counts_ref, *refs):
    totals = refs[:4]
    table_ref, out_ref, operand = refs[4:]
    real_lane = (lane_ids(HALF) & PROBES) == 0
    group = lane_ids(HALF) // 32
    zonal = 2 * row_ids(HALF)
    for pair in range(2):
        both = []
        for k in range(2):
            parts = [ref[:, k].astype(F32) for ref in totals[2 * pair : 2 * pair + 2]]
            both.append(parts[0] + parts[1])
        lanes = slice(pair * LANES, (pair + 1) * LANES)
        for parity in range(2):
            masked = []
            for k in range(2):
                x = both[k][:, 8 * parity : 8 * parity + 8].reshape(HALF, LANES)
                lat = 2 * pair + k
                count = jnp.where(
                    group < 2,
                    jnp.where(group == 0, counts_ref[lat], counts_ref[4 + lat]),
                    jnp.where(group == 2, counts_ref[8 + lat], counts_ref[12 + lat]),
                )
                factor = jnp.where(zonal + parity == 0, 1.0, 2.0)
                masked.append(x * jnp.where(zonal + parity < count, factor, 0.0))
            first, second = masked
            operand[parity, :HALF, lanes] = jnp.where(
                real_lane, first, pltpu.roll(second, PROBES, 1)
            ).astype(BF16)
            operand[parity, HALF:, lanes] = jnp.where(
                real_lane, pltpu.roll(first, LANES - PROBES, 1), second
            ).astype(BF16)
    even = jnp.dot(table_ref[0], operand[0], preferred_element_type=F32)
    odd = jnp.dot(table_ref[1], operand[1], preferred_element_type=F32)
    out_ref[0] = (even + odd).astype(BF16)
    out_ref[1] = (even - odd).astype(BF16)


def grid_total(counts, totals, forward):
    shape = (2, M, 2 * LANES)
    vmem = pl.BlockSpec(memory_space=pltpu.VMEM)
    return pl.pallas_call(
        grid_total_kernel,
        in_specs=[smem_spec()] + [vmem] * 5,
        out_shape=hbm_result(shape, BF16),
        scratch_shapes=[pltpu.VMEM(shape, BF16)],
        compiler_params=params(12),
        name="grid_total",
    )(counts, *totals, forward)


def place_matrix(coef_ref, lev_ref, taken_group):
    rows = row_ids(LANES)
    lanes = lane_ids(LANES)
    hit = (rows // 32 == taken_group) & ((rows & 31) == (lanes & 31))
    weights = jnp.where(hit, own_levels(coef_ref, lev_ref, lanes // 32), 0.0)
    return jnp.concatenate(halves(weights), axis=0)


def legendre_kernel(coef_ref, lev_ref, probes_ref, *refs):
    totals = refs[:4]
    table_ref, out_ref, mixed, turned = refs[4:]
    waves = probes_ref.shape[0]
    rows = table_ref.shape[2]

    @pl.when(pl.program_id(0) == 0)
    def _():
        parts = [ref[...].astype(F32) for ref in totals]
        total = ((parts[0] + parts[1]) + (parts[2] + parts[3])).astype(BF16)
        quarter = total.shape[1]
        wide = jnp.dot(
            twice(total.reshape(waves * quarter, LANES)),
            unpack_matrix(coef_ref, lev_ref),
            preferred_element_type=F32,
        )
        for m in range(waves):
            for g in range(4):
                piece = slice(g * quarter, (g + 1) * quarter)
                mixed[m, piece] = (
                    probes_ref[m, 0, piece].astype(F32)
                    + wide[m * quarter : (m + 1) * quarter, g * LANES : (g + 1) * LANES]
                ).astype(BF16)

    for m in range(waves):
        turned[pl.ds(slot(m), rows, stride=waves), :] = jnp.dot(
            table_ref[m, 0], mixed[m], preferred_element_type=F32
        )
    out_ref[...] = turned[...].astype(BF16).reshape(out_ref.shape)


def legendre_forward(probes, totals, legendre, coef, lev, parity):
    waves, _, degrees, _ = probes.shape
    lats = legendre.shape[2]
    blocks = lats // waves
    steps = 2
    total_spec = whole_spec(totals[0].shape)
    return pl.pallas_call(
        legendre_kernel,
        grid=(steps,),
        in_specs=[
            smem_spec(),
            smem_spec(),
            pl.BlockSpec((waves, 1, degrees, LANES), lambda g: (0, parity, 0, 0)),
        ]
        + [total_spec] * 4
        + [pl.BlockSpec((waves, 1, lats // steps, degrees), lambda g: (0, parity, g, 0))],
        out_specs=pl.BlockSpec((blocks // steps, waves, waves, LANES), lambda g: (g, 0, 0, 0)),
        out_shape=hbm_result((blocks, waves, waves, LANES), BF16),
        scratch_shapes=[
            pltpu.VMEM((waves, degrees, LANES), BF16),
            pltpu.VMEM((lats // steps * waves, LANES), F32),
        ],
        compiler_params=params(24),
        name="legendre_forward",
    )(coef, lev, in_hbm(probes), *totals, in_hbm(legendre))


HALF = M // 2


def mask_rows(count, parity):
    zonal = 2 * row_ids(HALF) + parity
    factor = jnp.where(zonal == 0, 1.0, 2.0)
    return jnp.where(zonal < count, factor, 0.0).astype(F32)


def load_waves(counts_ref, x_ref, operand, masked):
    step = pl.program_id(0)
    real_lane = (lane_ids(HALF) & PROBES) == 0
    for pair in range(2):
        both = [x_ref[:, 2 * pair + k].astype(F32) for k in range(2)]
        lanes = slice(pair * LANES, (pair + 1) * LANES)
        for parity in range(2):
            first, second = [
                x[:, 8 * parity : 8 * parity + 8].reshape(HALF, LANES) for x in both
            ]
            if masked:
                first = first * mask_rows(counts_ref[4 * step + 2 * pair], parity)
                second = second * mask_rows(counts_ref[4 * step + 2 * pair + 1], parity)
            operand[parity, :HALF, lanes] = jnp.where(
                real_lane, first, pltpu.roll(second, PROBES, 1)
            ).astype(BF16)
            operand[parity, HALF:, lanes] = jnp.where(
                real_lane, pltpu.roll(first, LANES - PROBES, 1), second
            ).astype(BF16)


def store_waves(counts_ref, fields, table_ref, out_ref, masked):
    step = pl.program_id(0)
    real_lane = (lane_ids(HALF) & PROBES) == 0
    results = {}
    for parity in range(2):
        cos_part = jnp.dot(table_ref[parity, :HALF], fields[parity], preferred_element_type=F32)
        sin_part = jnp.dot(table_ref[parity, HALF:], fields[parity], preferred_element_type=F32)
        for pair in range(2):
            cosine = cos_part[:, pair * LANES : (pair + 1) * LANES]
            sine = sin_part[:, pair * LANES : (pair + 1) * LANES]
            first = jnp.where(real_lane, cosine, pltpu.roll(sine, PROBES, 1))
            second = jnp.where(real_lane, pltpu.roll(cosine, LANES - PROBES, 1), sine)
            if masked:
                first = first * mask_rows(counts_ref[4 * step + 2 * pair], parity)
                second = second * mask_rows(counts_ref[4 * step + 2 * pair + 1], parity)
            results[2 * pair, parity] = first.reshape(-1, 8, LANES)
            results[2 * pair + 1, parity] = second.reshape(-1, 8, LANES)
    for k in range(4):
        out_ref[:, k] = jnp.concatenate([results[k, 0], results[k, 1]], axis=1).astype(BF16)


def grid_even_kernel(counts_ref, x_ref, table_ref, out_ref, operand, *, masked):
    load_waves(counts_ref, x_ref, operand, masked)
    even = jnp.dot(table_ref[0], operand[0], preferred_element_type=F32)
    odd = jnp.dot(table_ref[1], operand[1], preferred_element_type=F32)
    out_ref[0, 0] = (even + odd).astype(BF16)
    out_ref[0, 1] = (even - odd).astype(BF16)


def grid_middle_kernel(
    counts_ref, coef_ref, lev_ref, x_ref, even_ref, *refs, coupled, masked_in, masked_out
):
    if coupled:
        total_ref, refs = refs[0], refs[1:]
    gain_ref, forward_ref, inverse_ref, out_ref, odd_ref, operand, fields = refs
    if coupled:
        place = place_matrix(coef_ref, lev_ref, pl.program_id(0))
    load_waves(counts_ref, x_ref, operand, masked_in)
    size = 256
    for r in range(0, M, size):
        rows = slice(r, r + size)
        even = jnp.dot(forward_ref[0, rows], operand[0], preferred_element_type=F32)
        odd = jnp.dot(forward_ref[1, rows], operand[1], preferred_element_type=F32)
        for pair in range(2):
            lanes = slice(pair * LANES, (pair + 1) * LANES)
            kept = []
            for half, sent in enumerate((even[:, lanes] + odd[:, lanes], even[:, lanes] - odd[:, lanes])):
                base = even_ref[0, half, rows, lanes].astype(F32)
                if coupled:
                    base = base + jnp.dot(
                        twice(total_ref[half, rows, lanes]), place, preferred_element_type=F32
                    )
                longitudes = slice(half * M + r, half * M + r + size)
                north = gain_ref[0, pair, longitudes].astype(F32) * (base + sent)
                south = gain_ref[1, pair, longitudes].astype(F32) * (base - sent)
                kept.append((north + south, north - south))
            fields[0, rows, lanes] = (kept[0][0] + kept[1][0]).astype(BF16)
            fields[1, rows, lanes] = (kept[0][0] - kept[1][0]).astype(BF16)
            odd_ref[0, 0, rows, lanes] = (kept[0][1] + kept[1][1]).astype(BF16)
            odd_ref[0, 1, rows, lanes] = (kept[0][1] - kept[1][1]).astype(BF16)
    store_waves(counts_ref, fields, inverse_ref, out_ref, masked_out)


def grid_odd_kernel(counts_ref, odd_ref, table_ref, out_ref, *, masked):
    store_waves(counts_ref, odd_ref[0], table_ref, out_ref, masked)


def gain_kernel(gain_ref, spread_ref, out_ref):
    for h in range(2):
        out_ref[h, 0] = lax.dot_general(
            gain_ref[h, 0], spread_ref[...], (((0,), (0,)), ((), ())), preferred_element_type=F32
        ).astype(BF16)


def spread_gain(gain):
    pairs = gain.shape[1]
    return pl.pallas_call(
        gain_kernel,
        grid=(pairs,),
        in_specs=[
            pl.BlockSpec((2, 1, 8, 2 * M), lambda g: (0, g, 0, 0)),
            whole_spec((8, LANES)),
        ],
        out_specs=pl.BlockSpec((2, 1, 2 * M, LANES), lambda g: (0, g, 0, 0)),
        out_shape=hbm_result((2, pairs, 2 * M, LANES), BF16),
        compiler_params=params(8),
        name="spread_gain",
    )(gain, jnp.asarray(spread_table()))


def wave_block(x):
    return pl.BlockSpec((x.shape[0], 4, x.shape[2], LANES), lambda g: (0, g, 0, 0))


def grid_pass(arrive, depart, counts, gain, tables, coupling, masked_in, masked_out):
    forward, inverse = tables
    x_even = arrive(0)
    steps = x_even.shape[1] // 4
    field_spec = pl.BlockSpec((1, 2, M, 2 * LANES), lambda g: (g, 0, 0, 0))
    field_shape = (steps, 2, M, 2 * LANES)
    operand = pltpu.VMEM((2, M, 2 * LANES), BF16)
    even = pl.pallas_call(
        functools.partial(grid_even_kernel, masked=masked_in),
        grid=(steps,),
        in_specs=[smem_spec(), wave_block(x_even), whole_spec(forward.shape)],
        out_specs=field_spec,
        out_shape=hbm_result(field_shape, BF16),
        scratch_shapes=[operand],
        compiler_params=params(16),
        name="grid_even",
    )(counts, in_hbm(x_even), in_hbm(forward))
    x_odd = arrive(1)
    out_shape = hbm_result(x_odd.shape, BF16)
    coupled, coef, lev, total = coupling(x_even)
    y_even, odd = pl.pallas_call(
        functools.partial(
            grid_middle_kernel, coupled=coupled, masked_in=masked_in, masked_out=masked_out
        ),
        grid=(steps,),
        in_specs=[
            smem_spec(),
            smem_spec(),
            smem_spec(),
            wave_block(x_odd),
            field_spec,
        ]
        + [whole_spec(x.shape) for x in total]
        + [
            pl.BlockSpec((2, 2, 2 * M, LANES), lambda g: (0, g, 0, 0)),
            whole_spec(forward.shape),
            whole_spec(inverse.shape),
        ],
        out_specs=(wave_block(x_odd), field_spec),
        out_shape=(out_shape, hbm_result(field_shape, BF16)),
        scratch_shapes=[operand, operand],
        compiler_params=params(24),
        name="grid_middle",
    )(counts, coef, lev, x_odd, in_hbm(even), *[in_hbm(x) for x in total], in_hbm(gain), in_hbm(forward), in_hbm(inverse))
    depart(0, y_even)
    y_odd = odd_stage(counts, odd, inverse, x_odd, masked_out)
    depart(1, y_odd)


def odd_stage(counts, odd, inverse, like, masked_out):
    steps = odd.shape[0]
    field_spec = pl.BlockSpec((1, 2, M, 2 * LANES), lambda g: (g, 0, 0, 0))
    return pl.pallas_call(
        functools.partial(grid_odd_kernel, masked=masked_out),
        grid=(steps,),
        in_specs=[smem_spec(), field_spec, whole_spec(inverse.shape)],
        out_specs=wave_block(like),
        out_shape=hbm_result(like.shape, BF16),
        compiler_params=params(16),
        name="grid_odd",
    )(counts, in_hbm(odd), in_hbm(inverse))


def spread_rows(x_ref, scratch):
    chunk = 4
    per = x_ref.shape[1] * x_ref.shape[2]

    def widen(b, carry):
        scratch[pl.ds(b * chunk * per, chunk * per), :] = (
            x_ref[pl.ds(b * chunk, chunk)].astype(F32).reshape(chunk * per, LANES)
        )
        return carry

    lax.fori_loop(0, x_ref.shape[0] // chunk, widen, 0, unroll=2)


def transform_of(table, fields):
    return lax.dot_general(table, fields, (((0,), (0,)), ((), ())), preferred_element_type=F32)


def middle_kernel(first_ref, visc_ref, lev_ref, x_ref, table_ref, out_ref, taken, turned, *, parity):
    waves = x_ref.shape[2]
    lats = x_ref.shape[0] * x_ref.shape[1]
    degrees = table_ref.shape[3]
    spread_rows(x_ref, taken)
    visc = own_levels(visc_ref, lev_ref, lane_ids(degrees) // 32)

    def one_wave(m, carry):
        fields = taken[pl.ds(slot(m), lats, stride=waves), :].astype(BF16)
        table = table_ref[m, 0]
        tangent = transform_of(table, fields)
        degree = first_ref[0] + m + parity + 2 * row_ids(degrees)
        scaled = (degree * (degree + 1)).astype(F32) / float((M + K) * (M + K + 1))
        damp = 1.0 / (1.0 + scaled * visc)
        damped = (tangent * (damp * damp)).astype(BF16)
        turned[pl.ds(slot(m), lats, stride=waves), :] = jnp.dot(
            table, damped, preferred_element_type=F32
        )
        return carry

    lax.fori_loop(0, waves, one_wave, 0, unroll=2)
    per = x_ref.shape[1] * waves

    def narrow(b, carry):
        out_ref[pl.ds(b * 4, 4)] = (
            turned[pl.ds(b * 4 * per, 4 * per), :]
            .astype(BF16)
            .reshape(4, x_ref.shape[1], waves, LANES)
        )
        return carry

    lax.fori_loop(0, x_ref.shape[0] // 4, narrow, 0, unroll=2)


def middle_stage(x, legendre, viscosity, lev, wave_first, parity):
    waves, _, lats, degrees = legendre.shape
    return pl.pallas_call(
        functools.partial(middle_kernel, parity=parity),
        grid=(1,),
        in_specs=[
            smem_spec(),
            smem_spec(),
            smem_spec(),
            whole_spec(x.shape),
            pl.BlockSpec((waves, 1, lats, degrees), lambda g: (0, parity, 0, 0)),
        ],
        out_specs=whole_spec(x.shape),
        out_shape=hbm_result(x.shape, BF16),
        scratch_shapes=[pltpu.VMEM((lats * waves, LANES), F32)] * 2,
        compiler_params=params(26),
        name="middle_stage",
    )(wave_first, viscosity, lev, x, in_hbm(legendre))


def images_kernel(up_ref, down_ref, lev_ref, x_ref, table_ref, out_ref, part_ref, low_ref, taken):
    waves = x_ref.shape[2]
    lats = x_ref.shape[0] * x_ref.shape[1]
    count = table_ref.shape[0]
    step = pl.program_id(0)

    @pl.when(step == 0)
    def _():
        spread_rows(x_ref, taken)

    down_matrix = sum_matrix(down_ref, lev_ref)
    matrix = jnp.concatenate([sum_matrix(up_ref, lev_ref), down_matrix], axis=1)
    highs, lows = [], []
    for k in range(count):
        fields = taken[pl.ds(slot(step * count + k), lats, stride=waves), :].astype(BF16)
        high, low = halves(transform_of(table_ref[k, 0], fields))
        out_ref[k] = jnp.concatenate([high, low], axis=1)
        highs.append(high)
        lows.append(low)
    sums = jnp.dot(
        twice(jnp.concatenate(highs, axis=0)), matrix, preferred_element_type=F32
    )
    rest = jnp.dot(
        jnp.concatenate(lows, axis=0), down_matrix[:LANES], preferred_element_type=F32
    )
    degrees = table_ref.shape[3]
    for k in range(count):
        rows = slice(k * degrees, (k + 1) * degrees)
        part_ref[k] = pack_levels(sums[rows, :LANES]).astype(BF16)
        low_ref[k] = jnp.concatenate(
            halves(pack_levels(sums[rows, LANES:] + rest[rows])), axis=1
        )


def image_stage(x, legendre, up, down, lev, parity):
    x = in_hbm(x) if parity == 0 else x
    waves, _, lats, degrees = legendre.shape
    steps = 4
    count = waves // steps
    return pl.pallas_call(
        images_kernel,
        grid=(steps,),
        in_specs=[
            smem_spec(),
            smem_spec(),
            smem_spec(),
            whole_spec(x.shape),
            pl.BlockSpec((count, 1, lats, degrees), lambda g: (g, parity, 0, 0)),
        ],
        out_specs=(
            pl.BlockSpec((count, degrees, 2 * LANES), lambda g: (g, 0, 0)),
            pl.BlockSpec((count, degrees // 4, LANES), lambda g: (g, 0, 0)),
            pl.BlockSpec((count, degrees // 4, 2 * LANES), lambda g: (g, 0, 0)),
        ),
        out_shape=(
            hbm_result((waves, degrees, 2 * LANES), BF16),
            jax.ShapeDtypeStruct((waves, degrees // 4, LANES), BF16),
            hbm_result((waves, degrees // 4, 2 * LANES), BF16),
        ),
        scratch_shapes=[pltpu.VMEM((lats * waves, LANES), F32)],
        compiler_params=params(20),
        name="image_stage",
    )(up, down, lev, x, in_hbm(legendre))


def gram_of(high, both):
    return lax.dot_general(high, both, (((0,), (0,)), ((), ())), preferred_element_type=F32)


def gram_kernel(image_ref, out_ref):
    @pl.when(pl.program_id(0) == 0)
    def _():
        out_ref[...] = jnp.zeros_like(out_ref)

    rows = image_ref.shape[0] * image_ref.shape[1]
    both = image_ref[...].reshape(rows, 2 * LANES)
    out_ref[...] += gram_of(both[:, :LANES], both)


def gram_stage(images):
    waves, degrees, _ = images.shape
    steps = 4
    return pl.pallas_call(
        gram_kernel,
        grid=(steps,),
        in_specs=[pl.BlockSpec((waves // steps, degrees, 2 * LANES), lambda g: (g, 0, 0))],
        out_specs=whole_spec((LANES, 2 * LANES)),
        out_shape=jax.ShapeDtypeStruct((LANES, 2 * LANES), F32),
        compiler_params=params(12),
        name="gram_stage",
    )(in_hbm(images))


def finish_kernel(down_ref, lev_ref, *refs):
    first = lev_ref[0] * 4
    square = down_ref[first] * down_ref[first]
    for k in range(1, 4):
        square = square + down_ref[first + k] * down_ref[first + k]
    grams = refs[:2]
    lows = refs[2:4]
    totals = refs[4:12]
    total_ref, gram_ref = refs[12:]
    sums = grams[0][...] + grams[1][...]
    cross = sums[:, LANES:]
    gram = sums[:, :LANES] + (cross + cross.T)
    for p in range(2):
        parts = [ref[...].astype(F32) for ref in totals[4 * p : 4 * p + 4]]
        total = ((parts[0] + parts[1]) + (parts[2] + parts[3])).astype(BF16)
        total_ref[p] = total
        flat = total.reshape(-1, LANES)
        low = lows[p][...].reshape(-1, 2 * LANES)
        operand = jnp.concatenate([flat, low], axis=1)
        result = gram_of(flat, operand)
        mixed = result[:, LANES : 2 * LANES] + result[:, 2 * LANES :]
        gram = gram + square * result[:, :LANES] + (mixed + mixed.T)
    same = (row_ids(LANES) // PROBES) == (lane_ids(LANES) // PROBES)
    gram = jnp.where(same, gram, 0.0)
    summed = gram[0:PROBES]
    for b in range(1, LANES // PROBES):
        summed = summed + gram[b * PROBES : (b + 1) * PROBES]
    for shift in (64, 32, 16):
        summed = summed + pltpu.roll(summed, shift, 1)
    top_lane = (lane_ids(8) & PROBES) == 0
    packed = jnp.where(top_lane, summed[:8], summed[8:])
    gram_ref[...] = jnp.broadcast_to(packed[None], gram_ref.shape)


def finish_stage(grams, lows, totals, down, lev, copies):
    shape = totals[0].shape
    return pl.pallas_call(
        finish_kernel,
        in_specs=[smem_spec(), smem_spec()] + [pl.BlockSpec(memory_space=pltpu.VMEM)] * 12,
        out_shape=(
            hbm_result((2,) + shape, BF16),
            hbm_result((copies, 8, LANES), F32),
        ),
        compiler_params=params(16),
        name="finish_stage",
    )(down, lev, *grams, *lows, *totals)


def factor_of(gram):
    rows = row_ids(PROBES)
    lanes = lane_ids(PROBES) & (PROBES - 1)
    upper = jnp.zeros_like(gram)
    inverse = jnp.where(rows == lanes, 1.0, 0.0).astype(F32)
    for k in range(PROBES):
        scale = lax.rsqrt(gram[k : k + 1, k : k + 1])
        scale = scale * (1.5 - 0.5 * gram[k : k + 1, k : k + 1] * scale * scale)
        line = jnp.where(lanes[0:1] >= k, gram[k : k + 1] * scale, 0.0)
        solved = inverse[k : k + 1] * scale
        column = jnp.where(rows[:, 0:1] > k, gram[:, k : k + 1] * scale, 0.0)
        upper = jnp.where(rows == k, line, upper)
        gram = gram - column * line
        inverse = jnp.where(rows == k, solved, inverse - column * solved)
    return upper, inverse


def basis_kernel(
    own_ref, other_ref, full_ref, out_ref, factor_ref, mix, *, row_scale
):
    @pl.when(pl.program_id(0) == 0)
    def _():
        packed = own_ref[...] + other_ref[...]
        top_lane = (lane_ids(8) & PROBES) == 0
        gram = jnp.concatenate(
            [
                jnp.where(top_lane, packed, pltpu.roll(packed, PROBES, 1)),
                jnp.where(top_lane, pltpu.roll(packed, LANES - PROBES, 1), packed),
            ],
            axis=0,
        )
        upper, inverse = factor_of(gram)
        factor_ref[...] = upper[:, :PROBES] / row_scale
        pick = ((lane_ids(PROBES) & (PROBES - 1)) == row_ids(PROBES)).astype(BF16)
        same = (row_ids(LANES) // PROBES) == (lane_ids(LANES) // PROBES)
        high, low = halves(inverse * row_scale)
        mix_high = jnp.where(same, gram_of(high, pick), 0.0).astype(BF16)
        mix_low = jnp.where(same, gram_of(low, pick), 0.0).astype(BF16)
        mix[0:LANES] = mix_high
        mix[LANES : 2 * LANES] = mix_high
        mix[2 * LANES :] = mix_low

    for m in range(full_ref.shape[0]):
        for p in range(2):
            both = full_ref[m, p]
            value = jnp.dot(both, mix[: 2 * LANES], preferred_element_type=F32) + jnp.dot(
                both[:, :LANES], mix[2 * LANES :], preferred_element_type=F32
            )
            out_ref[m, p] = value.astype(BF16)


def full_kernel(down_ref, lev_ref, even_ref, odd_ref, total_ref, out_ref):
    _, waves, quarter, _ = total_ref.shape
    wide = jnp.dot(
        twice(total_ref[...].reshape(2 * waves * quarter, LANES)),
        unpack_matrix(down_ref, lev_ref),
        preferred_element_type=F32,
    )
    for p, image_ref in enumerate((even_ref, odd_ref)):
        for m in range(waves):
            first = (p * waves + m) * quarter
            for g in range(4):
                piece = slice(g * quarter, (g + 1) * quarter)
                both = image_ref[m, piece]
                full = (both[:, :LANES].astype(F32) + both[:, LANES:].astype(F32)) + wide[
                    first : first + quarter, g * LANES : (g + 1) * LANES
                ]
                out_ref[m, p, piece] = jnp.concatenate(halves(full), axis=1)


def full_stage(images, total, down, lev):
    waves, degrees, _ = images[0].shape
    steps = 4
    count = waves // steps
    image_spec = pl.BlockSpec((count, degrees, 2 * LANES), lambda g: (g, 0, 0))
    return pl.pallas_call(
        full_kernel,
        grid=(steps,),
        in_specs=[
            smem_spec(),
            smem_spec(),
            image_spec,
            image_spec,
            pl.BlockSpec((2, count, degrees // 4, LANES), lambda g: (0, g, 0, 0)),
        ],
        out_specs=pl.BlockSpec((count, 2, degrees, 2 * LANES), lambda g: (g, 0, 0, 0)),
        out_shape=hbm_result((waves, 2, degrees, 2 * LANES), BF16),
        compiler_params=params(14),
        name="full_stage",
    )(down, lev, in_hbm(images[0]), in_hbm(images[1]), in_hbm(total))


def basis_stage(grams, full, row_scale):
    waves, _, degrees, _ = full.shape
    steps = 4
    count = waves // steps
    return pl.pallas_call(
        functools.partial(basis_kernel, row_scale=row_scale),
        grid=(steps,),
        in_specs=[whole_spec((8, LANES))] * 2
        + [pl.BlockSpec((count, 2, degrees, 2 * LANES), lambda g: (g, 0, 0, 0))],
        out_specs=(
            pl.BlockSpec((count, 2, degrees, LANES), lambda g: (g, 0, 0, 0)),
            whole_spec((PROBES, PROBES)),
        ),
        out_shape=(
            hbm_result((waves, 2, degrees, LANES), BF16),
            hbm_result((PROBES, PROBES), F32),
        ),
        scratch_shapes=[pltpu.VMEM((3 * LANES, LANES), BF16)],
        compiler_params=params(14),
        name="basis_stage",
    )(*grams, in_hbm(full))


def exchange(blocks):
    return lax.all_to_all(blocks, "lat", split_axis=0, concat_axis=0, tiled=True)


def from_levels(part):
    count = lax.axis_size("lev")
    return [
        lax.ppermute(part, "lev", [(i, (i + k) % count) for i in range(count)])
        for k in range(1, count)
    ]


def add_partner(values, pairs):
    return (values.astype(F32) + lax.ppermute(values, "lev", pairs).astype(F32)).astype(BF16)


def shards(
    probes, legendre, quad_weight, trunc_counts, background, level_up, level_down, viscosity
):
    lat_count = lax.axis_size("lat")
    lev_count = lax.axis_size("lev")
    lat_index = lax.axis_index("lat")
    lev_index = lax.axis_index("lev")
    wave_local = probes.shape[0]
    level_local = probes.shape[3] // (2 * PROBES)
    lon_count = 2 * M

    lev = lev_index.astype(jnp.int32).reshape(1)
    wave_first = (lat_index * wave_local).astype(jnp.int32).reshape(1)
    forward = wave_tables(M)
    tables = (jnp.asarray(forward), jnp.asarray(np.ascontiguousarray(forward.transpose(0, 2, 1))))

    sent = {0: exchange(legendre_raw(probes, legendre, 0))}
    partial = level_partial(probes, level_down, lev, 1)
    totals = [partial] + from_levels(partial)
    sent[1] = exchange(legendre_forward(probes, totals, legendre, level_up, lev, 1))

    own_gain = lax.dynamic_slice_in_dim(background, lev_index * level_local, level_local, 2)
    own_gain = own_gain * (quad_weight / float(lon_count))[None, :, None, None]
    own_gain = own_gain.reshape(2, -1, 2, level_local, lon_count).swapaxes(2, 3)
    own_gain = own_gain.reshape(2, -1, 2 * level_local, lon_count).astype(BF16)
    gain = spread_gain(own_gain)

    folded = {}

    def depart(p, values):
        folded[p] = exchange(values)

    def couple_first(x):
        near = [(i, i ^ 1) for i in range(lev_count)]
        far = [(i, lev_count - 1 - i) for i in range(lev_count)]
        first, second = grid_sum(x, level_down, lev)
        first = add_partner(first, near)
        second = add_partner(second, far)
        parts = [
            first,
            lax.ppermute(first, "lev", far),
            second,
            lax.ppermute(second, "lev", near),
        ]
        total = grid_total(trunc_counts, parts, tables[0])
        return True, level_up, lev, [total]

    def couple_none(x):
        return False, level_up, lev, []

    grid_pass(lambda p: sent[p], depart, trunc_counts, gain, tables, couple_first, True, False)
    second = {
        p: exchange(middle_stage(folded[p], legendre, viscosity, lev, wave_first, p))
        for p in range(2)
    }
    folded2 = {}

    def depart2(p, values):
        folded2[p] = exchange(values)

    grid_pass(lambda p: second[p], depart2, trunc_counts, gain, tables, couple_none, False, True)
    images, lows, grams, totals = [], [], [], []
    for p in range(2):
        image, part, low = image_stage(folded2[p], legendre, level_up, level_down, lev, p)
        images.append(image)
        lows.append(low)
        grams.append(gram_stage(image))
        totals += [part] + from_levels(part)
    total, gram_copies = finish_stage(grams, lows, totals, level_down, lev, lat_count)
    received = exchange(gram_copies)
    full = full_stage(images, total, level_down, lev)
    over_lat = jnp.sum(received, axis=0)
    row_scale = math.sqrt(M * K * 2 * level_local * lev_count)
    near = [(i, i ^ 1) for i in range(lev_count)]
    far = [(i, lev_count - 1 - i) for i in range(lev_count)]
    pair_sum = over_lat + lax.ppermute(over_lat, "lev", near)
    return basis_stage([pair_sum, lax.ppermute(pair_sum, "lev", far)], full, row_scale)


def solution(mesh):
    placed = (
        P("lat", None, None, "lev"),
        P("lat", None, None, None),
        P("lat"),
        P("lat"),
        P(None, "lat", None, None),
        P(),
        P(),
        P(),
    )
    return jax.shard_map(
        shards,
        mesh=mesh,
        in_specs=placed,
        out_specs=(P("lat", None, None, "lev"), P()),
        check_vma=False,
    )
```
